128 devices in a mesh: rep: 8 (over z, core), tab: 16 (over x, y).
Axes of the slice: x: 4, y: 4, z: 4, core: 2. Of those that a mesh axis runs over, the one named last changes fastest.
Arguments:
- inputs: bfloat16 [16384, 4096], P(('rep', 'tab')), may hold values from -24 to 24
- grad_out: bfloat16 [16384, 4096], P(('rep', 'tab')), may hold values from -6 to 6
- query_weight: bfloat16 [4096, 1024], replicated, may hold values from -0.09375 to 0.09375
- sub_keys: bfloat16 [1024, 1024], replicated, may hold values from -6 to 6
- values: bfloat16 [4096, 4096], P('tab'), may hold values from -0.09375 to 0.09375
- owner: int32 [16384, 2, 1], P(('rep', 'tab')), may hold values from 0 to 15; in each aligned block of 256 rows (0 to 255, 256 to 511, ..., all dimensions but the last counted through in order) at most 32 rows name the same one
- slot_rows: int32 [16384, 2, 32], P(('rep', 'tab')), may hold values from 0 to 255, as said below
- sub_index: int32 [16384, 2, 2, 32], P(('rep', 'tab')), may hold values from 0 to 1023
Outputs:
- input_grad: bfloat16 [16384, 4096], P(('rep', 'tab'))
- weight_grad: float32 [4096, 1024], P('tab')
- key_grad: float32 [1024, 1024], P('tab')
- table_grad: bfloat16 [4096, 4096], P('tab')
The draws below stay inside these ranges and needn't reach their ends.
Inputs may be any that keep to these rules, and one draw needn't show every extreme that they name: `owner`: within the token-head pairs of one device (aligned blocks of 256 pairs), no shard number appears more than 32 times, and one appears exactly 32 times in some or all blocks. `slot_rows`: the 32 row numbers of one token and head are distinct.
All inputs are finite; a program needn't handle non-finite values.
Results may differ from the reference program's by a relative error of at most 0.0059.
Values may be sent and summed in bfloat16 or wider, within the bound.
A program may use at most 192 MiB of HBM per device.

```python
import math
import jax
import jax.numpy as jnp
import numpy as np
from jax import lax

D = 4096
HEADS = 2
DK = 512
NSUB = 1024
TOPK = 32
TOK_DEV = 128
VROW_DEV = 256
CAP = 32
TOKENS = 16384
ROWS = 4096
KW = 1024
N_TAB = 16


def draw_slot_rows(key, part):
    ranked = jax.random.randint(key, (TOKENS * HEADS, VROW_DEV), 0, 1048576) * VROW_DEV + jnp.arange(VROW_DEV, dtype=jnp.int32)[None, :]
    ordering = jnp.argsort(ranked, axis=1)
    return ordering[:, :TOPK].astype(jnp.int32).reshape(TOKENS, HEADS, TOPK)


def draw_sub_keys(key, part):
    key_scale = (DK // 2) ** (-0.5)
    base_key = jax.random.fold_in(key, 11)
    result = jax.random.normal(base_key, (NSUB, HEADS * DK), jnp.float32) * key_scale
    return result.astype(jnp.bfloat16)


def touch_ends(array, key, least, largest):
    longest = array.shape.index(max(array.shape))
    spots = []
    for shift in (0, 1):
        where = [jax.random.randint(jax.random.fold_in(key, axis), (), 0, length) for axis, length in enumerate(array.shape)]
        where[longest] = (where[longest] + shift) % array.shape[longest]
        spots.append(tuple(where))
    return array.at[spots[0]].set(least).at[spots[1]].set(largest)


def spiked(values, rng, source, target, shards_of, factor):
    def block_of(dim):
        return (jnp.arange(values.shape[dim]) // (values.shape[dim] // shards_of)).reshape((-1,) + (1,) * (values.ndim - 1 - dim))

    one_side = jax.random.permutation(rng, shards_of)[block_of(target)]
    other_side = (block_of(target) + shards_of // 2) % shards_of
    return jnp.where((block_of(source) == one_side) | (block_of(source) == other_side), factor * values, values)


def level_of(own_key, extent, split, low, high):
    def one(dim, shards_of):
        steps = jax.random.uniform(jax.random.fold_in(jax.random.fold_in(own_key, 6), dim), (shards_of,), jnp.float32, low / len(split), high / len(split))
        return jnp.repeat(jnp.exp(steps), extent[dim] // shards_of).reshape((-1,) + (1,) * (len(extent) - dim - 1))

    factor_of = one(*split[0])
    for cut in split[1:]:
        factor_of = factor_of * one(*cut)
    return factor_of


def shared_out(stream_key, own, number, rows, amount, top, most, skew):
    order = jax.random.permutation(stream_key, amount)
    packed, ordinary = shares(amount, rows * top, most, skew, True), shares(amount, rows * top, most, skew, False)
    places = jnp.arange(amount)

    def named(sizes, rotation):
        used = int((sizes > 0).sum())
        fixed = max(1, used // 4)
        moved = fixed + (places - fixed + rotation * (used - fixed)) % max(1, amount - fixed)
        return jnp.zeros((amount,), jnp.int32).at[order[jnp.where(places < fixed, places, moved)]].set(jnp.asarray(sizes, jnp.int32))

    sizes = jnp.where(number % 4 == 0, named(packed, number // 4), named(ordinary, number - number // 4 - 1))
    mixed = jax.random.permutation(jax.random.fold_in(own, 3), amount)
    donor, receiver = mixed[0:amount // 2 * 2:2], mixed[1:amount // 2 * 2:2]
    margin = jnp.minimum(sizes[donor] - 1, most - sizes[receiver]) // 2
    margin = jnp.where((donor == order[0]) | (receiver == order[0]) | (sizes[receiver] == 0), 0, jnp.maximum(margin, 0))
    moved = jax.random.randint(jax.random.fold_in(own, 4), (amount // 2,), 0, 1 << 20) % (margin + 1)
    sizes = sizes.at[donor].add(-moved).at[receiver].add(moved)
    members = jnp.searchsorted(jnp.cumsum(sizes), jnp.arange(rows * top), side="right").astype(jnp.int32)
    grid = members.reshape(top, rows).T
    grid = grid[jax.random.permutation(jax.random.fold_in(own, 1), rows)]
    rotation = jax.random.randint(jax.random.fold_in(own, 2), (rows, 1), 0, top)
    return jnp.take_along_axis(grid, (jnp.arange(top)[None, :] + rotation) % top, axis=1)


def shares(amount, total, bound, lean, full):
    loads = [(1 << 20) // math.isqrt(standing ** lean) + 1 for standing in range(1, amount + 1)]
    largest = bound if full else min(bound, max(-(-total // amount), total * loads[0] // sum(loads)))
    least = 1 if total - largest >= amount - 1 else 0
    holding, surplus = [largest] + [least] * (amount - 1), total - largest - least * (amount - 1)
    while surplus > 0:
        movable = [i for i in range(1, amount) if holding[i] < largest] or [i for i in range(1, amount) if holding[i] < bound]
        whole, left = sum([loads[i] for i in movable]), surplus
        for i in movable:
            more = min(bound - holding[i], max(1, left * loads[i] // whole), surplus)
            holding[i] = holding[i] + more
            surplus = surplus - more
    return np.array(holding)


def gaussian(key, extent, width, most, shards=(), kind=jnp.bfloat16):
    values = width * jax.random.normal(key, extent, jnp.float32)
    if shards:
        values = values * level_of(key, extent, shards, -0.22, 0.18)
    return jnp.clip(values, -most, most).astype(kind)


def gaussian_with(rng, shape, scale, reach, cuts, heavy, held_as=jnp.bfloat16):
    values = scale * jax.random.normal(rng, shape, jnp.float32)
    if cuts:
        values = values * level_of(rng, shape, cuts, -0.22, 0.18)
    return jnp.clip(spiked(values, jax.random.fold_in(rng, 3), *heavy), -reach, reach).astype(held_as)


def setup_inputs(seed: int = 0) -> dict:
    splits = jax.random.split(jax.random.key(seed), 9)
    inputs = gaussian_with(splits[0], (TOKENS, D), 1.0, 24.0, ((0, 128),), (0, 1, 128, 5.5))
    grad_out = gaussian(splits[1], (TOKENS, D), 1.0, 6.0, ((0, 128),))
    query_weight = gaussian(splits[2], (D, KW), D ** -0.5, 0.09375)
    sub_keys = draw_sub_keys(jax.random.fold_in(splits[8], 71), 0)
    values = gaussian(splits[4], (ROWS, D), D ** -0.5, 0.09375, ((0, 16),))
    owner_keys = jax.random.split(jax.random.fold_in(splits[5], 1), TOKENS * HEADS // (TOK_DEV * HEADS))
    owner_turns = jax.random.permutation(jax.random.fold_in(splits[5], 3), TOKENS * HEADS // (TOK_DEV * HEADS))
    owner = jax.vmap(lambda own, number: shared_out(jax.random.fold_in(splits[5], 2), own, number, TOK_DEV * HEADS, N_TAB, 1, CAP, 2))(owner_keys, owner_turns).reshape((TOKENS, HEADS, 1))
    slot_rows = draw_slot_rows(jax.random.fold_in(splits[8], 71), 0)
    sub_index = touch_ends(jax.random.randint(splits[7], (TOKENS, HEADS, 2, TOPK), 0, NSUB), jax.random.fold_in(splits[7], 1), 0, NSUB - 1).astype(jnp.int32)
    return {"inputs": inputs, "grad_out": grad_out, "query_weight": query_weight, "sub_keys": sub_keys, "values": values, "owner": owner, "slot_rows": slot_rows, "sub_index": sub_index}


def reference(inputs, grad_out, query_weight, sub_keys, values, owner, slot_rows, sub_index):
    blocks = 2 * HEADS
    half_width = DK // 2
    query_cols = HEADS * DK
    step_tokens = 64
    steps = TOKENS // step_tokens
    table_count = VROW_DEV * N_TAB
    key_blocks = sub_keys.astype(jnp.float32).reshape(NSUB, blocks, half_width)
    token_iota = jnp.arange(step_tokens, dtype=jnp.int32)[:, None, None]
    block_iota = jnp.arange(blocks, dtype=jnp.int32)[None, :, None]

    def one_step(carry, pieces):
        weight_acc, key_acc, table_acc = carry
        tok_in, tok_grad, tok_owner, tok_rows, tok_sub = pieces
        query = jnp.dot(tok_in, query_weight, preferred_element_type=jnp.float32)
        query_blocks = query.reshape(step_tokens, blocks, half_width)
        low_blocks = lax.optimization_barrier(query.astype(jnp.bfloat16)).astype(jnp.float32).reshape(step_tokens, blocks, half_width)
        half_scores = jnp.einsum("tbc,nbc->tbn", query_blocks, key_blocks, precision=lax.Precision.HIGHEST)
        picks = tok_sub.reshape(step_tokens, blocks, TOPK)
        chosen = jnp.take_along_axis(half_scores, picks, axis=2).reshape(step_tokens, HEADS, 2, TOPK)
        scores = chosen[:, :, 0] + chosen[:, :, 1]
        weights = jax.nn.softmax(scores, axis=-1)
        table_row = (tok_owner * VROW_DEV + tok_rows).reshape(-1).astype(jnp.int32)
        picked = values[table_row].astype(jnp.float32).reshape(step_tokens, HEADS, TOPK, D)
        grad_full = tok_grad.astype(jnp.float32)
        slot_grad = jnp.einsum("thkd,td->thk", picked, grad_full)
        score_grad = weights * (slot_grad - jnp.sum(weights * slot_grad, axis=-1, keepdims=True))
        spread = jnp.broadcast_to(score_grad[:, :, None, :], (step_tokens, HEADS, 2, TOPK)).reshape(step_tokens, blocks, TOPK)
        half_grad = jnp.zeros((step_tokens, blocks, NSUB), jnp.float32).at[token_iota, block_iota, picks].add(spread)
        half_grad = lax.optimization_barrier(half_grad.astype(jnp.bfloat16)).astype(jnp.float32)
        query_grad = jnp.einsum("tbn,nbc->tbc", half_grad, key_blocks).reshape(step_tokens, query_cols).astype(jnp.bfloat16)
        input_grad = jnp.dot(query_grad, query_weight.T, preferred_element_type=jnp.float32).astype(jnp.bfloat16)
        weight_acc = weight_acc + jnp.dot(tok_in.T, query_grad, preferred_element_type=jnp.float32)
        key_acc = key_acc + jnp.einsum("tbn,tbc->nbc", half_grad, low_blocks).reshape(NSUB, query_cols)
        low_weights = lax.optimization_barrier(weights.astype(jnp.bfloat16)).astype(jnp.float32)
        terms = (low_weights[:, :, :, None] * grad_full[:, None, None, :]).reshape(-1, D)
        table_acc = table_acc.at[table_row].add(terms)
        return (weight_acc, key_acc, table_acc), input_grad

    start = (jnp.zeros((D, query_cols), jnp.float32), jnp.zeros((NSUB, query_cols), jnp.float32), jnp.zeros((table_count, D), jnp.float32))
    pieces = (inputs.reshape(steps, step_tokens, D), grad_out.reshape(steps, step_tokens, D), owner.reshape(steps, step_tokens, HEADS, 1), slot_rows.reshape(steps, step_tokens, HEADS, TOPK), sub_index.reshape(steps, step_tokens, HEADS, 2, TOPK))
    (weight_acc, key_acc, table_acc), input_grads = lax.scan(one_step, start, pieces)
    return (input_grads.reshape(TOKENS, D), weight_acc, key_acc, table_acc.astype(jnp.bfloat16))
```

```python
import functools

import jax
import jax.numpy as jnp
from jax import lax
from jax.experimental import pallas as pl
from jax.experimental.pallas import tpu as pltpu
from jax.sharding import PartitionSpec as P

BF = jnp.bfloat16
F32 = jnp.float32
I32 = jnp.int32


def dot_nn(a, b):
    return lax.dot_general(a, b, (((1,), (0,)), ((), ())), preferred_element_type=F32)


def dot_nt(a, b):
    return lax.dot_general(a, b, (((1,), (1,)), ((), ())), preferred_element_type=F32)


def dot_tn(a, b):
    return lax.dot_general(a, b, (((0,), (0,)), ((), ())), preferred_element_type=F32)


def three(x):
    a = x.astype(BF)
    rest = x - a.astype(F32)
    b = rest.astype(BF)
    c = (rest - b.astype(F32)).astype(BF)
    return a, b, c


def iota(shape, dim):
    return lax.broadcasted_iota(I32, shape, dim)


def dispatch_kernel(capacity, own_row, own_col, grad, rows, payload, slot_row):
    messages = own_row.shape[1]
    tokens = grad.shape[0]
    slots, wide = payload.shape
    width = grad.shape[1]
    same = own_row[...] == own_col[...]
    earlier = iota((messages, messages), 0) < iota((messages, messages), 1)
    rank = jnp.sum(jnp.where(same & earlier, 1, 0), axis=0, keepdims=True)
    place = own_row[...] * capacity + rank
    slot_row[...] = place
    hit = jnp.where(iota((slots, messages), 0) == place, 1.0, 0.0)
    either = hit[:, :tokens]
    for head in range(1, messages // tokens):
        either = either + hit[:, head * tokens : (head + 1) * tokens]
    either = either.astype(BF)
    step = 512
    for at in range(0, width, step):
        payload[:, at : at + step] = dot_nn(either, grad[:, at : at + step]).astype(BF)
    payload[:, width:] = dot_nn(hit.astype(BF), rows[...]).astype(BF)


def score_kernel(
    heads, inputs, weight, keys, picks, slot_col, low_out, weights_out, send_out, acc
):
    step = pl.program_id(0)

    @pl.when(step == 0)
    def _():
        acc[...] = jnp.zeros_like(acc)

    acc[...] += dot_nn(inputs[...], weight[...])

    @pl.when(step == pl.num_programs(0) - 1)
    def _():
        tokens, cols = acc.shape
        lanes = picks.shape[1]
        blocks = 2 * heads
        half = cols // blocks
        count = keys.shape[0]
        low_out[...] = acc[...].astype(BF)
        pick = picks[...]
        low = pick % 128
        high = pick // 128
        lane_block = iota((tokens, lanes), 1) // (lanes // blocks)
        chosen = jnp.zeros((tokens, lanes), F32)
        for b in range(blocks):
            parts = three(acc[:, b * half : (b + 1) * half])
            block_keys = keys[:, b * half : (b + 1) * half]
            for j in range(count // 128):
                rows = block_keys[j * 128 : (j + 1) * 128]
                score = dot_nt(parts[2], rows) + dot_nt(parts[1], rows) + dot_nt(parts[0], rows)
                got = jnp.take_along_axis(score, low, axis=1)
                chosen = jnp.where((high == j) & (lane_block == b), got, chosen)
        top = lanes // blocks
        even = lane_block % 2 == 0
        other = jnp.where(
            even, pltpu.roll(chosen, lanes - top, axis=1), pltpu.roll(chosen, top, axis=1)
        )
        scores = chosen + other
        head_of = lane_block // 2
        peak = jnp.zeros((tokens, lanes), F32)
        for h in range(heads):
            most = jnp.max(jnp.where(head_of == h, scores, -jnp.inf), axis=1, keepdims=True)
            peak = jnp.where(head_of == h, most, peak)
        raised = jnp.exp(scores - peak)
        total = jnp.zeros((tokens, lanes), F32)
        for h in range(heads):
            part = jnp.sum(jnp.where(head_of == h, raised, 0.0), axis=1, keepdims=True)
            total = jnp.where(head_of == h, part * 0.5, total)
        soft = raised / total
        weights_out[...] = soft
        slots = send_out.shape[0]
        low_soft = soft.astype(BF).astype(F32)
        sent = jnp.zeros((slots, lanes), F32)
        for h in range(heads):
            hit = jnp.where(
                iota((tokens, slots), 1) == slot_col[h * tokens : (h + 1) * tokens], 1.0, 0.0
            ).astype(BF)
            turned = low_soft if h == 0 else pltpu.roll(low_soft, lanes - h * 2 * top, axis=1)
            sent = sent + dot_tn(hit, turned.astype(BF))
        send_out[...] = sent.astype(BF)


def shard_kernel(width, arrived, values, back):
    product = dot_nt(arrived[:, :width], values[...])
    pick = arrived[:, width:].astype(I32)
    out = jnp.zeros(pick.shape, F32)
    for j in range(values.shape[0] // 128):
        got = jnp.take_along_axis(product[:, j * 128 : (j + 1) * 128], pick % 128, axis=1)
        out = jnp.where(pick // 128 == j, got, out)
    back[...] = out


def table_kernel(top, arrived, rows, soft, part, spread):
    @pl.when(pl.program_id(0) == 0)
    def _():
        count, slots = spread.shape
        row_t = rows[...].astype(F32).T
        soft_t = soft[...].astype(F32).T
        for at in range(0, slots, 128):
            names = iota((count, 128), 0).astype(F32)
            held = jnp.zeros((count, 128), F32)
            for k in range(top):
                held = held + jnp.where(
                    names == row_t[k : k + 1, at : at + 128], soft_t[k : k + 1, at : at + 128], 0.0
                )
            spread[:, at : at + 128] = held.astype(BF)

    part[...] = dot_nn(spread[...], arrived[...]).astype(BF)


def grad_kernel(heads, returned, slot_col, soft, picks, keys, half_out, query_out, placed):
    tokens, lanes = soft.shape
    blocks = 2 * heads
    top = lanes // blocks
    slots = returned.shape[0]
    head_of = iota((tokens, lanes), 1) // (2 * top)
    parts = three(returned[...])
    slot_grad = jnp.zeros((tokens, lanes), F32)
    for h in range(heads):
        hit = jnp.where(
            iota((tokens, slots), 1) == slot_col[h * tokens : (h + 1) * tokens], 1.0, 0.0
        ).astype(BF)
        got = dot_nn(hit, parts[2]) + dot_nn(hit, parts[1]) + dot_nn(hit, parts[0])
        slot_grad = jnp.where(head_of == h, got, slot_grad)
    weights = soft[...]
    scaled = weights * slot_grad
    mean = jnp.zeros((tokens, lanes), F32)
    for h in range(heads):
        part = jnp.sum(jnp.where(head_of == h, scaled, 0.0), axis=1, keepdims=True)
        mean = jnp.where(head_of == h, part * 0.5, mean)
    score_grad = weights * (slot_grad - mean)
    count = keys.shape[0]
    tiles = count // 128
    pick = picks[...]
    low = pick % 128
    high = pick // 128 + tiles * (iota((tokens, lanes), 1) // top)
    for t in range(tokens):
        left = jnp.where(
            iota((blocks * tiles, lanes), 0) == high[t : t + 1], score_grad[t : t + 1], 0.0
        ).astype(BF)
        right = jnp.where(iota((128, lanes), 0) == low[t : t + 1], 1.0, 0.0).astype(BF)
        placed[t] = dot_nt(left, right)
    half = query_out.shape[1] // blocks
    quarter = half_out.shape[2]
    each = quarter // 128
    for b in range(blocks):
        total = jnp.zeros((tokens, half), F32)
        for q in range(count // quarter):
            for i in range(each):
                row = b * tiles + q * each + i
                sums = placed[:, row, :].astype(BF)
                half_out[q * blocks + b, :, i * 128 : (i + 1) * 128] = sums
                at = (q * each + i) * 128
                total = total + dot_nn(sums, keys[at : at + 128, b * half : (b + 1) * half])
        query_out[:, b * half : (b + 1) * half] = total.astype(BF)


VM = pl.BlockSpec(memory_space=pltpu.VMEM)
LIMIT = 56 * 1024 * 1024


def local(body, out_shape, **more):
    return pl.pallas_call(
        body,
        out_shape=out_shape,
        compiler_params=pltpu.CompilerParams(vmem_limit_bytes=LIMIT),
        **more,
    )


def sds(shape, dtype):
    return jax.ShapeDtypeStruct(shape, dtype)


def on_device(inputs, grad_out, query_weight, sub_keys, values, owner, slot_rows, sub_index):
    tokens, width = inputs.shape
    cols = query_weight.shape[1]
    count = sub_keys.shape[0]
    heads, top = slot_rows.shape[1:]
    blocks = 2 * heads
    lanes = blocks * top
    shards = lax.axis_size("tab")
    groups = lax.axis_size("rep")
    messages = tokens * heads
    capacity = 2 * messages // shards
    slots = shards * capacity
    table_rows = values.shape[0]
    across = functools.partial(lax.all_to_all, axis_name="tab", tiled=True)

    own_row = owner.reshape(tokens, heads).T.reshape(1, messages)
    own_col = own_row.reshape(messages, 1)
    rows4 = jnp.tile(jnp.transpose(slot_rows, (1, 0, 2)).reshape(messages, top), (1, blocks))
    payload, slot_row = local(
        functools.partial(dispatch_kernel, capacity),
        (sds((slots, width + lanes), BF), sds((1, messages), I32)),
        name="dispatch",
    )(own_row, own_col, grad_out, rows4.astype(BF))
    arrived = across(
        payload.reshape(shards, capacity, width + lanes), split_axis=0, concat_axis=0
    ).reshape(slots, width + lanes)
    slot_col = slot_row.reshape(messages, 1)
    picks = sub_index.reshape(tokens, lanes)

    depth = 512
    low_query, weights, send_weights = local(
        functools.partial(score_kernel, heads),
        (sds((tokens, cols), BF), sds((tokens, lanes), F32), sds((slots, lanes), BF)),
        grid=(width // depth,),
        in_specs=[
            pl.BlockSpec((tokens, depth), lambda i: (0, i)),
            pl.BlockSpec((depth, cols), lambda i: (i, 0)),
            pl.BlockSpec((count, cols), lambda i: (0, 0)),
            pl.BlockSpec((tokens, lanes), lambda i: (0, 0)),
            pl.BlockSpec((messages, 1), lambda i: (0, 0)),
        ],
        out_specs=(
            pl.BlockSpec((tokens, cols), lambda i: (0, 0)),
            pl.BlockSpec((tokens, lanes), lambda i: (0, 0)),
            pl.BlockSpec((slots, lanes), lambda i: (0, 0)),
        ),
        scratch_shapes=[pltpu.VMEM((tokens, cols), F32)],
        name="scores",
    )(inputs, query_weight, sub_keys, picks, slot_col)

    back = local(
        functools.partial(shard_kernel, width),
        sds((slots, lanes), F32),
        grid=(slots // 128,),
        in_specs=[
            pl.BlockSpec((128, width + lanes), lambda i: (i, 0)),
            pl.BlockSpec((table_rows, width), lambda i: (0, 0)),
        ],
        out_specs=pl.BlockSpec((128, lanes), lambda i: (i, 0)),
        name="shard",
    )(arrived, values)
    returned = across(back.reshape(shards, capacity, lanes), split_axis=0, concat_axis=0)
    returned = returned.reshape(slots, lanes)

    arrived_weights = across(
        send_weights.reshape(shards, capacity, lanes), split_axis=0, concat_axis=0
    ).reshape(slots, lanes)
    table_part = local(
        functools.partial(table_kernel, top),
        sds((table_rows, width), BF),
        grid=(width // 512,),
        in_specs=[
            pl.BlockSpec((slots, 512), lambda i: (0, i)),
            pl.BlockSpec((slots, lanes), lambda i: (0, width // lanes)),
            pl.BlockSpec((slots, lanes), lambda i: (0, 0)),
        ],
        out_specs=pl.BlockSpec((table_rows, 512), lambda i: (0, i)),
        scratch_shapes=[pltpu.VMEM((table_rows, slots), BF)],
        name="table",
    )(arrived, arrived, arrived_weights)
    table_pieces = lax.all_to_all(
        table_part.reshape(groups, table_rows // groups, width), "rep", 0, 0, tiled=True
    )
    table_piece = jnp.sum(table_pieces.astype(F32), axis=0).astype(BF)
    table_grad = lax.all_gather(table_piece, "rep", axis=0, tiled=True)

    quarters = shards // blocks
    quarter = count // quarters
    half_grad, query_grad = local(
        functools.partial(grad_kernel, heads),
        (sds((shards, tokens, quarter), BF), sds((tokens, cols), BF)),
        scratch_shapes=[pltpu.VMEM((tokens, blocks * count // 128, 128), F32)],
        name="grads",
    )(returned, slot_col, weights, picks, sub_keys)
    input_grad = lax.dot_general(
        query_grad, query_weight, (((1,), (1,)), ((), ())), preferred_element_type=F32
    ).astype(BF)

    weight_rows = width // shards
    half = cols // blocks
    early = jnp.concatenate(
        [
            jnp.transpose(inputs.reshape(tokens, shards, weight_rows), (1, 0, 2)),
            jnp.tile(jnp.transpose(low_query.reshape(tokens, blocks, half), (1, 0, 2)), (quarters, 1, 1)),
        ],
        axis=2,
    )
    early = across(early, split_axis=0, concat_axis=0).reshape(shards * tokens, weight_rows + half)
    group_inputs = early[:, :weight_rows]
    group_query = early[:, weight_rows:]
    group_half = across(half_grad, split_axis=0, concat_axis=0).reshape(shards * tokens, quarter)
    group_grad = lax.all_gather(query_grad, "tab", axis=0, tiled=True)
    weight_part = dot_tn(group_inputs, group_grad)
    key_part = dot_tn(group_half, group_query)
    key_rows = count // shards
    members = [[q * blocks + b for b in range(blocks)] for q in range(quarters)]
    key_part = lax.all_to_all(
        key_part.reshape(blocks, key_rows, half), "tab", 0, 0, axis_index_groups=members, tiled=True
    )
    key_part = jnp.transpose(key_part, (1, 0, 2)).reshape(key_rows, cols)
    weight_grad, key_grad = lax.psum((weight_part, key_part), "rep")
    return (input_grad, weight_grad, key_grad, table_grad)


def solution(mesh):
    placed = (
        P(("rep", "tab"), None),
        P(("rep", "tab"), None),
        P(),
        P(),
        P("tab", None),
        P(("rep", "tab"), None, None),
        P(("rep", "tab"), None, None),
        P(("rep", "tab"), None, None, None),
    )
    return jax.shard_map(
        on_device,
        mesh=mesh,
        in_specs=placed,
        out_specs=(P(("rep", "tab"), None), P("tab", None), P("tab", None), P("tab", None)),
        check_vma=False,
    )
```

```python
import functools

import jax
import jax.numpy as jnp
from jax import lax
from jax.experimental import pallas as pl
from jax.experimental.pallas import tpu as pltpu
from jax.sharding import PartitionSpec as P

BF = jnp.bfloat16
F32 = jnp.float32
I32 = jnp.int32


def dot_nn(a, b):
    return lax.dot_general(a, b, (((1,), (0,)), ((), ())), preferred_element_type=F32)


def dot_nt(a, b):
    return lax.dot_general(a, b, (((1,), (1,)), ((), ())), preferred_element_type=F32)


def dot_tn(a, b):
    return lax.dot_general(a, b, (((0,), (0,)), ((), ())), preferred_element_type=F32)


def three(x):
    a = x.astype(BF)
    rest = x - a.astype(F32)
    b = rest.astype(BF)
    c = (rest - b.astype(F32)).astype(BF)
    return a, b, c


def iota(shape, dim):
    return lax.broadcasted_iota(I32, shape, dim)


def dispatch_kernel(capacity, own_row, own_col, grad, rows, payload, slot_row):
    messages = own_row.shape[1]
    tokens = grad.shape[0]
    slots, wide = payload.shape
    width = grad.shape[1]
    same = own_row[...] == own_col[...]
    earlier = iota((messages, messages), 0) < iota((messages, messages), 1)
    rank = jnp.sum(jnp.where(same & earlier, 1, 0), axis=0, keepdims=True)
    place = own_row[...] * capacity + rank
    slot_row[...] = place
    hit = jnp.where(iota((slots, messages), 0) == place, 1.0, 0.0)
    either = hit[:, :tokens]
    for head in range(1, messages // tokens):
        either = either + hit[:, head * tokens : (head + 1) * tokens]
    either = either.astype(BF)
    step = 512
    for at in range(0, width, step):
        payload[:, at : at + step] = dot_nn(either, grad[:, at : at + step]).astype(BF)
    payload[:, width:] = dot_nn(hit.astype(BF), rows[...]).astype(BF)


def score_kernel(
    heads, inputs, weight, keys, picks, slot_col, low_out, weights_out, send_out, acc
):
    step = pl.program_id(0)

    @pl.when(step == 0)
    def _():
        acc[...] = jnp.zeros_like(acc)

    acc[...] += dot_nn(inputs[...], weight[...])

    @pl.when(step == pl.num_programs(0) - 1)
    def _():
        tokens, cols = acc.shape
        lanes = picks.shape[1]
        blocks = 2 * heads
        half = cols // blocks
        count = keys.shape[0]
        low_out[...] = acc[...].astype(BF)
        pick = picks[...]
        low = pick % 128
        high = pick // 128
        lane_block = iota((tokens, lanes), 1) // (lanes // blocks)
        chosen = jnp.zeros((tokens, lanes), F32)
        for b in range(blocks):
            parts = three(acc[:, b * half : (b + 1) * half])
            block_keys = keys[:, b * half : (b + 1) * half]
            for j in range(count // 128):
                rows = block_keys[j * 128 : (j + 1) * 128]
                score = dot_nt(parts[2], rows) + dot_nt(parts[1], rows) + dot_nt(parts[0], rows)
                got = jnp.take_along_axis(score, low, axis=1)
                chosen = jnp.where((high == j) & (lane_block == b), got, chosen)
        top = lanes // blocks
        even = lane_block % 2 == 0
        other = jnp.where(
            even, pltpu.roll(chosen, lanes - top, axis=1), pltpu.roll(chosen, top, axis=1)
        )
        scores = chosen + other
        head_of = lane_block // 2
        peak = jnp.zeros((tokens, lanes), F32)
        for h in range(heads):
            most = jnp.max(jnp.where(head_of == h, scores, -jnp.inf), axis=1, keepdims=True)
            peak = jnp.where(head_of == h, most, peak)
        raised = jnp.exp(scores - peak)
        total = jnp.zeros((tokens, lanes), F32)
        for h in range(heads):
            part = jnp.sum(jnp.where(head_of == h, raised, 0.0), axis=1, keepdims=True)
            total = jnp.where(head_of == h, part * 0.5, total)
        soft = raised / total
        weights_out[...] = soft
        slots = send_out.shape[0]
        low_soft = soft.astype(BF).astype(F32)
        sent = jnp.zeros((slots, lanes), F32)
        for h in range(heads):
            hit = jnp.where(
                iota((tokens, slots), 1) == slot_col[h * tokens : (h + 1) * tokens], 1.0, 0.0
            ).astype(BF)
            turned = low_soft if h == 0 else pltpu.roll(low_soft, lanes - h * 2 * top, axis=1)
            sent = sent + dot_tn(hit, turned.astype(BF))
        send_out[...] = sent.astype(BF)


def shard_kernel(width, arrived, values, after, back):
    product = dot_nt(arrived[:, :width], values[...])
    pick = arrived[:, width:].astype(I32)
    out = jnp.zeros(pick.shape, F32)
    for j in range(values.shape[0] // 128):
        got = jnp.take_along_axis(product[:, j * 128 : (j + 1) * 128], pick % 128, axis=1)
        out = jnp.where(pick // 128 == j, got, out)
    back[...] = out


def table_kernel(top, arrived, rows, soft, part, spread):
    @pl.when(pl.program_id(0) == 0)
    def _():
        count, slots = spread.shape
        row_t = rows[...].astype(F32).T
        soft_t = soft[...].astype(F32).T
        for at in range(0, slots, 128):
            names = iota((count, 128), 0).astype(F32)
            held = jnp.zeros((count, 128), F32)
            for k in range(top):
                held = held + jnp.where(
                    names == row_t[k : k + 1, at : at + 128], soft_t[k : k + 1, at : at + 128], 0.0
                )
            spread[:, at : at + 128] = held.astype(BF)

    part[...] = dot_nn(spread[...], arrived[...]).astype(BF)


def grad_kernel(heads, returned, slot_col, soft, picks, keys, half_out, query_out, placed):
    tokens, lanes = soft.shape
    blocks = 2 * heads
    top = lanes // blocks
    slots = returned.shape[0]
    head_of = iota((tokens, lanes), 1) // (2 * top)
    parts = three(returned[...])
    slot_grad = jnp.zeros((tokens, lanes), F32)
    for h in range(heads):
        hit = jnp.where(
            iota((tokens, slots), 1) == slot_col[h * tokens : (h + 1) * tokens], 1.0, 0.0
        ).astype(BF)
        got = dot_nn(hit, parts[2]) + dot_nn(hit, parts[1]) + dot_nn(hit, parts[0])
        slot_grad = jnp.where(head_of == h, got, slot_grad)
    weights = soft[...]
    scaled = weights * slot_grad
    mean = jnp.zeros((tokens, lanes), F32)
    for h in range(heads):
        part = jnp.sum(jnp.where(head_of == h, scaled, 0.0), axis=1, keepdims=True)
        mean = jnp.where(head_of == h, part * 0.5, mean)
    score_grad = weights * (slot_grad - mean)
    count = keys.shape[0]
    tiles = count // 128
    pick = picks[...]
    low = pick % 128
    high = pick // 128 + tiles * (iota((tokens, lanes), 1) // top)
    for t in range(tokens):
        left = jnp.where(
            iota((blocks * tiles, lanes), 0) == high[t : t + 1], score_grad[t : t + 1], 0.0
        ).astype(BF)
        right = jnp.where(iota((128, lanes), 0) == low[t : t + 1], 1.0, 0.0).astype(BF)
        placed[t] = dot_nt(left, right)
    half = query_out.shape[1] // blocks
    quarter = half_out.shape[2]
    each = quarter // 128
    for b in range(blocks):
        total = jnp.zeros((tokens, half), F32)
        for q in range(count // quarter):
            for i in range(each):
                row = b * tiles + q * each + i
                sums = placed[:, row, :].astype(BF)
                half_out[q * blocks + b, :, i * 128 : (i + 1) * 128] = sums
                at = (q * each + i) * 128
                total = total + dot_nn(sums, keys[at : at + 128, b * half : (b + 1) * half])
        query_out[:, b * half : (b + 1) * half] = total.astype(BF)


VM = pl.BlockSpec(memory_space=pltpu.VMEM)
LIMIT = 56 * 1024 * 1024


def local(body, out_shape, micros, **more):
    return pl.pallas_call(
        body,
        out_shape=out_shape,
        cost_estimate=pl.CostEstimate(
            flops=micros * 1000000000, bytes_accessed=micros * 1000000, transcendentals=0
        ),
        compiler_params=pltpu.CompilerParams(vmem_limit_bytes=LIMIT),
        **more,
    )


def sds(shape, dtype):
    return jax.ShapeDtypeStruct(shape, dtype)


def on_device(inputs, grad_out, query_weight, sub_keys, values, owner, slot_rows, sub_index):
    tokens, width = inputs.shape
    cols = query_weight.shape[1]
    count = sub_keys.shape[0]
    heads, top = slot_rows.shape[1:]
    blocks = 2 * heads
    lanes = blocks * top
    shards = lax.axis_size("tab")
    groups = lax.axis_size("rep")
    messages = tokens * heads
    capacity = 2 * messages // shards
    slots = shards * capacity
    table_rows = values.shape[0]
    across = functools.partial(lax.all_to_all, axis_name="tab", tiled=True)

    own_row = owner.reshape(tokens, heads).T.reshape(1, messages)
    own_col = own_row.reshape(messages, 1)
    rows4 = jnp.tile(jnp.transpose(slot_rows, (1, 0, 2)).reshape(messages, top), (1, blocks))
    payload, slot_row = local(
        functools.partial(dispatch_kernel, capacity),
        (sds((slots, width + lanes), BF), sds((1, messages), I32)),
        name="dispatch",
        micros=5,
    )(own_row, own_col, grad_out, rows4.astype(BF))
    arrived = across(
        payload.reshape(shards, capacity, width + lanes), split_axis=0, concat_axis=0
    ).reshape(slots, width + lanes)
    slot_col = slot_row.reshape(messages, 1)
    picks = sub_index.reshape(tokens, lanes)

    depth = 512
    low_query, weights, send_weights = local(
        functools.partial(score_kernel, heads),
        (sds((tokens, cols), BF), sds((tokens, lanes), F32), sds((slots, lanes), BF)),
        grid=(width // depth,),
        in_specs=[
            pl.BlockSpec((tokens, depth), lambda i: (0, i)),
            pl.BlockSpec((depth, cols), lambda i: (i, 0)),
            pl.BlockSpec((count, cols), lambda i: (0, 0)),
            pl.BlockSpec((tokens, lanes), lambda i: (0, 0)),
            pl.BlockSpec((messages, 1), lambda i: (0, 0)),
        ],
        out_specs=(
            pl.BlockSpec((tokens, cols), lambda i: (0, 0)),
            pl.BlockSpec((tokens, lanes), lambda i: (0, 0)),
            pl.BlockSpec((slots, lanes), lambda i: (0, 0)),
        ),
        scratch_shapes=[pltpu.VMEM((tokens, cols), F32)],
        name="scores",
        micros=11,
    )(inputs, query_weight, sub_keys, picks, slot_col)

    back = local(
        functools.partial(shard_kernel, width),
        sds((slots, lanes), F32),
        grid=(slots // 128,),
        in_specs=[
            pl.BlockSpec((128, width + lanes), lambda i: (i, 0)),
            pl.BlockSpec((table_rows, width), lambda i: (0, 0)),
            pl.BlockSpec(memory_space=pl.ANY),
        ],
        out_specs=pl.BlockSpec((128, lanes), lambda i: (i, 0)),
        name="shard",
        micros=7,
    )(arrived, values, weights)
    returned = across(back.reshape(shards, capacity, lanes), split_axis=0, concat_axis=0)
    returned = returned.reshape(slots, lanes)

    arrived_weights = across(
        send_weights.reshape(shards, capacity, lanes), split_axis=0, concat_axis=0
    ).reshape(slots, lanes)
    table_part = local(
        functools.partial(table_kernel, top),
        sds((table_rows, width), BF),
        grid=(width // 512,),
        in_specs=[
            pl.BlockSpec((slots, 512), lambda i: (0, i)),
            pl.BlockSpec((slots, lanes), lambda i: (0, width // lanes)),
            pl.BlockSpec((slots, lanes), lambda i: (0, 0)),
        ],
        out_specs=pl.BlockSpec((table_rows, 512), lambda i: (0, i)),
        scratch_shapes=[pltpu.VMEM((table_rows, slots), BF)],
        name="table",
        micros=9,
    )(arrived, arrived, arrived_weights)
    table_pieces = lax.all_to_all(
        table_part.reshape(groups, table_rows // groups, width), "rep", 0, 0, tiled=True
    )
    table_piece = jnp.sum(table_pieces.astype(F32), axis=0).astype(BF)
    table_grad = lax.all_gather(table_piece, "rep", axis=0, tiled=True)

    quarters = shards // blocks
    quarter = count // quarters
    half_grad, query_grad = local(
        functools.partial(grad_kernel, heads),
        (sds((shards, tokens, quarter), BF), sds((tokens, cols), BF)),
        scratch_shapes=[pltpu.VMEM((tokens, blocks * count // 128, 128), F32)],
        name="grads",
        micros=7,
    )(returned, slot_col, weights, picks, sub_keys)
    input_grad = lax.dot_general(
        query_grad, query_weight, (((1,), (1,)), ((), ())), preferred_element_type=F32
    ).astype(BF)

    weight_rows = width // shards
    half = cols // blocks
    early = jnp.concatenate(
        [
            jnp.transpose(inputs.reshape(tokens, shards, weight_rows), (1, 0, 2)),
            jnp.tile(jnp.transpose(low_query.reshape(tokens, blocks, half), (1, 0, 2)), (quarters, 1, 1)),
        ],
        axis=2,
    )
    early = across(early, split_axis=0, concat_axis=0).reshape(shards * tokens, weight_rows + half)
    group_inputs = early[:, :weight_rows]
    group_query = early[:, weight_rows:]
    group_half = across(half_grad, split_axis=0, concat_axis=0).reshape(shards * tokens, quarter)
    group_grad = lax.all_gather(query_grad, "tab", axis=0, tiled=True)
    weight_part = dot_tn(group_inputs, group_grad)
    key_part = dot_tn(group_half, group_query)
    key_rows = count // shards
    members = [[q * blocks + b for b in range(blocks)] for q in range(quarters)]
    key_part = lax.all_to_all(
        key_part.reshape(blocks, key_rows, half), "tab", 0, 0, axis_index_groups=members, tiled=True
    )
    key_part = jnp.transpose(key_part, (1, 0, 2)).reshape(key_rows, cols)
    share = jnp.concatenate([weight_part, key_part], axis=0).astype(BF)
    share_rows = share.shape[0] // groups
    pieces = lax.all_to_all(share.reshape(groups, share_rows, cols), "rep", 0, 0, tiled=True)
    piece = jnp.sum(pieces.astype(F32), axis=0)
    whole = lax.all_gather(piece, "rep", axis=0, tiled=True)
    weight_grad = whole[:weight_rows]
    key_grad = whole[weight_rows:]
    return (input_grad, weight_grad, key_grad, table_grad)


def solution(mesh):
    placed = (
        P(("rep", "tab"), None),
        P(("rep", "tab"), None),
        P(),
        P(),
        P("tab", None),
        P(("rep", "tab"), None, None),
        P(("rep", "tab"), None, None),
        P(("rep", "tab"), None, None, None),
    )
    return jax.shard_map(
        on_device,
        mesh=mesh,
        in_specs=placed,
        out_specs=(P(("rep", "tab"), None), P("tab", None), P("tab", None), P("tab", None)),
        check_vma=False,
    )
```

```python
import jax
import jax.numpy as jnp
from jax import lax
from jax.experimental import pallas as pl
from jax.experimental.pallas import tpu as pltpu
from jax.sharding import PartitionSpec as P

BF = jnp.bfloat16
F32 = jnp.float32
I32 = jnp.int32


def dot_nn(a, b):
    return lax.dot_general(a, b, (((1,), (0,)), ((), ())), preferred_element_type=F32)


def dot_nt(a, b):
    return lax.dot_general(a, b, (((1,), (1,)), ((), ())), preferred_element_type=F32)


def dot_tn(a, b):
    return lax.dot_general(a, b, (((0,), (0,)), ((), ())), preferred_element_type=F32)


def three(x):
    a = x.astype(BF)
    rest = x - a.astype(F32)
    b = rest.astype(BF)
    c = (rest - b.astype(F32)).astype(BF)
    return a, b, c


def iota(shape, dim):
    return lax.broadcasted_iota(I32, shape, dim)

MESH = pl.DeviceIdType.MESH
TURNS = (0, 1, 3, 2)


def whole_kernel(
    own, rows_t, picks_t, grad, inputs, weight, keys, values,
    in_grad, w_grad, k_grad, t_grad,
    pay, arr, inp, wt, key, val, acc, low, soft, score, wsend, wrecv, back, ret, spread,
    tpart, tcore, thalf, tz, placed, hsend, hrecv, lrecv, qg, gq, ginp, ksend, krecv, wacc,
    psend, precv, load_sem, ssem, rsem,
):
    heads, tokens = own.shape
    width = grad.shape[1]
    shards, capacity, wide = pay.shape
    lanes = picks_t.shape[0]
    blocks = 2 * heads
    top = lanes // blocks
    cols = acc.shape[1]
    half = cols // blocks
    count = key.shape[0]
    tiles = count // 128
    table_rows = val.shape[0]
    slots = shards * capacity
    side = 4
    band = slots // side
    me, r = lax.axis_index("tab"), lax.axis_index("rep")
    mx, my = me // side, lax.rem(me, side)
    mz, mc = r // 2, lax.rem(r, 2)
    used = [0]

    def at_tab(dx, dy):
        return lax.rem(mx + dx, side) * side + lax.rem(my + dy, side)

    def send(src, dst, device, numbers=None):
        if numbers is None:
            numbers = (used[0], used[0])
            used[0] += 1
        copy = pltpu.make_async_remote_copy(
            src_ref=src,
            dst_ref=dst,
            send_sem=ssem.at[numbers[0]],
            recv_sem=rsem.at[numbers[1]],
            device_id=device,
            device_id_type=MESH,
        )
        copy.start()
        return copy

    loads = [pltpu.make_async_copy(inputs, inp, load_sem.at[0])]
    depth = width // 4
    for i in range(4):
        piece = pl.ds(i * depth, depth)
        loads.append(pltpu.make_async_copy(weight.at[piece], wt.at[piece], load_sem.at[1 + i]))
    loads.append(pltpu.make_async_copy(keys, key, load_sem.at[5]))
    loads.append(pltpu.make_async_copy(values, val, load_sem.at[6]))
    for load in loads:
        load.start()
    barrier = pltpu.get_barrier_semaphore()
    for d in range(1, shards):
        pl.semaphore_signal(
            barrier, inc=1, device_id={"tab": lax.rem(me + d, shards)}, device_id_type=MESH
        )
    for d in range(1, 8):
        pl.semaphore_signal(
            barrier, inc=1, device_id={"rep": lax.rem(r + d, 8)}, device_id_type=MESH
        )

    owned = jnp.concatenate([own[h : h + 1, :] for h in range(heads)], axis=1)
    messages = heads * tokens
    across = jnp.broadcast_to(owned, (messages, messages))
    same = across == across.T
    earlier = iota((messages, messages), 0) < iota((messages, messages), 1)
    rank = jnp.sum(jnp.where(same & earlier, 1.0, 0.0), axis=0, keepdims=True).astype(I32)
    place = owned * capacity + rank
    row_lanes = []
    for h in range(heads):
        one = rows_t[h * top : (h + 1) * top, :].astype(F32)
        row_lanes.append(jnp.concatenate([one] * blocks, axis=0).T)
    row_lanes = jnp.concatenate(row_lanes, axis=0).astype(BF)

    outgoing = []
    for turn, dx in enumerate(TURNS):
        gx = lax.rem(mx + dx, side)
        hit = jnp.where(iota((band, messages), 0) + gx * band == place, 1.0, 0.0)
        either = hit[:, :tokens]
        for h in range(1, heads):
            either = either + hit[:, h * tokens : (h + 1) * tokens]
        either = either.astype(BF)
        here = pl.ds(gx * side, side)
        for at in range(0, width, 512):
            block = dot_nn(either, grad[:, at : at + 512]).astype(BF)
            pay[here, :, at : at + 512] = block.reshape(side, capacity, 512)
        block = dot_nn(hit.astype(BF), row_lanes).astype(BF)
        pay[here, :, width:] = block.reshape(side, capacity, wide - width)
        if turn == 0:
            pl.semaphore_wait(barrier, shards + 6)
        for dy in TURNS:
            if dx or dy:
                p = at_tab(dx, dy)
                outgoing.append(send(pay.at[p], arr.at[me], {"tab": p}))
            else:
                outgoing.append(None)
    arr[me] = pay[me]

    loads[0].wait()
    for i in range(4):
        loads[1 + i].wait()
        part = dot_nn(inp[:, i * depth : (i + 1) * depth], wt[i * depth : (i + 1) * depth, :])
        acc[...] = part if i == 0 else acc[...] + part
    low[...] = acc[...].astype(BF)
    lows = []
    for d in range(1, 8):
        p = lax.rem(r + d, 8)
        piece = pl.ds(pl.multiple_of((p // 2) * half, half), half)
        lows.append(send(low.at[:, piece], lrecv.at[r], {"rep": p}))
    lrecv[r] = low[:, pl.ds(pl.multiple_of(mz * half, half), half)]
    pick = picks_t[...].T
    low_pick = pick % 128
    high_pick = pick // 128
    lane_block = iota((tokens, lanes), 1) // top
    head_of = lane_block // 2
    chosen = jnp.zeros((tokens, lanes), F32)
    loads[5].wait()
    for b in range(blocks):
        parts = three(acc[:, b * half : (b + 1) * half])
        for j in range(tiles):
            names = key[j * 128 : (j + 1) * 128, b * half : (b + 1) * half]
            part = dot_nt(parts[2], names) + dot_nt(parts[1], names) + dot_nt(parts[0], names)
            got = jnp.take_along_axis(part, low_pick, axis=1)
            chosen = jnp.where((high_pick == j) & (lane_block == b), got, chosen)
    even = lane_block % 2 == 0
    other = jnp.where(
        even, pltpu.roll(chosen, lanes - top, axis=1), pltpu.roll(chosen, top, axis=1)
    )
    scores = chosen + other

    def over_heads(x, fill, reduce):
        out = jnp.zeros((tokens, lanes), F32)
        for h in range(heads):
            one = reduce(jnp.where(head_of == h, x, fill), axis=1, keepdims=True)
            out = jnp.where(head_of == h, one, out)
        return out

    raised = jnp.exp(scores - over_heads(scores, -jnp.inf, jnp.max))
    weights = raised / (over_heads(raised, 0.0, jnp.sum) * 0.5)
    soft[...] = weights
    low_soft = weights.astype(BF).astype(F32)

    def hits(h):
        column = jnp.broadcast_to(place[:, h * tokens : (h + 1) * tokens], (tokens, tokens)).T
        column = jnp.concatenate([column] * (slots // tokens), axis=1)
        return jnp.where(iota((tokens, slots), 1) == column, 1.0, 0.0).astype(BF)

    sent = jnp.zeros((slots, lanes), F32)
    for h in range(heads):
        turned = low_soft if h == 0 else pltpu.roll(low_soft, lanes - h * 2 * top, axis=1)
        sent = sent + dot_tn(hits(h), turned.astype(BF))
    wsend[...] = sent.astype(BF).reshape(shards, capacity, lanes)
    weighing = []
    for dx in TURNS:
        for dy in TURNS:
            if dx or dy:
                p = at_tab(dx, dy)
                weighing.append(send(wsend.at[p], wrecv.at[me], {"tab": p}))
    wrecv[me] = wsend[me]

    loads[6].wait()
    returning = []
    for turn, dx in enumerate(TURNS):
        for copy in outgoing[turn * side : (turn + 1) * side]:
            if copy is not None:
                copy.wait_recv()
        gx = lax.rem(mx - dx + side, side)
        here = pl.ds(gx * side, side)
        product = dot_nt(arr[here, :, :width].reshape(band, width), val[...])
        name = arr[here, :, width:].reshape(band, lanes).astype(I32)
        out = jnp.zeros((band, lanes), F32)
        for j in range(table_rows // 128):
            got = jnp.take_along_axis(product[:, j * 128 : (j + 1) * 128], name % 128, axis=1)
            out = jnp.where(name // 128 == j, got, out)
        back[here] = out.reshape(side, capacity, lanes)
        for dy in TURNS:
            if dx or dy:
                p = at_tab(side - dx, side - dy)
                returning.append(send(back.at[p], ret.at[me], {"tab": p}))
    ret[me] = back[me]
    spreading = []
    piece_width = width // shards
    for dx in TURNS:
        for dy in TURNS:
            if dx or dy:
                p = at_tab(dx, dy)
                piece = pl.ds(pl.multiple_of(p * piece_width, piece_width), piece_width)
                spreading.append(send(inp.at[:, piece], ginp.at[me], {"tab": p}))
    ginp[me] = inp[:, pl.ds(pl.multiple_of(me * piece_width, piece_width), piece_width)]

    for copy in weighing:
        copy.wait_recv()

    def spread_band(g, carry):
        here = pl.ds(g * side, side)
        row_t = arr[here, :, width:].reshape(band, lanes).astype(F32).T
        soft_t = wrecv[here].reshape(band, lanes).astype(F32).T
        names = iota((table_rows, band), 0).astype(F32)
        held = jnp.zeros((table_rows, band), F32)
        for k in range(top):
            held = held + jnp.where(names == row_t[k : k + 1], soft_t[k : k + 1], 0.0)
        spread[:, pl.ds(pl.multiple_of(g * band, band), band)] = held.astype(BF)
        return carry

    lax.fori_loop(0, side, spread_band, 0)

    for copy in returning:
        copy.wait_recv()
    parts = three(ret[...].reshape(slots, lanes))
    slot_grad = jnp.zeros((tokens, lanes), F32)
    for h in range(heads):
        hit = hits(h)
        got = dot_nn(hit, parts[2]) + dot_nn(hit, parts[1]) + dot_nn(hit, parts[0])
        slot_grad = jnp.where(head_of == h, got, slot_grad)
    weights = soft[...]
    mean = over_heads(weights * slot_grad, 0.0, jnp.sum) * 0.5
    score[0] = weights * (slot_grad - mean)
    score[1] = low_pick.astype(F32)
    score[2] = (high_pick + tiles * lane_block).astype(F32)

    def place_band(i, carry):
        here = pl.ds(pl.multiple_of(i * 8, 8), 8)
        amount, low8, high8 = score[0, here, :], score[1, here, :], score[2, here, :]
        high_names = iota((blocks * tiles, lanes), 0).astype(F32)
        low_names = iota((128, lanes), 0).astype(F32)
        for u in range(8):
            left = jnp.where(high_names == high8[u : u + 1], amount[u : u + 1], 0.0).astype(BF)
            right = jnp.where(low_names == low8[u : u + 1], 1.0, 0.0).astype(BF)
            placed[i * 8 + u] = dot_nt(left, right)
        return carry

    lax.fori_loop(0, tokens // 8, place_band, 0)
    for b in range(blocks):
        total = jnp.zeros((tokens, half), F32)
        for j in range(tiles):
            sums = placed[:, b * tiles + j, :].astype(BF)
            hsend[2 * b + j % 2, :, (j // 2) * 128 : (j // 2 + 1) * 128] = sums
            total = total + dot_nn(sums, key[j * 128 : (j + 1) * 128, b * half : (b + 1) * half])
        qg[:, b * half : (b + 1) * half] = total.astype(BF)

    middle = cols // 2
    left, right = pl.ds(0, middle), pl.ds(middle, middle)
    first = []
    for d in (1, 3, 2):
        p = at_tab(0, d)
        first.append((d, 0, send(qg.at[:, left], gq.at[me, :, left], {"tab": p})))
        p = at_tab(d, 0)
        first.append((d, 1, send(qg.at[:, right], gq.at[me, :, right], {"tab": p})))
    second = []

    def forward(e, kind):
        for d in (1, 3, 2):
            if kind == 0:
                part = gq.at[at_tab(0, side - e), :, left]
                second.append(send(part, part, {"tab": at_tab(d, 0)}))
            else:
                part = gq.at[at_tab(side - e, 0), :, right]
                second.append(send(part, part, {"tab": at_tab(0, d)}))

    gq[me] = qg[...]
    for kind in (0, 1):
        forward(0, kind)
    halves = []
    for d in range(1, 8):
        p = lax.rem(r + d, 8)
        halves.append(send(hsend.at[p], hrecv.at[r], {"rep": p}))
    hrecv[r] = hsend[r]

    for at in range(0, width, 512):
        column = arr[:, :, at : at + 512].reshape(slots, 512)
        tpart[:, at : at + 512] = dot_nn(spread[...], column).astype(BF)
    own_half = table_rows // 2
    mate = mz * 2 + 1 - mc
    mine = pl.ds(pl.multiple_of(mc * own_half, own_half), own_half)
    theirs = pl.ds(pl.multiple_of((1 - mc) * own_half, own_half), own_half)
    swap = send(tpart.at[theirs], tcore, {"rep": mate})
    for e, kind, copy in first:
        copy.wait_recv()
        forward(e, kind)
    for at in range(0, width, 512):
        in_grad[:, at : at + 512] = dot_nt(qg[...], wt[at : at + 512, :]).astype(BF)

    swap.wait_recv()
    quarter = own_half // 4
    for z in range(4):
        row = pl.multiple_of(mc * own_half, own_half) + z * quarter
        mixed = tpart[pl.ds(row, quarter), :].astype(F32)
        mixed = mixed + tcore[z * quarter : (z + 1) * quarter, :].astype(F32)
        thalf[z] = mixed.astype(BF)
    table_in = []
    for d in (1, 3, 2):
        z = lax.rem(mz + d, 4)
        table_in.append(send(thalf.at[z], tz.at[mz], {"rep": z * 2 + mc}))
    tz[mz] = thalf[mz]

    for copy in lows + halves:
        copy.wait_recv()
    key_part = dot_tn(
        hrecv[...].reshape(8 * tokens, count // 2), lrecv[...].reshape(8 * tokens, half)
    )
    key_rows = count // shards
    ksend[...] = key_part.astype(BF).reshape(8, key_rows, half)
    key_base = used[0]
    used[0] += shards
    key_out = []
    for i in range(2):
        for dx in range(side):
            x = lax.rem(mx + dx, side)
            p = x * side + 2 * mc + i
            copy = pltpu.make_async_remote_copy(
                src_ref=ksend.at[x * 2 + i],
                dst_ref=krecv.at[me],
                send_sem=ssem.at[key_base + i * side + dx],
                recv_sem=rsem.at[key_base + me],
                device_id={"tab": p},
                device_id_type=MESH,
            )
            key_out.append((i, dx, copy))
            if dx:
                copy.start()
            else:

                @pl.when(my != 2 * mc + i)
                def _(copy=copy):
                    copy.start()

                @pl.when(my == 2 * mc + i)
                def _(x=x, i=i):
                    krecv[me] = ksend[x * 2 + i]

    for copy in table_in:
        copy.wait_recv()
    summed = tz[0].astype(F32)
    for z in range(1, 4):
        summed = summed + tz[z].astype(F32)
    table_row = pl.multiple_of(mc * own_half + mz * quarter, quarter)
    table_mine = t_grad.at[pl.ds(table_row, quarter)]
    table_mine[...] = summed.astype(BF)
    table_out = []
    for d in (1, 3, 2):
        z = lax.rem(mz + d, 4)
        table_out.append((d, send(table_mine, table_mine, {"rep": z * 2 + mc})))
    table_last = [send(table_mine, table_mine, {"rep": mate})]

    key_last = used[0]
    used[0] += 8
    keeper = my // 2
    key_block = pl.ds(pl.multiple_of(mz * half, half), half)

    def key_share(d):
        return pltpu.make_async_remote_copy(
            src_ref=k_grad.at[:, key_block],
            dst_ref=k_grad.at[:, key_block],
            send_sem=ssem.at[key_last + d],
            recv_sem=rsem.at[key_last + mz],
            device_id={"rep": lax.rem(r + d, 8)},
            device_id_type=MESH,
        )

    @pl.when(keeper == mc)
    def _():
        for d in range(1, shards):
            q = lax.rem(me + d, shards)
            pltpu.make_async_remote_copy(
                src_ref=ksend.at[0],
                dst_ref=krecv.at[q],
                send_sem=ssem.at[key_base],
                recv_sem=rsem.at[key_base + q],
                device_id={"tab": q},
                device_id_type=MESH,
            ).wait_recv()
        total = krecv[0].astype(F32)
        for q in range(1, shards):
            total = total + krecv[q].astype(F32)
        k_grad[:, key_block] = total
        for d in range(1, 8):
            key_share(d).start()

    for copy in spreading + second:
        copy.wait_recv()
    for g in range(side):
        near = ginp[g * side : (g + 1) * side].reshape(side * tokens, piece_width)
        far = gq[g * side : (g + 1) * side].reshape(side * tokens, cols)
        part = dot_tn(near, far)
        wacc[...] = part if g == 0 else wacc[...] + part
    share = piece_width // 8
    psend[...] = wacc[...].astype(BF).reshape(8, share, cols)
    sums_in = []
    for d in range(1, 8):
        p = lax.rem(r + d, 8)
        sums_in.append(send(psend.at[p], precv.at[r], {"rep": p}))
    precv[r] = psend[r]
    for d, copy in table_out:
        copy.wait_recv()
        row = pl.multiple_of(mc * own_half + lax.rem(mz - d + 4, 4) * quarter, quarter)
        part = t_grad.at[pl.ds(row, quarter)]
        table_last.append(send(part, part, {"rep": mate}))
    for copy in sums_in:
        copy.wait_recv()
    total = precv[0].astype(F32)
    for q in range(1, 8):
        total = total + precv[q].astype(F32)
    mine = w_grad.at[pl.ds(pl.multiple_of(r * share, share), share)]
    mine[...] = total
    sums_out, sums_last = [], []
    for d in (1, 3, 2):
        z = lax.rem(mz + d, 4)
        sums_out.append((d, send(mine, mine, {"rep": z * 2 + mc})))
    sums_last.append(send(mine, mine, {"rep": mate}))
    for d, copy in sums_out:
        copy.wait_recv()
        row = pl.multiple_of((lax.rem(mz - d + 4, 4) * 2 + mc) * share, share)
        part = w_grad.at[pl.ds(row, share)]
        sums_last.append(send(part, part, {"rep": mate}))

    for b in range(4):

        @pl.when((b != mz) | (keeper != mc))
        def _(b=b):
            part = k_grad.at[:, b * half : (b + 1) * half]
            pltpu.make_async_remote_copy(
                src_ref=part,
                dst_ref=part,
                send_sem=ssem.at[key_last],
                recv_sem=rsem.at[key_last + b],
                device_id={"rep": mate},
                device_id_type=MESH,
            ).wait_recv()

    for copy in table_last + sums_last:
        copy.wait_recv()
    for i, dx, copy in key_out:
        if dx:
            copy.wait_send()
        else:

            @pl.when(my != 2 * mc + i)
            def _(copy=copy):
                copy.wait_send()

    @pl.when(keeper == mc)
    def _():
        for d in range(1, 8):
            key_share(d).wait_send()

    done = [copy for copy in outgoing if copy is not None] + lows + weighing + returning
    done = done + spreading + [copy for _, _, copy in first] + second + halves + [swap]
    done = done + table_in + [copy for _, copy in table_out] + table_last
    done = done + sums_in + [copy for _, copy in sums_out] + sums_last
    for copy in done:
        copy.wait_send()
    assert used[0] <= ssem.shape[0]


def sds(shape, dtype):
    return jax.ShapeDtypeStruct(shape, dtype)


def on_device(inputs, grad_out, query_weight, sub_keys, values, owner, slot_rows, sub_index):
    tokens, width = inputs.shape
    cols = query_weight.shape[1]
    count = sub_keys.shape[0]
    heads, top = slot_rows.shape[1:]
    blocks = 2 * heads
    lanes = blocks * top
    half = cols // blocks
    shards = lax.axis_size("tab")
    capacity = 2 * tokens * heads // shards
    slots = shards * capacity
    table_rows = values.shape[0]
    own = jnp.transpose(owner, (1, 2, 0)).reshape(heads, tokens)
    rows_t = jnp.transpose(slot_rows, (1, 2, 0)).reshape(heads * top, tokens)
    picks_t = jnp.transpose(sub_index, (1, 2, 3, 0)).reshape(lanes, tokens)
    vmem = pl.BlockSpec(memory_space=pltpu.VMEM)
    anywhere = pl.BlockSpec(memory_space=pl.ANY)
    V = pltpu.VMEM
    wide = width + lanes
    return pl.pallas_call(
        whole_kernel,
        out_shape=(
            sds((tokens, width), BF),
            sds((width // shards, cols), F32),
            sds((count // shards, cols), F32),
            sds((table_rows, width), BF),
        ),
        in_specs=[vmem] * 4 + [anywhere] * 4,
        out_specs=(vmem,) * 4,
        scratch_shapes=[
            V((shards, capacity, wide), BF),
            V((shards, capacity, wide), BF),
            V((tokens, width), BF),
            V((width, cols), BF),
            V((count, cols), BF),
            V((table_rows, width), BF),
            V((tokens, cols), F32),
            V((tokens, cols), BF),
            V((tokens, lanes), F32),
            V((3, tokens, lanes), F32),
            V((shards, capacity, lanes), BF),
            V((shards, capacity, lanes), BF),
            V((shards, capacity, lanes), F32),
            V((shards, capacity, lanes), F32),
            V((table_rows, slots), BF),
            V((table_rows, width), BF),
            V((table_rows // 2, width), BF),
            V((4, table_rows // 8, width), BF),
            V((4, table_rows // 8, width), BF),
            V((tokens, blocks * count // 128, 128), F32),
            V((8, tokens, count // 2), BF),
            V((8, tokens, count // 2), BF),
            V((8, tokens, half), BF),
            V((tokens, cols), BF),
            V((shards, tokens, cols), BF),
            V((shards, tokens, width // shards), BF),
            V((8, count // shards, half), BF),
            V((shards, count // shards, half), BF),
            V((width // shards, cols), F32),
            V((8, width // shards // 8, cols), BF),
            V((8, width // shards // 8, cols), BF),
            pltpu.SemaphoreType.DMA((7,)),
            pltpu.SemaphoreType.DMA((192,)),
            pltpu.SemaphoreType.DMA((192,)),
        ],
        compiler_params=pltpu.CompilerParams(
            collective_id=0, has_side_effects=True, vmem_limit_bytes=60 * 1024 * 1024
        ),
        name="whole",
    )(own, rows_t, picks_t, grad_out, inputs, query_weight, sub_keys, values)


def solution(mesh):
    placed = (
        P(("rep", "tab"), None),
        P(("rep", "tab"), None),
        P(),
        P(),
        P("tab", None),
        P(("rep", "tab"), None, None),
        P(("rep", "tab"), None, None),
        P(("rep", "tab"), None, None, None),
    )
    return jax.shard_map(
        on_device,
        mesh=mesh,
        in_specs=placed,
        out_specs=(P(("rep", "tab"), None), P("tab", None), P("tab", None), P("tab", None)),
        check_vma=False,
    )
```

```python
import jax
import jax.numpy as jnp
from jax import lax
from jax.experimental import pallas as pl
from jax.experimental.pallas import tpu as pltpu
from jax.sharding import PartitionSpec as P

BF = jnp.bfloat16
F32 = jnp.float32
I32 = jnp.int32


def dot_nn(a, b):
    return lax.dot_general(a, b, (((1,), (0,)), ((), ())), preferred_element_type=F32)


def dot_nt(a, b):
    return lax.dot_general(a, b, (((1,), (1,)), ((), ())), preferred_element_type=F32)


def dot_tn(a, b):
    return lax.dot_general(a, b, (((0,), (0,)), ((), ())), preferred_element_type=F32)


def three(x):
    a = x.astype(BF)
    rest = x - a.astype(F32)
    b = rest.astype(BF)
    c = (rest - b.astype(F32)).astype(BF)
    return a, b, c


def iota(shape, dim):
    return lax.broadcasted_iota(I32, shape, dim)

MESH = pl.DeviceIdType.MESH
NEAR = (1, 3, 2)


class Copies:
    def __init__(self, send_sems, recv_sems):
        self.send_sems, self.recv_sems = send_sems, recv_sems
        self.copies, self.got = [], []
        self.used = 0

    def take(self, number):
        self.used += number
        assert self.used <= self.send_sems.shape[0]
        return self.used - number

    def send(self, src, dst, device):
        at = self.take(1)
        copy = pltpu.make_async_remote_copy(
            src_ref=src,
            dst_ref=dst,
            send_sem=self.send_sems.at[at],
            recv_sem=self.recv_sems.at[at],
            device_id=device,
            device_id_type=MESH,
        )
        copy.start()
        self.copies.append(copy)
        self.got.append(False)
        return len(self.copies) - 1

    def wait(self, *which):
        for i in which:
            if not self.got[i]:
                self.copies[i].wait_recv()
                self.got[i] = True

    def finish(self):
        self.wait(*range(len(self.copies)))
        for copy in self.copies:
            copy.wait_send()


def whole_kernel(
    own, rows_t, picks_t, grad, inputs, weight, keys, values,
    in_grad, w_grad, k_grad, t_grad,
    pay, mid, arr, inp, wt, key, val, acc, low, soft, score, wsend, wrecv, back, ret, spread,
    tpart, tcore, thalf, tz, placed, hsend, hrecv, lrecv, qg, gq, ginp, near, ksend, krecv, kfin,
    psend, precv, wfin, load_sem, ssem, rsem,
):
    heads, tokens = own.shape
    width = grad.shape[1]
    side, rows = pay.shape[1], pay.shape[3]
    shards = side * side
    lanes = picks_t.shape[0]
    blocks = 2 * heads
    top = lanes // blocks
    cols = acc.shape[1]
    half = cols // blocks
    count = key.shape[0]
    tiles = count // 128
    table_rows = val.shape[0]
    slots = 2 * shards * rows
    me, r = lax.axis_index("tab"), lax.axis_index("rep")
    mx, my = me // side, lax.rem(me, side)
    mz, mc = r // 2, lax.rem(r, 2)
    mate = {"rep": mz * 2 + 1 - mc}
    copies = Copies(ssem, rsem)
    send, wait = copies.send, copies.wait

    def up(at, by):
        return lax.rem(at + by + side, side)

    def tab(dx, dy):
        return up(mx, dx) * side + up(my, dy)

    def at_z(d):
        return {"rep": up(mz, d) * 2 + mc}

    loads = [pltpu.make_async_copy(inputs, inp, load_sem.at[0])]
    depth = width // 4
    for i in range(4):
        piece = pl.ds(i * depth, depth)
        loads.append(pltpu.make_async_copy(weight.at[piece], wt.at[piece], load_sem.at[1 + i]))
    loads.append(pltpu.make_async_copy(keys, key, load_sem.at[5]))
    loads.append(pltpu.make_async_copy(values, val, load_sem.at[6]))
    for load in loads:
        load.start()
    barrier = pltpu.get_barrier_semaphore()
    for d in range(1, shards):
        pl.semaphore_signal(
            barrier, inc=1, device_id={"tab": lax.rem(me + d, shards)}, device_id_type=MESH
        )
    for d in range(1, 8):
        pl.semaphore_signal(
            barrier, inc=1, device_id={"rep": lax.rem(r + d, 8)}, device_id_type=MESH
        )

    owned = jnp.concatenate([own[h : h + 1, :] for h in range(heads)], axis=1)
    messages = heads * tokens
    across = jnp.broadcast_to(owned, (messages, messages))
    same = across == across.T
    earlier = iota((messages, messages), 0) < iota((messages, messages), 1)
    rank = jnp.sum(jnp.where(same & earlier, 1.0, 0.0), axis=0, keepdims=True).astype(I32)
    place = (rank // rows) * (shards * rows) + owned * rows + rank % rows

    def hit_rows(part):
        at = iota((shards * rows, messages), 0) + part * shards * rows
        return jnp.where(at == place, 1.0, 0.0)

    phase_one = {}
    for part in range(2):
        hit = hit_rows(part)
        either = hit[:, :tokens]
        for h in range(1, heads):
            either = either + hit[:, h * tokens : (h + 1) * tokens]
        either = either.astype(BF)
        for at in range(0, width, 512):
            block = dot_nn(either, grad[:, at : at + 512]).astype(BF)
            pay[part, :, :, :, at : at + 512] = block.reshape(side, side, rows, 512)
        if part == 0:
            pl.semaphore_wait(barrier, shards + 6)
        for d in NEAR:
            for e in (0,) + NEAR:
                if part == 0:
                    src, device = pay.at[0, up(mx, e), up(my, d)], {"tab": tab(0, d)}
                    onward = mid.at[0, my, up(mx, e)]
                else:
                    src, device = pay.at[1, up(mx, d), up(my, e)], {"tab": tab(d, 0)}
                    onward = mid.at[1, mx, up(my, e)]
                dst = onward if e else arr.at[part, me]
                phase_one[part, d, e] = send(src, dst, device)
    phase_two = {}

    def pass_on(part, d, e):
        if part == 0:
            src = mid.at[0, up(my, -d), up(mx, e)] if d else pay.at[0, up(mx, e), my]
            dst, device = arr.at[0, tab(0, -d)], {"tab": tab(e, 0)}
        else:
            src = mid.at[1, up(mx, -d), up(my, e)] if d else pay.at[1, mx, up(my, e)]
            dst, device = arr.at[1, tab(-d, 0)], {"tab": tab(0, e)}
        phase_two[part, d, e] = send(src, dst, device)

    for part in range(2):
        for e in NEAR:
            pass_on(part, 0, e)
        arr[part, me] = pay[part, mx, my]

    loads[0].wait()
    for i in range(4):
        loads[1 + i].wait()
        piece = dot_nn(inp[:, i * depth : (i + 1) * depth], wt[i * depth : (i + 1) * depth, :])
        acc[...] = piece if i == 0 else acc[...] + piece
    low[...] = acc[...].astype(BF)
    lows = []
    for d in range(1, 8):
        p = lax.rem(r + d, 8)
        piece = pl.ds(pl.multiple_of((p // 2) * half, half), half)
        lows.append(send(low.at[:, piece], lrecv.at[r], {"rep": p}))
    lrecv[r] = low[:, pl.ds(pl.multiple_of(mz * half, half), half)]
    pick = picks_t[...].T
    low_pick = pick % 128
    high_pick = pick // 128
    lane_block = iota((tokens, lanes), 1) // top
    head_of = lane_block // 2
    chosen = jnp.zeros((tokens, lanes), F32)
    loads[5].wait()
    for b in range(blocks):
        parts = three(acc[:, b * half : (b + 1) * half])
        for j in range(tiles):
            names = key[j * 128 : (j + 1) * 128, b * half : (b + 1) * half]
            part = dot_nt(parts[2], names) + dot_nt(parts[1], names) + dot_nt(parts[0], names)
            got = jnp.take_along_axis(part, low_pick, axis=1)
            chosen = jnp.where((high_pick == j) & (lane_block == b), got, chosen)
    even = lane_block % 2 == 0
    other = jnp.where(
        even, pltpu.roll(chosen, lanes - top, axis=1), pltpu.roll(chosen, top, axis=1)
    )
    scores = chosen + other

    def over_heads(x, fill, reduce):
        out = jnp.zeros((tokens, lanes), F32)
        for h in range(heads):
            one = reduce(jnp.where(head_of == h, x, fill), axis=1, keepdims=True)
            out = jnp.where(head_of == h, one, out)
        return out

    raised = jnp.exp(scores - over_heads(scores, -jnp.inf, jnp.max))
    weights = raised / (over_heads(raised, 0.0, jnp.sum) * 0.5)
    soft[...] = weights
    low_soft = weights.astype(BF).astype(F32)

    def hits(h):
        column = jnp.broadcast_to(place[:, h * tokens : (h + 1) * tokens], (tokens, tokens)).T
        column = jnp.concatenate([column] * (slots // tokens), axis=1)
        return jnp.where(iota((tokens, slots), 1) == column, 1.0, 0.0).astype(BF)

    sent = jnp.zeros((slots, 2 * lanes), F32)
    for h in range(heads):
        one = rows_t[h * top : (h + 1) * top, :].astype(F32)
        numbers = jnp.concatenate([one] * blocks, axis=0).T
        turned = low_soft if h == 0 else pltpu.roll(low_soft, lanes - h * 2 * top, axis=1)
        sent = sent + dot_tn(hits(h), jnp.concatenate([numbers, turned], axis=1).astype(BF))
    wsend[...] = sent.astype(BF).reshape(2, shards, rows, 2 * lanes)

    def pass_all(d):
        for e in (0,) + NEAR:
            for part in range(2):
                wait(phase_one[part, d, e])
                if e:
                    pass_on(part, d, e)

    pass_all(1)
    weighing = []
    for dx in range(side):
        for dy in range(side):
            if dx or dy:
                p = tab(dx, dy)
                weighing.append(send(wsend.at[:, p], wrecv.at[:, me], {"tab": p}))
    wrecv[:, me] = wsend[:, me]
    pass_all(3)
    pass_all(2)

    wait(*weighing)
    band = 128
    per_band = band // rows

    def spread_band(g, carry):
        part, at = g // (shards // per_band), lax.rem(g, shards // per_band) * per_band
        block = wrecv[part, pl.ds(at, per_band)].reshape(band, 2 * lanes).astype(F32)
        row_t, soft_t = block[:, :lanes].T, block[:, lanes:].T
        names = iota((table_rows, band), 0).astype(F32)
        held = jnp.zeros((table_rows, band), F32)
        for k in range(top):
            held = held + jnp.where(names == row_t[k : k + 1], soft_t[k : k + 1], 0.0)
        spread[:, pl.ds(pl.multiple_of(g * band, band), band)] = held.astype(BF)
        return carry

    lax.fori_loop(0, slots // band, spread_band, 0)

    loads[6].wait()
    for d in (0,) + NEAR:
        for e in NEAR:
            for part in range(2):
                wait(phase_two[part, d, e])
    for part in range(2):
        for q in range(0, shards, per_band):
            here = slice(q, q + per_band)
            product = dot_nt(arr[part, here].reshape(band, width), val[...])
            name = wrecv[part, here, :, :lanes].reshape(band, lanes).astype(I32)
            out = jnp.zeros((band, lanes), F32)
            for j in range(table_rows // 128):
                got = jnp.take_along_axis(product[:, j * 128 : (j + 1) * 128], name % 128, axis=1)
                out = jnp.where(name // 128 == j, got, out)
            back[part, here] = out.reshape(per_band, rows, lanes)
    returning = []
    for dx in range(side):
        for dy in range(side):
            if dx or dy:
                p = tab(dx, dy)
                returning.append(send(back.at[:, p], ret.at[:, me], {"tab": p}))
    ret[:, me] = back[:, me]
    spreading = []
    piece_width = width // shards
    for dx in (0,) + NEAR:
        for dy in (0,) + NEAR:
            if dx or dy:
                p = tab(dx, dy)
                piece = pl.ds(pl.multiple_of(p * piece_width, piece_width), piece_width)
                spreading.append(send(inp.at[:, piece], ginp.at[me], {"tab": p}))
    ginp[me] = inp[:, pl.ds(pl.multiple_of(me * piece_width, piece_width), piece_width)]

    own_half = table_rows // 2
    quarter = own_half // 4
    for at in range(0, width, 512):
        column = arr[:, :, :, at : at + 512].reshape(slots, 512)
        tpart[:, at : at + 512] = dot_nn(spread[...], column).astype(BF)
    swaps = {}
    for d in NEAR + (0,):
        z = up(mz, d)
        row = pl.multiple_of((1 - mc) * own_half + z * quarter, quarter)
        swaps[d] = send(tpart.at[pl.ds(row, quarter)], tcore.at[z], mate)

    wait(*returning)
    parts = three(ret[...].reshape(slots, lanes))
    slot_grad = jnp.zeros((tokens, lanes), F32)
    for h in range(heads):
        hit = hits(h)
        got = dot_nn(hit, parts[2]) + dot_nn(hit, parts[1]) + dot_nn(hit, parts[0])
        slot_grad = jnp.where(head_of == h, got, slot_grad)
    weights = soft[...]
    mean = over_heads(weights * slot_grad, 0.0, jnp.sum) * 0.5
    score[0] = weights * (slot_grad - mean)
    score[1] = low_pick.astype(F32)
    score[2] = (high_pick + tiles * lane_block).astype(F32)

    def place_band(i, carry):
        here = pl.ds(pl.multiple_of(i * 8, 8), 8)
        amount, low8, high8 = score[0, here, :], score[1, here, :], score[2, here, :]
        high_names = iota((blocks * tiles, lanes), 0).astype(F32)
        low_names = iota((128, lanes), 0).astype(F32)
        for u in range(8):
            left = jnp.where(high_names == high8[u : u + 1], amount[u : u + 1], 0.0).astype(BF)
            right = jnp.where(low_names == low8[u : u + 1], 1.0, 0.0).astype(BF)
            placed[i * 8 + u] = dot_nt(left, right)
        return carry

    lax.fori_loop(0, tokens // 8, place_band, 0)
    first, second = {}, {}

    def crossed(b, one, two):
        return tab(two, one) if b % 2 == 0 else tab(one, two)

    def part_on(b, e, d):
        at = crossed(b, -e, 0)
        src = gq.at[b, at] if e else qg.at[b]
        second[b, e, d] = send(src, gq.at[b, at], {"tab": crossed(b, 0, d)})

    for b in range(blocks):
        total = jnp.zeros((tokens, half), F32)
        for j in range(tiles):
            sums = placed[:, b * tiles + j, :].astype(BF)
            hsend[2 * b + j % 2, :, (j // 2) * 128 : (j // 2 + 1) * 128] = sums
            total = total + dot_nn(sums, key[j * 128 : (j + 1) * 128, b * half : (b + 1) * half])
        qg[b] = total.astype(BF)
        gq[b, me] = total.astype(BF)
        for d in (1, -1, 2):
            first[b, d] = send(qg.at[b], gq.at[b, me], {"tab": crossed(b, d, 0)})
        if b < 2:
            for d in (1, -1):
                part_on(b, 0, d)

    table_in = {}
    for d in NEAR + (0,):
        z = up(mz, d)
        wait(swaps[d])
        row = pl.multiple_of(mc * own_half + z * quarter, quarter)
        thalf[z] = (tpart[pl.ds(row, quarter), :].astype(F32) + tcore[z].astype(F32)).astype(BF)
        if d:
            table_in[d] = send(thalf.at[z], tz.at[mz], at_z(d))
        else:
            tz[mz] = thalf[mz]
    halves = []
    for d in range(1, 8):
        p = lax.rem(r + d, 8)
        halves.append(send(hsend.at[p], hrecv.at[r], {"rep": p}))
    hrecv[r] = hsend[r]

    def cross(pair):
        for e in (1, -1, 2):
            for b in pair:
                wait(first[b, e])
                for d in (1, -1):
                    part_on(b, e, d)

    def round_again(pair):
        for e, d in ((0, 1), (1, 1), (-1, -1), (2, -1)):
            for b in pair:
                wait(second[b, e, d])
                at = crossed(b, -e, -d)
                block = gq.at[b, at]
                second[b, e, 2 * d] = send(block, block, {"tab": crossed(b, 0, d)})

    def whole_pair(pair):
        for (b, e, d), copy in list(second.items()):
            if b in pair:
                wait(copy)

    cross((0, 1))
    for b in (2, 3):
        for d in (1, -1):
            part_on(b, 0, d)
    joined = jnp.concatenate([qg[b] for b in range(blocks)], axis=1)
    for at in range(0, width, 512):
        in_grad[:, at : at + 512] = dot_nt(joined, wt[at : at + 512, :]).astype(BF)
    round_again((0, 1))
    cross((2, 3))
    wait(*spreading)

    def turn(q, carry):
        near[:, pl.ds(pl.multiple_of(q * tokens, tokens), tokens)] = ginp[q].astype(F32).T.astype(BF)
        return carry

    lax.fori_loop(0, shards, turn, 0)

    share = piece_width // 8
    sums_in = {}

    def weigh(pair, n):
        whole_pair(pair)
        for i, b in enumerate(pair):
            part = dot_nn(near[...], gq[b].reshape(shards * tokens, half)).astype(BF)
            psend[n, :, :, i * half : (i + 1) * half] = part.reshape(8, share, half)
        sums_in[n] = []
        for d in range(1, 8):
            p = lax.rem(r + d, 8)
            sums_in[n].append(send(psend.at[n, p], precv.at[n, r], {"rep": p}))
        precv[n, r] = psend[n, r]

    weigh((0, 1), 0)
    round_again((2, 3))
    wait(*table_in.values())
    summed = tz[0].astype(F32)
    for z in range(1, 4):
        summed = summed + tz[z].astype(F32)

    def table_rows_of(z):
        return t_grad.at[pl.ds(pl.multiple_of(mc * own_half + z * quarter, quarter), quarter)]

    table_mine = table_rows_of(mz)
    table_mine[...] = summed.astype(BF)
    table_out = {d: send(table_mine, table_mine, at_z(d)) for d in (1, -1)}
    send(table_mine, table_mine, mate)

    wait(*lows, *halves)
    key_part = dot_tn(
        hrecv[...].reshape(8 * tokens, count // 2), lrecv[...].reshape(8 * tokens, half)
    )
    key_rows = count // shards
    ksend[...] = key_part.astype(BF).reshape(8, key_rows, half)
    key_base = copies.take(shards)
    key_out = []
    for i in range(2):
        for dx in range(side):
            x = lax.rem(mx + dx, side)
            copy = pltpu.make_async_remote_copy(
                src_ref=ksend.at[x * 2 + i],
                dst_ref=krecv.at[me],
                send_sem=ssem.at[key_base + i * side + dx],
                recv_sem=rsem.at[key_base + me],
                device_id={"tab": x * side + 2 * mc + i},
                device_id_type=MESH,
            )
            key_out.append((i, dx, copy))
            if dx:
                copy.start()
            else:

                @pl.when(my != 2 * mc + i)
                def _(copy=copy):
                    copy.start()

                @pl.when(my == 2 * mc + i)
                def _(x=x, i=i):
                    krecv[me] = ksend[x * 2 + i]

    before, after = table_rows_of(up(mz, -1)), table_rows_of(up(mz, 1))
    wait(table_out[1])
    lower = before.at[pl.ds(0, quarter // 2)]
    send(lower, lower, at_z(1))
    send(before, before, mate)
    wait(table_out[-1])
    upper = after.at[pl.ds(quarter // 2, quarter // 2)]
    send(upper, upper, at_z(-1))
    send(after, after, mate)
    table_far = [len(copies.copies) - 4, len(copies.copies) - 2]

    weigh((2, 3), 1)
    key_last = copies.take(8)
    keeper = my // 2

    def key_share(d):
        return pltpu.make_async_remote_copy(
            src_ref=kfin.at[mz],
            dst_ref=kfin.at[mz],
            send_sem=ssem.at[key_last + d],
            recv_sem=rsem.at[key_last + mz],
            device_id={"rep": lax.rem(r + d, 8)},
            device_id_type=MESH,
        )

    @pl.when(keeper == mc)
    def _():
        for d in range(1, shards):
            q = lax.rem(me + d, shards)
            pltpu.make_async_remote_copy(
                src_ref=ksend.at[0],
                dst_ref=krecv.at[q],
                send_sem=ssem.at[key_base],
                recv_sem=rsem.at[key_base + q],
                device_id={"tab": q},
                device_id_type=MESH,
            ).wait_recv()
        total = krecv[0].astype(F32)
        for q in range(1, shards):
            total = total + krecv[q].astype(F32)
        kfin[mz] = total.astype(BF)
        for d in range(1, 8):
            key_share(d).start()

    sums_out = {}
    for n in range(2):
        wait(*sums_in[n])
        total = precv[n, 0].astype(F32)
        for q in range(1, 8):
            total = total + precv[n, q].astype(F32)
        wfin[n, r] = total.astype(BF)
        mine = wfin.at[n, r]
        for d in NEAR:
            sums_out[n, d] = send(mine, mine, at_z(d))
        send(mine, mine, mate)
    wait(*table_far)
    across_z = table_rows_of(up(mz, 2))
    send(across_z, across_z, mate)
    for n in range(2):
        for d in NEAR:
            wait(sums_out[n, d])
            part = wfin.at[n, up(mz, -d) * 2 + mc]
            send(part, part, mate)

    for b in range(4):

        @pl.when((b != mz) | (keeper != mc))
        def _(b=b):
            pltpu.make_async_remote_copy(
                src_ref=kfin.at[b],
                dst_ref=kfin.at[b],
                send_sem=ssem.at[key_last],
                recv_sem=rsem.at[key_last + b],
                device_id=mate,
                device_id_type=MESH,
            ).wait_recv()

    for b in range(4):
        k_grad[:, b * half : (b + 1) * half] = kfin[b].astype(F32)
    wait(*range(len(copies.copies)))
    for n in range(2):
        done = wfin[n].reshape(piece_width, 2 * half).astype(F32)
        w_grad[:, n * 2 * half : (n + 1) * 2 * half] = done
    for i, dx, copy in key_out:
        if dx:
            copy.wait_send()
        else:

            @pl.when(my != 2 * mc + i)
            def _(copy=copy):
                copy.wait_send()

    @pl.when(keeper == mc)
    def _():
        for d in range(1, 8):
            key_share(d).wait_send()

    copies.finish()


def deliver_kernel(*refs):
    number = len(refs) // 2
    for i in range(number):
        refs[number + i][...] = refs[i][...]


def sds(shape, dtype):
    return jax.ShapeDtypeStruct(shape, dtype)


def on_device(inputs, grad_out, query_weight, sub_keys, values, owner, slot_rows, sub_index):
    tokens, width = inputs.shape
    cols = query_weight.shape[1]
    count = sub_keys.shape[0]
    heads, top = slot_rows.shape[1:]
    blocks = 2 * heads
    lanes = blocks * top
    half = cols // blocks
    shards = lax.axis_size("tab")
    side = 4
    rows = tokens * heads // shards
    slots = 2 * shards * rows
    table_rows = values.shape[0]
    own = jnp.transpose(owner, (1, 2, 0)).reshape(heads, tokens)
    rows_t = jnp.transpose(slot_rows, (1, 2, 0)).reshape(heads * top, tokens)
    picks_t = jnp.transpose(sub_index, (1, 2, 3, 0)).reshape(lanes, tokens)
    vmem = pl.BlockSpec(memory_space=pltpu.VMEM)
    anywhere = pl.BlockSpec(memory_space=pl.ANY)
    V = pltpu.VMEM
    shapes = (
        sds((tokens, width), BF),
        sds((width // shards, cols), F32),
        sds((count // shards, cols), F32),
        sds((table_rows, width), BF),
    )
    results = pl.pallas_call(
        whole_kernel,
        out_shape=shapes,
        in_specs=[vmem] * 4 + [anywhere] * 4,
        out_specs=(vmem,) * 4,
        scratch_shapes=[
            V((2, side, side, rows, width), BF),
            V((2, side, side, rows, width), BF),
            V((2, shards, rows, width), BF),
            V((tokens, width), BF),
            V((width, cols), BF),
            V((count, cols), BF),
            V((table_rows, width), BF),
            V((tokens, cols), F32),
            V((tokens, cols), BF),
            V((tokens, lanes), F32),
            V((3, tokens, lanes), F32),
            V((2, shards, rows, 2 * lanes), BF),
            V((2, shards, rows, 2 * lanes), BF),
            V((2, shards, rows, lanes), F32),
            V((2, shards, rows, lanes), F32),
            V((table_rows, slots), BF),
            V((table_rows, width), BF),
            V((4, table_rows // 8, width), BF),
            V((4, table_rows // 8, width), BF),
            V((4, table_rows // 8, width), BF),
            V((tokens, blocks * count // 128, 128), F32),
            V((8, tokens, count // 2), BF),
            V((8, tokens, count // 2), BF),
            V((8, tokens, half), BF),
            V((blocks, tokens, half), BF),
            V((blocks, shards, tokens, half), BF),
            V((shards, tokens, width // shards), BF),
            V((width // shards, shards * tokens), BF),
            V((8, count // shards, half), BF),
            V((shards, count // shards, half), BF),
            V((4, count // shards, half), BF),
            V((2, 8, width // shards // 8, 2 * half), BF),
            V((2, 8, width // shards // 8, 2 * half), BF),
            V((2, 8, width // shards // 8, 2 * half), BF),
            pltpu.SemaphoreType.DMA((7,)),
            pltpu.SemaphoreType.DMA((288,)),
            pltpu.SemaphoreType.DMA((288,)),
        ],
        compiler_params=pltpu.CompilerParams(
            collective_id=0, has_side_effects=True, vmem_limit_bytes=60 * 1024 * 1024
        ),
        name="whole",
    )(own, rows_t, picks_t, grad_out, inputs, query_weight, sub_keys, values)
    steps = 4
    specs = [pl.BlockSpec((x.shape[0] // steps, x.shape[1]), lambda i: (i, 0)) for x in shapes]
    return pl.pallas_call(
        deliver_kernel,
        out_shape=shapes,
        grid=(steps,),
        in_specs=specs,
        out_specs=tuple(specs),
        name="deliver",
    )(*results)


def solution(mesh):
    placed = (
        P(("rep", "tab"), None),
        P(("rep", "tab"), None),
        P(),
        P(),
        P("tab", None),
        P(("rep", "tab"), None, None),
        P(("rep", "tab"), None, None),
        P(("rep", "tab"), None, None, None),
    )
    return jax.shard_map(
        on_device,
        mesh=mesh,
        in_specs=placed,
        out_specs=(P(("rep", "tab"), None), P("tab", None), P("tab", None), P("tab", None)),
        check_vma=False,
    )
```

```python
import jax
import jax.numpy as jnp
from jax import lax
from jax.experimental import pallas as pl
from jax.experimental.pallas import tpu as pltpu
from jax.sharding import PartitionSpec as P

BF = jnp.bfloat16
F32 = jnp.float32
I32 = jnp.int32


def dot_nn(a, b):
    return lax.dot_general(a, b, (((1,), (0,)), ((), ())), preferred_element_type=F32)


def dot_nt(a, b):
    return lax.dot_general(a, b, (((1,), (1,)), ((), ())), preferred_element_type=F32)


def dot_tn(a, b):
    return lax.dot_general(a, b, (((0,), (0,)), ((), ())), preferred_element_type=F32)


def three(x):
    a = x.astype(BF)
    rest = x - a.astype(F32)
    b = rest.astype(BF)
    c = (rest - b.astype(F32)).astype(BF)
    return a, b, c


def iota(shape, dim):
    return lax.broadcasted_iota(I32, shape, dim)

MESH = pl.DeviceIdType.MESH
NEAR = (1, 3, 2)


class Copies:
    def __init__(self, send_sems, recv_sems):
        self.send_sems, self.recv_sems = send_sems, recv_sems
        self.copies, self.got = [], []
        self.used = 0

    def take(self, number):
        self.used += number
        assert self.used <= self.send_sems.shape[0]
        return self.used - number

    def send(self, src, dst, device):
        at = self.take(1)
        copy = pltpu.make_async_remote_copy(
            src_ref=src,
            dst_ref=dst,
            send_sem=self.send_sems.at[at],
            recv_sem=self.recv_sems.at[at],
            device_id=device,
            device_id_type=MESH,
        )
        copy.start()
        self.copies.append(copy)
        self.got.append(False)
        return len(self.copies) - 1

    def wait(self, *which):
        for i in which:
            if not self.got[i]:
                self.copies[i].wait_recv()
                self.got[i] = True

    def finish(self):
        self.wait(*range(len(self.copies)))
        for copy in self.copies:
            copy.wait_send()


def whole_kernel(
    own, rows_t, picks_t, grad, inputs, weight, keys, values,
    in_grad, w_grad, k_grad, t_grad,
    pay, mid, arr, inp, wt, key, val, acc, low, soft, score, wsend, wrecv, back, ret, spread,
    tpart, tcore, thalf, tz, placed, hsend, hrecv, lrecv, qg, gq, ginp, near, ksend, krecv, kfin,
    psend, precv, wfin, load_sem, ssem, rsem,
):
    heads, tokens = own.shape
    width = grad.shape[1]
    side, rows = pay.shape[1], pay.shape[3]
    shards = side * side
    lanes = picks_t.shape[0]
    blocks = 2 * heads
    top = lanes // blocks
    cols = acc.shape[1]
    half = cols // blocks
    count = key.shape[0]
    tiles = count // 128
    table_rows = val.shape[0]
    slots = 2 * shards * rows
    me, r = lax.axis_index("tab"), lax.axis_index("rep")
    mx, my = me // side, lax.rem(me, side)
    mz, mc = r // 2, lax.rem(r, 2)
    mate = {"rep": mz * 2 + 1 - mc}
    copies = Copies(ssem, rsem)
    send, wait = copies.send, copies.wait

    def up(at, by):
        return lax.rem(at + by + side, side)

    def tab(dx, dy):
        return up(mx, dx) * side + up(my, dy)

    def at_z(d):
        return {"rep": up(mz, d) * 2 + mc}

    loads = [pltpu.make_async_copy(inputs, inp, load_sem.at[0])]
    depth = width // 4
    for i in range(4):
        piece = pl.ds(i * depth, depth)
        loads.append(pltpu.make_async_copy(weight.at[piece], wt.at[piece], load_sem.at[1 + i]))
    loads.append(pltpu.make_async_copy(keys, key, load_sem.at[5]))
    loads.append(pltpu.make_async_copy(values, val, load_sem.at[6]))
    for load in loads:
        load.start()
    barrier = pltpu.get_barrier_semaphore()
    for d in range(1, shards):
        pl.semaphore_signal(
            barrier, inc=1, device_id={"tab": lax.rem(me + d, shards)}, device_id_type=MESH
        )
    for d in range(1, 8):
        pl.semaphore_signal(
            barrier, inc=1, device_id={"rep": lax.rem(r + d, 8)}, device_id_type=MESH
        )

    owned = jnp.concatenate([own[h : h + 1, :] for h in range(heads)], axis=1)
    messages = heads * tokens
    across = jnp.broadcast_to(owned, (messages, messages))
    same = across == across.T
    earlier = iota((messages, messages), 0) < iota((messages, messages), 1)
    rank = jnp.sum(jnp.where(same & earlier, 1.0, 0.0), axis=0, keepdims=True).astype(I32)
    place = (rank // rows) * (shards * rows) + owned * rows + rank % rows

    def hit_rows(part):
        at = iota((shards * rows, messages), 0) + part * shards * rows
        return jnp.where(at == place, 1.0, 0.0)

    phase_one = {}
    for part in range(2):
        hit = hit_rows(part)
        either = hit[:, :tokens]
        for h in range(1, heads):
            either = either + hit[:, h * tokens : (h + 1) * tokens]
        either = either.astype(BF)
        for at in range(0, width, 512):
            block = dot_nn(either, grad[:, at : at + 512]).astype(BF)
            pay[part, :, :, :, at : at + 512] = block.reshape(side, side, rows, 512)
        if part == 0:
            pl.semaphore_wait(barrier, shards + 6)
        for d in NEAR:
            for e in (0,) + NEAR:
                if part == 0:
                    src, device = pay.at[0, up(mx, e), up(my, d)], {"tab": tab(0, d)}
                    onward = mid.at[0, my, up(mx, e)]
                else:
                    src, device = pay.at[1, up(mx, d), up(my, e)], {"tab": tab(d, 0)}
                    onward = mid.at[1, mx, up(my, e)]
                dst = onward if e else arr.at[part, me]
                phase_one[part, d, e] = send(src, dst, device)
    phase_two = {}

    def pass_on(part, d, e):
        if part == 0:
            src = mid.at[0, up(my, -d), up(mx, e)] if d else pay.at[0, up(mx, e), my]
            dst, device = arr.at[0, tab(0, -d)], {"tab": tab(e, 0)}
        else:
            src = mid.at[1, up(mx, -d), up(my, e)] if d else pay.at[1, mx, up(my, e)]
            dst, device = arr.at[1, tab(-d, 0)], {"tab": tab(0, e)}
        phase_two[part, d, e] = send(src, dst, device)

    for part in range(2):
        for e in NEAR:
            pass_on(part, 0, e)
        arr[part, me] = pay[part, mx, my]

    loads[0].wait()
    for i in range(4):
        loads[1 + i].wait()
        piece = dot_nn(inp[:, i * depth : (i + 1) * depth], wt[i * depth : (i + 1) * depth, :])
        acc[...] = piece if i == 0 else acc[...] + piece
    low[...] = acc[...].astype(BF)
    lows = []
    for d in range(1, 8):
        p = lax.rem(r + d, 8)
        piece = pl.ds(pl.multiple_of((p // 2) * half, half), half)
        lows.append(send(low.at[:, piece], lrecv.at[r], {"rep": p}))
    lrecv[r] = low[:, pl.ds(pl.multiple_of(mz * half, half), half)]
    pick = picks_t[...].T
    low_pick = pick % 128
    high_pick = pick // 128
    lane_block = iota((tokens, lanes), 1) // top
    head_of = lane_block // 2
    chosen = jnp.zeros((tokens, lanes), F32)
    loads[5].wait()
    for b in range(blocks):
        parts = three(acc[:, b * half : (b + 1) * half])
        for j in range(tiles):
            names = key[j * 128 : (j + 1) * 128, b * half : (b + 1) * half]
            part = dot_nt(parts[2], names) + dot_nt(parts[1], names) + dot_nt(parts[0], names)
            got = jnp.take_along_axis(part, low_pick, axis=1)
            chosen = jnp.where((high_pick == j) & (lane_block == b), got, chosen)
    even = lane_block % 2 == 0
    other = jnp.where(
        even, pltpu.roll(chosen, lanes - top, axis=1), pltpu.roll(chosen, top, axis=1)
    )
    scores = chosen + other

    def over_heads(x, fill, reduce):
        out = jnp.zeros((tokens, lanes), F32)
        for h in range(heads):
            one = reduce(jnp.where(head_of == h, x, fill), axis=1, keepdims=True)
            out = jnp.where(head_of == h, one, out)
        return out

    raised = jnp.exp(scores - over_heads(scores, -jnp.inf, jnp.max))
    weights = raised / (over_heads(raised, 0.0, jnp.sum) * 0.5)
    soft[...] = weights
    low_soft = weights.astype(BF).astype(F32)

    def hits(h):
        column = jnp.broadcast_to(place[:, h * tokens : (h + 1) * tokens], (tokens, tokens)).T
        column = jnp.concatenate([column] * (slots // tokens), axis=1)
        return jnp.where(iota((tokens, slots), 1) == column, 1.0, 0.0).astype(BF)

    sent = jnp.zeros((slots, 2 * lanes), F32)
    for h in range(heads):
        one = rows_t[h * top : (h + 1) * top, :].astype(F32)
        numbers = jnp.concatenate([one] * blocks, axis=0).T
        turned = low_soft if h == 0 else pltpu.roll(low_soft, lanes - h * 2 * top, axis=1)
        sent = sent + dot_tn(hits(h), jnp.concatenate([numbers, turned], axis=1).astype(BF))
    wsend[...] = sent.astype(BF).reshape(2, shards, rows, 2 * lanes)

    def pass_all(d):
        for e in (0,) + NEAR:
            for part in range(2):
                wait(phase_one[part, d, e])
                if e:
                    pass_on(part, d, e)

    pass_all(1)
    weighing = []
    for dx in range(side):
        for dy in range(side):
            if dx or dy:
                p = tab(dx, dy)
                weighing.append(send(wsend.at[:, p], wrecv.at[:, me], {"tab": p}))
    wrecv[:, me] = wsend[:, me]
    pass_all(3)
    pass_all(2)

    wait(*weighing)
    band = 128
    per_band = band // rows

    def spread_band(g, carry):
        part, at = g // (shards // per_band), lax.rem(g, shards // per_band) * per_band
        block = wrecv[part, pl.ds(at, per_band)].reshape(band, 2 * lanes).astype(F32)
        row_t, soft_t = block[:, :lanes].T, block[:, lanes:].T
        names = iota((table_rows, band), 0).astype(F32)
        held = jnp.zeros((table_rows, band), F32)
        for k in range(top):
            held = held + jnp.where(names == row_t[k : k + 1], soft_t[k : k + 1], 0.0)
        spread[:, pl.ds(pl.multiple_of(g * band, band), band)] = held.astype(BF)
        return carry

    lax.fori_loop(0, slots // band, spread_band, 0)

    loads[6].wait()
    for d in (0,) + NEAR:
        for e in NEAR:
            for part in range(2):
                wait(phase_two[part, d, e])
    for part in range(2):
        for q in range(0, shards, per_band):
            here = slice(q, q + per_band)
            product = dot_nt(arr[part, here].reshape(band, width), val[...])
            name = wrecv[part, here, :, :lanes].reshape(band, lanes).astype(I32)
            out = jnp.zeros((band, lanes), F32)
            for j in range(table_rows // 128):
                got = jnp.take_along_axis(product[:, j * 128 : (j + 1) * 128], name % 128, axis=1)
                out = jnp.where(name // 128 == j, got, out)
            back[part, here] = out.reshape(per_band, rows, lanes)
    returning = []
    for dx in range(side):
        for dy in range(side):
            if dx or dy:
                p = tab(dx, dy)
                returning.append(send(back.at[:, p], ret.at[:, me], {"tab": p}))
    ret[:, me] = back[:, me]
    spreading = []
    piece_width = width // shards
    for dx in (0,) + NEAR:
        for dy in (0,) + NEAR:
            if dx or dy:
                p = tab(dx, dy)
                piece = pl.ds(pl.multiple_of(p * piece_width, piece_width), piece_width)
                spreading.append(send(inp.at[:, piece], ginp.at[me], {"tab": p}))
    ginp[me] = inp[:, pl.ds(pl.multiple_of(me * piece_width, piece_width), piece_width)]

    own_half = table_rows // 2
    quarter = own_half // 4
    for at in range(0, width, 512):
        column = arr[:, :, :, at : at + 512].reshape(slots, 512)
        tpart[:, at : at + 512] = dot_nn(spread[...], column).astype(BF)
    swaps = {}
    for d in NEAR + (0,):
        z = up(mz, d)
        row = pl.multiple_of((1 - mc) * own_half + z * quarter, quarter)
        swaps[d] = send(tpart.at[pl.ds(row, quarter)], tcore.at[z], mate)

    wait(*returning)
    parts = three(ret[...].reshape(slots, lanes))
    slot_grad = jnp.zeros((tokens, lanes), F32)
    for h in range(heads):
        hit = hits(h)
        got = dot_nn(hit, parts[2]) + dot_nn(hit, parts[1]) + dot_nn(hit, parts[0])
        slot_grad = jnp.where(head_of == h, got, slot_grad)
    weights = soft[...]
    mean = over_heads(weights * slot_grad, 0.0, jnp.sum) * 0.5
    score_grad = weights * (slot_grad - mean)
    pairs = tokens // 2
    early_lanes = iota((pairs, lanes), 1) < lanes // 2

    def place_head(h):
        def pack(x):
            turned = pltpu.roll(x, lanes // 2, axis=1)
            one, two = (x, turned) if h == 0 else (turned, x)
            return jnp.where(early_lanes, one[:pairs], two[pairs:])

        score[0] = pack(score_grad)
        score[1] = pack(low_pick.astype(F32))
        score[2] = pack(high_pick.astype(F32)) + (tiles * lane_block[:pairs]).astype(F32)

        def place_band(i, carry):
            here = pl.ds(pl.multiple_of(i * 8, 8), 8)
            amount, low8, high8 = score[0, here, :], score[1, here, :], score[2, here, :]
            high_names = iota((blocks * tiles, lanes), 0).astype(F32)
            low_names = iota((128, lanes), 0).astype(F32)
            for u in range(8):
                left = jnp.where(high_names == high8[u : u + 1], amount[u : u + 1], 0.0).astype(BF)
                right = jnp.where(low_names == low8[u : u + 1], 1.0, 0.0).astype(BF)
                sums = dot_nt(left, right)
                placed[i * 8 + u] = sums[: 2 * tiles]
                placed[i * 8 + u + pairs] = sums[2 * tiles :]
            return carry

        lax.fori_loop(0, pairs // 8, place_band, 0)

    first, second = {}, {}

    def crossed(b, one, two):
        return tab(two, one) if b % 2 == 0 else tab(one, two)

    def part_on(b, e, d):
        at = crossed(b, -e, 0)
        src = gq.at[b, at] if e else qg.at[b]
        second[b, e, d] = send(src, gq.at[b, at], {"tab": crossed(b, 0, d)})

    table_in = {}
    for b in range(blocks):
        if b % 2 == 0:
            place_head(b // 2)
        total = jnp.zeros((tokens, half), F32)
        for j in range(tiles):
            sums = placed[:, b % 2 * tiles + j, :].astype(BF)
            hsend[2 * b + j % 2, :, (j // 2) * 128 : (j // 2 + 1) * 128] = sums
            total = total + dot_nn(sums, key[j * 128 : (j + 1) * 128, b * half : (b + 1) * half])
        qg[b] = total.astype(BF)
        gq[b, me] = total.astype(BF)
        for d in (1, -1, 2):
            first[b, d] = send(qg.at[b], gq.at[b, me], {"tab": crossed(b, d, 0)})
        if b < 2:
            for d in (1, -1):
                part_on(b, 0, d)
        if b != 1:
            continue
        for d in NEAR + (0,):
            z = up(mz, d)
            wait(swaps[d])
            row = pl.multiple_of(mc * own_half + z * quarter, quarter)
            joint = tpart[pl.ds(row, quarter), :].astype(F32) + tcore[z].astype(F32)
            thalf[z] = joint.astype(BF)
            if d:
                table_in[d] = send(thalf.at[z], tz.at[mz], at_z(d))
            else:
                tz[mz] = thalf[mz]

    halves = []
    for d in range(1, 8):
        p = lax.rem(r + d, 8)
        halves.append(send(hsend.at[p], hrecv.at[r], {"rep": p}))
    hrecv[r] = hsend[r]

    def cross(pair):
        for e in (1, -1, 2):
            for b in pair:
                wait(first[b, e])
                for d in (1, -1):
                    part_on(b, e, d)

    def round_again(pair):
        for e, d in ((0, 1), (1, 1), (-1, -1), (2, -1)):
            for b in pair:
                wait(second[b, e, d])
                at = crossed(b, -e, -d)
                block = gq.at[b, at]
                second[b, e, 2 * d] = send(block, block, {"tab": crossed(b, 0, d)})

    def whole_pair(pair):
        for (b, e, d), copy in list(second.items()):
            if b in pair:
                wait(copy)

    cross((0, 1))
    for b in (2, 3):
        for d in (1, -1):
            part_on(b, 0, d)
    joined = jnp.concatenate([qg[b] for b in range(blocks)], axis=1)
    for at in range(0, width, 512):
        in_grad[:, at : at + 512] = dot_nt(joined, wt[at : at + 512, :]).astype(BF)
    round_again((0, 1))
    cross((2, 3))
    wait(*table_in.values())
    summed = tz[0].astype(F32)
    for z in range(1, 4):
        summed = summed + tz[z].astype(F32)

    def table_rows_of(z):
        return t_grad.at[pl.ds(pl.multiple_of(mc * own_half + z * quarter, quarter), quarter)]

    table_mine = table_rows_of(mz)
    table_mine[...] = summed.astype(BF)
    table_out = {d: send(table_mine, table_mine, at_z(d)) for d in (1, -1)}
    send(table_mine, table_mine, mate)
    wait(*spreading)

    def turn(q, carry):
        near[:, pl.ds(pl.multiple_of(q * tokens, tokens), tokens)] = ginp[q].astype(F32).T.astype(BF)
        return carry

    lax.fori_loop(0, shards, turn, 0)

    share = piece_width // 8
    sums_in = {}

    def weigh(pair, n):
        whole_pair(pair)
        for i, b in enumerate(pair):
            part = dot_nn(near[...], gq[b].reshape(shards * tokens, half)).astype(BF)
            psend[n, :, :, i * half : (i + 1) * half] = part.reshape(8, share, half)
        sums_in[n] = []
        for d in range(1, 8):
            p = lax.rem(r + d, 8)
            sums_in[n].append(send(psend.at[n, p], precv.at[n, r], {"rep": p}))
        precv[n, r] = psend[n, r]

    weigh((0, 1), 0)
    round_again((2, 3))

    wait(*lows, *halves)
    key_part = dot_tn(
        hrecv[...].reshape(8 * tokens, count // 2), lrecv[...].reshape(8 * tokens, half)
    )
    key_rows = count // shards
    ksend[...] = key_part.astype(BF).reshape(8, key_rows, half)
    key_base = copies.take(shards)
    key_out = []
    for i in range(2):
        for dx in range(side):
            x = lax.rem(mx + dx, side)
            copy = pltpu.make_async_remote_copy(
                src_ref=ksend.at[x * 2 + i],
                dst_ref=krecv.at[me],
                send_sem=ssem.at[key_base + i * side + dx],
                recv_sem=rsem.at[key_base + me],
                device_id={"tab": x * side + 2 * mc + i},
                device_id_type=MESH,
            )
            key_out.append((i, dx, copy))
            if dx:
                copy.start()
            else:

                @pl.when(my != 2 * mc + i)
                def _(copy=copy):
                    copy.start()

                @pl.when(my == 2 * mc + i)
                def _(x=x, i=i):
                    krecv[me] = ksend[x * 2 + i]

    before, after = table_rows_of(up(mz, -1)), table_rows_of(up(mz, 1))
    wait(table_out[1])
    lower = before.at[pl.ds(0, quarter // 2)]
    send(lower, lower, at_z(1))
    send(before, before, mate)
    wait(table_out[-1])
    upper = after.at[pl.ds(quarter // 2, quarter // 2)]
    send(upper, upper, at_z(-1))
    send(after, after, mate)
    table_far = [len(copies.copies) - 4, len(copies.copies) - 2]

    weigh((2, 3), 1)
    key_last = copies.take(8)
    keeper = my // 2

    def key_share(d):
        return pltpu.make_async_remote_copy(
            src_ref=kfin.at[mz],
            dst_ref=kfin.at[mz],
            send_sem=ssem.at[key_last + d],
            recv_sem=rsem.at[key_last + mz],
            device_id={"rep": lax.rem(r + d, 8)},
            device_id_type=MESH,
        )

    @pl.when(keeper == mc)
    def _():
        for d in range(1, shards):
            q = lax.rem(me + d, shards)
            pltpu.make_async_remote_copy(
                src_ref=ksend.at[0],
                dst_ref=krecv.at[q],
                send_sem=ssem.at[key_base],
                recv_sem=rsem.at[key_base + q],
                device_id={"tab": q},
                device_id_type=MESH,
            ).wait_recv()
        total = krecv[0].astype(F32)
        for q in range(1, shards):
            total = total + krecv[q].astype(F32)
        kfin[mz] = total.astype(BF)
        for d in range(1, 8):
            key_share(d).start()

    for n in range(2):
        wait(*sums_in[n])
        total = precv[n, 0].astype(F32)
        for q in range(1, 8):
            total = total + precv[n, q].astype(F32)
        wfin[n, r] = total.astype(BF)
        mine = wfin.at[n, r]
        for d in range(1, 8):
            send(mine, mine, {"rep": lax.rem(r + d, 8)})
    wait(*table_far)
    across_z = table_rows_of(up(mz, 2))
    send(across_z, across_z, mate)

    for b in range(4):

        @pl.when((b != mz) | (keeper != mc))
        def _(b=b):
            pltpu.make_async_remote_copy(
                src_ref=kfin.at[b],
                dst_ref=kfin.at[b],
                send_sem=ssem.at[key_last],
                recv_sem=rsem.at[key_last + b],
                device_id=mate,
                device_id_type=MESH,
            ).wait_recv()

    for b in range(4):
        k_grad[:, b * half : (b + 1) * half] = kfin[b].astype(F32)
    wait(*range(len(copies.copies)))
    for n in range(2):
        done = wfin[n].reshape(piece_width, 2 * half).astype(F32)
        w_grad[:, n * 2 * half : (n + 1) * 2 * half] = done
    for i, dx, copy in key_out:
        if dx:
            copy.wait_send()
        else:

            @pl.when(my != 2 * mc + i)
            def _(copy=copy):
                copy.wait_send()

    @pl.when(keeper == mc)
    def _():
        for d in range(1, 8):
            key_share(d).wait_send()

    copies.finish()


def deliver_kernel(*refs):
    number = len(refs) // 2
    for i in range(number):
        refs[number + i][...] = refs[i][...]


def sds(shape, dtype):
    return jax.ShapeDtypeStruct(shape, dtype)


def on_device(inputs, grad_out, query_weight, sub_keys, values, owner, slot_rows, sub_index):
    tokens, width = inputs.shape
    cols = query_weight.shape[1]
    count = sub_keys.shape[0]
    heads, top = slot_rows.shape[1:]
    blocks = 2 * heads
    lanes = blocks * top
    half = cols // blocks
    shards = lax.axis_size("tab")
    side = 4
    rows = tokens * heads // shards
    slots = 2 * shards * rows
    table_rows = values.shape[0]
    own = jnp.transpose(owner, (1, 2, 0)).reshape(heads, tokens)
    rows_t = jnp.transpose(slot_rows, (1, 2, 0)).reshape(heads * top, tokens)
    picks_t = jnp.transpose(sub_index, (1, 2, 3, 0)).reshape(lanes, tokens)
    vmem = pl.BlockSpec(memory_space=pltpu.VMEM)
    anywhere = pl.BlockSpec(memory_space=pl.ANY)
    V = pltpu.VMEM
    shapes = (
        sds((tokens, width), BF),
        sds((width // shards, cols), F32),
        sds((count // shards, cols), F32),
        sds((table_rows, width), BF),
    )
    results = pl.pallas_call(
        whole_kernel,
        out_shape=shapes,
        in_specs=[vmem] * 4 + [anywhere] * 4,
        out_specs=(vmem,) * 4,
        scratch_shapes=[
            V((2, side, side, rows, width), BF),
            V((2, side, side, rows, width), BF),
            V((2, shards, rows, width), BF),
            V((tokens, width), BF),
            V((width, cols), BF),
            V((count, cols), BF),
            V((table_rows, width), BF),
            V((tokens, cols), F32),
            V((tokens, cols), BF),
            V((tokens, lanes), F32),
            V((3, tokens // 2, lanes), F32),
            V((2, shards, rows, 2 * lanes), BF),
            V((2, shards, rows, 2 * lanes), BF),
            V((2, shards, rows, lanes), F32),
            V((2, shards, rows, lanes), F32),
            V((table_rows, slots), BF),
            V((table_rows, width), BF),
            V((4, table_rows // 8, width), BF),
            V((4, table_rows // 8, width), BF),
            V((4, table_rows // 8, width), BF),
            V((tokens, 2 * count // 128, 128), F32),
            V((8, tokens, count // 2), BF),
            V((8, tokens, count // 2), BF),
            V((8, tokens, half), BF),
            V((blocks, tokens, half), BF),
            V((blocks, shards, tokens, half), BF),
            V((shards, tokens, width // shards), BF),
            V((width // shards, shards * tokens), BF),
            V((8, count // shards, half), BF),
            V((shards, count // shards, half), BF),
            V((4, count // shards, half), BF),
            V((2, 8, width // shards // 8, 2 * half), BF),
            V((2, 8, width // shards // 8, 2 * half), BF),
            V((2, 8, width // shards // 8, 2 * half), BF),
            pltpu.SemaphoreType.DMA((7,)),
            pltpu.SemaphoreType.DMA((288,)),
            pltpu.SemaphoreType.DMA((288,)),
        ],
        compiler_params=pltpu.CompilerParams(
            collective_id=0, has_side_effects=True, vmem_limit_bytes=60 * 1024 * 1024
        ),
        name="whole",
    )(own, rows_t, picks_t, grad_out, inputs, query_weight, sub_keys, values)
    steps = 4
    specs = [pl.BlockSpec((x.shape[0] // steps, x.shape[1]), lambda i: (i, 0)) for x in shapes]
    return pl.pallas_call(
        deliver_kernel,
        out_shape=shapes,
        grid=(steps,),
        in_specs=specs,
        out_specs=tuple(specs),
        name="deliver",
    )(*results)


def solution(mesh):
    placed = (
        P(("rep", "tab"), None),
        P(("rep", "tab"), None),
        P(),
        P(),
        P("tab", None),
        P(("rep", "tab"), None, None),
        P(("rep", "tab"), None, None),
        P(("rep", "tab"), None, None, None),
    )
    return jax.shard_map(
        on_device,
        mesh=mesh,
        in_specs=placed,
        out_specs=(P(("rep", "tab"), None), P("tab", None), P("tab", None), P("tab", None)),
        check_vma=False,
    )
```

```python
import jax
import jax.numpy as jnp
from jax import lax
from jax.experimental import pallas as pl
from jax.experimental.pallas import tpu as pltpu
from jax.sharding import PartitionSpec as P

BF = jnp.bfloat16
F32 = jnp.float32
I32 = jnp.int32


def dot_nn(a, b):
    return lax.dot_general(a, b, (((1,), (0,)), ((), ())), preferred_element_type=F32)


def dot_nt(a, b):
    return lax.dot_general(a, b, (((1,), (1,)), ((), ())), preferred_element_type=F32)


def dot_tn(a, b):
    return lax.dot_general(a, b, (((0,), (0,)), ((), ())), preferred_element_type=F32)


def three(x):
    a = x.astype(BF)
    rest = x - a.astype(F32)
    b = rest.astype(BF)
    c = (rest - b.astype(F32)).astype(BF)
    return a, b, c


def iota(shape, dim):
    return lax.broadcasted_iota(I32, shape, dim)

MESH = pl.DeviceIdType.MESH
NEAR = (1, 3, 2)


class Copies:
    def __init__(self, send_sems, recv_sems):
        self.send_sems, self.recv_sems = send_sems, recv_sems
        self.copies, self.got = [], []
        self.used = 0

    def take(self, number):
        self.used += number
        assert self.used <= self.send_sems.shape[0]
        return self.used - number

    def send(self, src, dst, device):
        at = self.take(1)
        copy = pltpu.make_async_remote_copy(
            src_ref=src,
            dst_ref=dst,
            send_sem=self.send_sems.at[at],
            recv_sem=self.recv_sems.at[at],
            device_id=device,
            device_id_type=MESH,
        )
        copy.start()
        self.copies.append(copy)
        self.got.append(False)
        return len(self.copies) - 1

    def wait(self, *which):
        for i in which:
            if not self.got[i]:
                self.copies[i].wait_recv()
                self.got[i] = True

    def finish(self):
        self.wait(*range(len(self.copies)))
        for copy in self.copies:
            copy.wait_send()


def whole_kernel(
    own, rows_t, picks_t, grad, inputs, weight, keys, values,
    in_grad, w_grad, k_grad, t_grad,
    pay, mid, arr, inp, wt, key, val, acc, low, soft, score, wsend, wrecv, back, ret, spread,
    tpart, tcore, thalf, tz, placed, hsend, hrecv, lrecv, qg, gq, ginp, near, ksend, krecv, kfin,
    psend, precv, wfin, load_sem, ssem, rsem,
):
    heads, tokens = own.shape
    width = grad.shape[1]
    side, rows = pay.shape[1], pay.shape[3]
    shards = side * side
    lanes = picks_t.shape[0]
    blocks = 2 * heads
    top = lanes // blocks
    cols = acc.shape[1]
    half = cols // blocks
    count = key.shape[0]
    tiles = count // 128
    table_rows = val.shape[0]
    slots = 2 * shards * rows
    me, r = lax.axis_index("tab"), lax.axis_index("rep")
    mx, my = me // side, lax.rem(me, side)
    mz, mc = r // 2, lax.rem(r, 2)
    mate = {"rep": mz * 2 + 1 - mc}
    copies = Copies(ssem, rsem)
    send, wait = copies.send, copies.wait

    def up(at, by):
        return lax.rem(at + by + side, side)

    def tab(dx, dy):
        return up(mx, dx) * side + up(my, dy)

    def at_z(d):
        return {"rep": up(mz, d) * 2 + mc}

    loads = [pltpu.make_async_copy(inputs, inp, load_sem.at[0])]
    depth = width // 4
    for i in range(4):
        piece = pl.ds(i * depth, depth)
        loads.append(pltpu.make_async_copy(weight.at[piece], wt.at[piece], load_sem.at[1 + i]))
    loads.append(pltpu.make_async_copy(keys, key, load_sem.at[5]))
    loads.append(pltpu.make_async_copy(values, val, load_sem.at[6]))
    for load in loads:
        load.start()
    barrier = pltpu.get_barrier_semaphore()
    for d in range(1, shards):
        pl.semaphore_signal(
            barrier, inc=1, device_id={"tab": lax.rem(me + d, shards)}, device_id_type=MESH
        )
    for d in range(1, 8):
        pl.semaphore_signal(
            barrier, inc=1, device_id={"rep": lax.rem(r + d, 8)}, device_id_type=MESH
        )

    owned = jnp.concatenate([own[h : h + 1, :] for h in range(heads)], axis=1)
    messages = heads * tokens
    across = jnp.broadcast_to(owned, (messages, messages))
    same = across == across.T
    earlier = iota((messages, messages), 0) < iota((messages, messages), 1)
    rank = jnp.sum(jnp.where(same & earlier, 1.0, 0.0), axis=0, keepdims=True).astype(I32)
    place = (rank // rows) * (shards * rows) + owned * rows + rank % rows

    def hit_rows(part):
        at = iota((shards * rows, messages), 0) + part * shards * rows
        return jnp.where(at == place, 1.0, 0.0)

    phase_one = {}
    for part in range(2):
        hit = hit_rows(part)
        either = hit[:, :tokens]
        for h in range(1, heads):
            either = either + hit[:, h * tokens : (h + 1) * tokens]
        either = either.astype(BF)
        for at in range(0, width, 512):
            block = dot_nn(either, grad[:, at : at + 512]).astype(BF)
            pay[part, :, :, :, at : at + 512] = block.reshape(side, side, rows, 512)
        if part == 0:
            pl.semaphore_wait(barrier, shards + 6)
        for d in NEAR:
            for e in (0,) + NEAR:
                if part == 0:
                    src, device = pay.at[0, up(mx, e), up(my, d)], {"tab": tab(0, d)}
                    onward = mid.at[0, my, up(mx, e)]
                else:
                    src, device = pay.at[1, up(mx, d), up(my, e)], {"tab": tab(d, 0)}
                    onward = mid.at[1, mx, up(my, e)]
                dst = onward if e else arr.at[part, me]
                phase_one[part, d, e] = send(src, dst, device)
    phase_two = {}

    def pass_on(part, d, e):
        if part == 0:
            src = mid.at[0, up(my, -d), up(mx, e)] if d else pay.at[0, up(mx, e), my]
            dst, device = arr.at[0, tab(0, -d)], {"tab": tab(e, 0)}
        else:
            src = mid.at[1, up(mx, -d), up(my, e)] if d else pay.at[1, mx, up(my, e)]
            dst, device = arr.at[1, tab(-d, 0)], {"tab": tab(0, e)}
        phase_two[part, d, e] = send(src, dst, device)

    for part in range(2):
        for e in NEAR:
            pass_on(part, 0, e)
        arr[part, me] = pay[part, mx, my]

    loads[0].wait()
    for i in range(4):
        loads[1 + i].wait()
        piece = dot_nn(inp[:, i * depth : (i + 1) * depth], wt[i * depth : (i + 1) * depth, :])
        acc[...] = piece if i == 0 else acc[...] + piece
    low[...] = acc[...].astype(BF)
    lows = []
    for d in range(1, 8):
        p = lax.rem(r + d, 8)
        piece = pl.ds(pl.multiple_of((p // 2) * half, half), half)
        lows.append(send(low.at[:, piece], lrecv.at[r], {"rep": p}))
    lrecv[r] = low[:, pl.ds(pl.multiple_of(mz * half, half), half)]
    pick = picks_t[...].T
    low_pick = pick % 128
    high_pick = pick // 128
    lane_block = iota((tokens, lanes), 1) // top
    head_of = lane_block // 2
    chosen = jnp.zeros((tokens, lanes), F32)
    loads[5].wait()
    for b in range(blocks):
        parts = three(acc[:, b * half : (b + 1) * half])
        for j in range(tiles):
            names = key[j * 128 : (j + 1) * 128, b * half : (b + 1) * half]
            part = dot_nt(parts[2], names) + dot_nt(parts[1], names) + dot_nt(parts[0], names)
            got = jnp.take_along_axis(part, low_pick, axis=1)
            chosen = jnp.where((high_pick == j) & (lane_block == b), got, chosen)
    even = lane_block % 2 == 0
    other = jnp.where(
        even, pltpu.roll(chosen, lanes - top, axis=1), pltpu.roll(chosen, top, axis=1)
    )
    scores = chosen + other

    def over_heads(x, fill, reduce):
        out = jnp.zeros((tokens, lanes), F32)
        for h in range(heads):
            one = reduce(jnp.where(head_of == h, x, fill), axis=1, keepdims=True)
            out = jnp.where(head_of == h, one, out)
        return out

    raised = jnp.exp(scores - over_heads(scores, -jnp.inf, jnp.max))
    weights = raised / (over_heads(raised, 0.0, jnp.sum) * 0.5)
    soft[...] = weights
    low_soft = weights.astype(BF).astype(F32)

    def hits(h):
        column = jnp.broadcast_to(place[:, h * tokens : (h + 1) * tokens], (tokens, tokens)).T
        column = jnp.concatenate([column] * (slots // tokens), axis=1)
        return jnp.where(iota((tokens, slots), 1) == column, 1.0, 0.0).astype(BF)

    sent = jnp.zeros((slots, 2 * lanes), F32)
    for h in range(heads):
        one = rows_t[h * top : (h + 1) * top, :].astype(F32)
        numbers = jnp.concatenate([one] * blocks, axis=0).T
        turned = low_soft if h == 0 else pltpu.roll(low_soft, lanes - h * 2 * top, axis=1)
        sent = sent + dot_tn(hits(h), jnp.concatenate([numbers, turned], axis=1).astype(BF))
    wsend[...] = sent.astype(BF).reshape(2, shards, rows, 2 * lanes)

    def pass_all(d):
        for e in (0,) + NEAR:
            for part in range(2):
                wait(phase_one[part, d, e])
                if e:
                    pass_on(part, d, e)

    pass_all(1)
    weighing = []
    for dx in range(side):
        for dy in range(side):
            if dx or dy:
                p = tab(dx, dy)
                weighing.append(send(wsend.at[:, p], wrecv.at[:, me], {"tab": p}))
    wrecv[:, me] = wsend[:, me]
    pass_all(3)
    pass_all(2)

    wait(*weighing)
    band = 128
    per_band = band // rows

    def spread_band(g, carry):
        part, at = g // (shards // per_band), lax.rem(g, shards // per_band) * per_band
        block = wrecv[part, pl.ds(at, per_band)].reshape(band, 2 * lanes).astype(F32)
        row_t, soft_t = block[:, :lanes].T, block[:, lanes:].T
        names = iota((table_rows, band), 0).astype(F32)
        held = jnp.zeros((table_rows, band), F32)
        for k in range(top):
            held = held + jnp.where(names == row_t[k : k + 1], soft_t[k : k + 1], 0.0)
        spread[:, pl.ds(pl.multiple_of(g * band, band), band)] = held.astype(BF)
        return carry

    lax.fori_loop(0, slots // band, spread_band, 0)

    loads[6].wait()
    for d in (0,) + NEAR:
        for e in NEAR:
            for part in range(2):
                wait(phase_two[part, d, e])
    for part in range(2):
        for q in range(0, shards, per_band):
            here = slice(q, q + per_band)
            product = dot_nt(arr[part, here].reshape(band, width), val[...])
            name = wrecv[part, here, :, :lanes].reshape(band, lanes).astype(I32)
            out = jnp.zeros((band, lanes), F32)
            for j in range(table_rows // 128):
                got = jnp.take_along_axis(product[:, j * 128 : (j + 1) * 128], name % 128, axis=1)
                out = jnp.where(name // 128 == j, got, out)
            back[part, here] = out.reshape(per_band, rows, lanes)
    returning = []
    for dx in range(side):
        for dy in range(side):
            if dx or dy:
                p = tab(dx, dy)
                returning.append(send(back.at[:, p], ret.at[:, me], {"tab": p}))
    ret[:, me] = back[:, me]
    spreading = []
    piece_width = width // shards
    for dx in (0,) + NEAR:
        for dy in (0,) + NEAR:
            if dx or dy:
                p = tab(dx, dy)
                piece = pl.ds(pl.multiple_of(p * piece_width, piece_width), piece_width)
                spreading.append(send(inp.at[:, piece], ginp.at[me], {"tab": p}))
    ginp[me] = inp[:, pl.ds(pl.multiple_of(me * piece_width, piece_width), piece_width)]

    own_half = table_rows // 2
    quarter = own_half // 4
    for at in range(0, width, 512):
        column = arr[:, :, :, at : at + 512].reshape(slots, 512)
        tpart[:, at : at + 512] = dot_nn(spread[...], column).astype(BF)
    swaps = {}
    for d in NEAR + (0,):
        z = up(mz, d)
        row = pl.multiple_of((1 - mc) * own_half + z * quarter, quarter)
        swaps[d] = send(tpart.at[pl.ds(row, quarter)], tcore.at[z], mate)

    wait(*returning)
    parts = three(ret[...].reshape(slots, lanes))
    slot_grad = jnp.zeros((tokens, lanes), F32)
    for h in range(heads):
        hit = hits(h)
        got = dot_nn(hit, parts[2]) + dot_nn(hit, parts[1]) + dot_nn(hit, parts[0])
        slot_grad = jnp.where(head_of == h, got, slot_grad)
    weights = soft[...]
    mean = over_heads(weights * slot_grad, 0.0, jnp.sum) * 0.5
    score_grad = weights * (slot_grad - mean)
    pairs = tokens // 2
    early_lanes = iota((pairs, lanes), 1) < lanes // 2

    def place_head(h):
        def pack(x):
            turned = pltpu.roll(x, lanes // 2, axis=1)
            one, two = (x, turned) if h == 0 else (turned, x)
            return jnp.where(early_lanes, one[:pairs], two[pairs:])

        score[0] = pack(score_grad)
        score[1] = pack(low_pick.astype(F32))
        score[2] = pack(high_pick.astype(F32)) + (tiles * lane_block[:pairs]).astype(F32)

        def place_band(i, carry):
            here = pl.ds(pl.multiple_of(i * 8, 8), 8)
            amount, low8, high8 = score[0, here, :], score[1, here, :], score[2, here, :]
            high_names = iota((blocks * tiles, lanes), 0).astype(F32)
            low_names = iota((128, lanes), 0).astype(F32)
            for u in range(8):
                left = jnp.where(high_names == high8[u : u + 1], amount[u : u + 1], 0.0).astype(BF)
                right = jnp.where(low_names == low8[u : u + 1], 1.0, 0.0).astype(BF)
                sums = dot_nt(left, right)
                placed[i * 8 + u] = sums[: 2 * tiles]
                placed[i * 8 + u + pairs] = sums[2 * tiles :]
            return carry

        lax.fori_loop(0, pairs // 8, place_band, 0)

    first, second = {}, {}

    def crossed(b, one, two):
        return tab(two, one) if b % 2 == 0 else tab(one, two)

    def part_on(b, e, d):
        at = crossed(b, -e, 0)
        src = gq.at[b, at] if e else qg.at[b]
        second[b, e, d] = send(src, gq.at[b, at], {"tab": crossed(b, 0, d)})

    table_in = {}
    for b in range(blocks):
        if b % 2 == 0:
            place_head(b // 2)
        total = jnp.zeros((tokens, half), F32)
        for j in range(tiles):
            sums = placed[:, b % 2 * tiles + j, :].astype(BF)
            hsend[2 * b + j % 2, :, (j // 2) * 128 : (j // 2 + 1) * 128] = sums
            total = total + dot_nn(sums, key[j * 128 : (j + 1) * 128, b * half : (b + 1) * half])
        qg[b] = total.astype(BF)
        gq[b, me] = total.astype(BF)
        for d in (1, -1, 2):
            first[b, d] = send(qg.at[b], gq.at[b, me], {"tab": crossed(b, d, 0)})
        if b < 2:
            for d in (1, -1):
                part_on(b, 0, d)
        if b != 1:
            continue
        for d in NEAR + (0,):
            z = up(mz, d)
            wait(swaps[d])
            row = pl.multiple_of(mc * own_half + z * quarter, quarter)
            joint = tpart[pl.ds(row, quarter), :].astype(F32) + tcore[z].astype(F32)
            thalf[z] = joint.astype(BF)
            if d:
                table_in[d] = send(thalf.at[z], tz.at[mz], at_z(d))
            else:
                tz[mz] = thalf[mz]

    halves = []
    for d in range(1, 8):
        p = lax.rem(r + d, 8)
        halves.append(send(hsend.at[p], hrecv.at[r], {"rep": p}))
    hrecv[r] = hsend[r]

    def cross(pair):
        for e in (1, -1, 2):
            for b in pair:
                wait(first[b, e])
                for d in (1, -1):
                    part_on(b, e, d)

    def round_again(pair):
        for e, d in ((0, 1), (1, 1), (-1, -1), (2, -1)):
            for b in pair:
                wait(second[b, e, d])
                at = crossed(b, -e, -d)
                block = gq.at[b, at]
                second[b, e, 2 * d] = send(block, block, {"tab": crossed(b, 0, d)})

    def whole_pair(pair):
        for (b, e, d), copy in list(second.items()):
            if b in pair:
                wait(copy)

    cross((0, 1))
    for b in (2, 3):
        for d in (1, -1):
            part_on(b, 0, d)
    joined = jnp.concatenate([qg[b] for b in range(blocks)], axis=1)
    for at in range(0, width, 512):
        in_grad[:, at : at + 512] = dot_nt(joined, wt[at : at + 512, :]).astype(BF)
    round_again((0, 1))
    cross((2, 3))
    wait(*table_in.values())
    summed = tz[0].astype(F32)
    for z in range(1, 4):
        summed = summed + tz[z].astype(F32)

    def table_rows_of(z):
        return t_grad.at[pl.ds(pl.multiple_of(mc * own_half + z * quarter, quarter), quarter)]

    table_mine = table_rows_of(mz)
    table_mine[...] = summed.astype(BF)
    table_out = {d: send(table_mine, table_mine, at_z(d)) for d in (1, -1)}
    send(table_mine, table_mine, mate)
    wait(*spreading)

    def turn(q, carry):
        near[:, pl.ds(pl.multiple_of(q * tokens, tokens), tokens)] = ginp[q].astype(F32).T.astype(BF)
        return carry

    lax.fori_loop(0, shards, turn, 0)

    share = piece_width // 8
    sums_in = {}

    def weigh(pair, n):
        whole_pair(pair)
        for i, b in enumerate(pair):
            part = dot_nn(near[...], gq[b].reshape(shards * tokens, half)).astype(BF)
            psend[n, :, :, i * half : (i + 1) * half] = part.reshape(8, share, half)
        sums_in[n] = []
        for d in range(1, 8):
            p = lax.rem(r + d, 8)
            sums_in[n].append(send(psend.at[n, p], precv.at[n, r], {"rep": p}))
        precv[n, r] = psend[n, r]

    weigh((0, 1), 0)
    round_again((2, 3))

    weigh((2, 3), 1)

    wait(*lows, *halves)
    key_part = dot_tn(
        hrecv[...].reshape(8 * tokens, count // 2), lrecv[...].reshape(8 * tokens, half)
    )
    key_rows = count // shards
    ksend[...] = key_part.astype(BF).reshape(8, key_rows, half)
    key_base = copies.take(shards)
    key_out = []
    for i in range(2):
        for dx in range(side):
            x = lax.rem(mx + dx, side)
            copy = pltpu.make_async_remote_copy(
                src_ref=ksend.at[x * 2 + i],
                dst_ref=krecv.at[me],
                send_sem=ssem.at[key_base + i * side + dx],
                recv_sem=rsem.at[key_base + me],
                device_id={"tab": x * side + 2 * mc + i},
                device_id_type=MESH,
            )
            key_out.append((i, dx, copy))
            if dx:
                copy.start()
            else:

                @pl.when(my != 2 * mc + i)
                def _(copy=copy):
                    copy.start()

                @pl.when(my == 2 * mc + i)
                def _(x=x, i=i):
                    krecv[me] = ksend[x * 2 + i]

    before, after = table_rows_of(up(mz, -1)), table_rows_of(up(mz, 1))
    wait(table_out[1])
    lower = before.at[pl.ds(0, quarter // 2)]
    send(lower, lower, at_z(1))
    send(before, before, mate)
    wait(table_out[-1])
    upper = after.at[pl.ds(quarter // 2, quarter // 2)]
    send(upper, upper, at_z(-1))
    send(after, after, mate)
    table_far = [len(copies.copies) - 4, len(copies.copies) - 2]

    key_last = copies.take(8)
    keeper = my // 2

    def key_share(d):
        return pltpu.make_async_remote_copy(
            src_ref=kfin.at[mz],
            dst_ref=kfin.at[mz],
            send_sem=ssem.at[key_last + d],
            recv_sem=rsem.at[key_last + mz],
            device_id={"rep": lax.rem(r + d, 8)},
            device_id_type=MESH,
        )

    @pl.when(keeper == mc)
    def _():
        for d in range(1, shards):
            q = lax.rem(me + d, shards)
            pltpu.make_async_remote_copy(
                src_ref=ksend.at[0],
                dst_ref=krecv.at[q],
                send_sem=ssem.at[key_base],
                recv_sem=rsem.at[key_base + q],
                device_id={"tab": q},
                device_id_type=MESH,
            ).wait_recv()
        total = krecv[0].astype(F32)
        for q in range(1, shards):
            total = total + krecv[q].astype(F32)
        kfin[mz] = total.astype(BF)
        for d in range(1, 8):
            key_share(d).start()

    for n in range(2):
        wait(*sums_in[n])
        total = precv[n, 0].astype(F32)
        for q in range(1, 8):
            total = total + precv[n, q].astype(F32)
        wfin[n, r] = total.astype(BF)
        mine = wfin.at[n, r]
        for d in range(1, 8):
            send(mine, mine, {"rep": lax.rem(r + d, 8)})
    wait(*table_far)
    across_z = table_rows_of(up(mz, 2))
    send(across_z, across_z, mate)

    for b in range(4):

        @pl.when((b != mz) | (keeper != mc))
        def _(b=b):
            pltpu.make_async_remote_copy(
                src_ref=kfin.at[b],
                dst_ref=kfin.at[b],
                send_sem=ssem.at[key_last],
                recv_sem=rsem.at[key_last + b],
                device_id=mate,
                device_id_type=MESH,
            ).wait_recv()

    for b in range(4):
        k_grad[:, b * half : (b + 1) * half] = kfin[b].astype(F32)
    wait(*range(len(copies.copies)))
    for n in range(2):
        done = wfin[n].reshape(piece_width, 2 * half).astype(F32)
        w_grad[:, n * 2 * half : (n + 1) * 2 * half] = done
    for i, dx, copy in key_out:
        if dx:
            copy.wait_send()
        else:

            @pl.when(my != 2 * mc + i)
            def _(copy=copy):
                copy.wait_send()

    @pl.when(keeper == mc)
    def _():
        for d in range(1, 8):
            key_share(d).wait_send()

    copies.finish()


def deliver_kernel(*refs):
    number = len(refs) // 2
    for i in range(number):
        refs[number + i][...] = refs[i][...]


def sds(shape, dtype):
    return jax.ShapeDtypeStruct(shape, dtype)


def on_device(inputs, grad_out, query_weight, sub_keys, values, owner, slot_rows, sub_index):
    tokens, width = inputs.shape
    cols = query_weight.shape[1]
    count = sub_keys.shape[0]
    heads, top = slot_rows.shape[1:]
    blocks = 2 * heads
    lanes = blocks * top
    half = cols // blocks
    shards = lax.axis_size("tab")
    side = 4
    rows = tokens * heads // shards
    slots = 2 * shards * rows
    table_rows = values.shape[0]
    own = jnp.transpose(owner, (1, 2, 0)).reshape(heads, tokens)
    rows_t = jnp.transpose(slot_rows, (1, 2, 0)).reshape(heads * top, tokens)
    picks_t = jnp.transpose(sub_index, (1, 2, 3, 0)).reshape(lanes, tokens)
    vmem = pl.BlockSpec(memory_space=pltpu.VMEM)
    anywhere = pl.BlockSpec(memory_space=pl.ANY)
    V = pltpu.VMEM
    shapes = (
        sds((tokens, width), BF),
        sds((width // shards, cols), F32),
        sds((count // shards, cols), F32),
        sds((table_rows, width), BF),
    )
    results = pl.pallas_call(
        whole_kernel,
        out_shape=shapes,
        in_specs=[vmem] * 4 + [anywhere] * 4,
        out_specs=(vmem,) * 4,
        scratch_shapes=[
            V((2, side, side, rows, width), BF),
            V((2, side, side, rows, width), BF),
            V((2, shards, rows, width), BF),
            V((tokens, width), BF),
            V((width, cols), BF),
            V((count, cols), BF),
            V((table_rows, width), BF),
            V((tokens, cols), F32),
            V((tokens, cols), BF),
            V((tokens, lanes), F32),
            V((3, tokens // 2, lanes), F32),
            V((2, shards, rows, 2 * lanes), BF),
            V((2, shards, rows, 2 * lanes), BF),
            V((2, shards, rows, lanes), F32),
            V((2, shards, rows, lanes), F32),
            V((table_rows, slots), BF),
            V((table_rows, width), BF),
            V((4, table_rows // 8, width), BF),
            V((4, table_rows // 8, width), BF),
            V((4, table_rows // 8, width), BF),
            V((tokens, 2 * count // 128, 128), F32),
            V((8, tokens, count // 2), BF),
            V((8, tokens, count // 2), BF),
            V((8, tokens, half), BF),
            V((blocks, tokens, half), BF),
            V((blocks, shards, tokens, half), BF),
            V((shards, tokens, width // shards), BF),
            V((width // shards, shards * tokens), BF),
            V((8, count // shards, half), BF),
            V((shards, count // shards, half), BF),
            V((4, count // shards, half), BF),
            V((2, 8, width // shards // 8, 2 * half), BF),
            V((2, 8, width // shards // 8, 2 * half), BF),
            V((2, 8, width // shards // 8, 2 * half), BF),
            pltpu.SemaphoreType.DMA((7,)),
            pltpu.SemaphoreType.DMA((288,)),
            pltpu.SemaphoreType.DMA((288,)),
        ],
        compiler_params=pltpu.CompilerParams(
            collective_id=0, has_side_effects=True, vmem_limit_bytes=60 * 1024 * 1024
        ),
        name="whole",
    )(own, rows_t, picks_t, grad_out, inputs, query_weight, sub_keys, values)
    steps = 4
    specs = [pl.BlockSpec((x.shape[0] // steps, x.shape[1]), lambda i: (i, 0)) for x in shapes]
    return pl.pallas_call(
        deliver_kernel,
        out_shape=shapes,
        grid=(steps,),
        in_specs=specs,
        out_specs=tuple(specs),
        name="deliver",
    )(*results)


def solution(mesh):
    placed = (
        P(("rep", "tab"), None),
        P(("rep", "tab"), None),
        P(),
        P(),
        P("tab", None),
        P(("rep", "tab"), None, None),
        P(("rep", "tab"), None, None),
        P(("rep", "tab"), None, None, None),
    )
    return jax.shard_map(
        on_device,
        mesh=mesh,
        in_specs=placed,
        out_specs=(P(("rep", "tab"), None), P("tab", None), P("tab", None), P("tab", None)),
        check_vma=False,
    )
```

```python
import functools

import jax
import jax.numpy as jnp
from jax import lax
from jax.experimental import pallas as pl
from jax.experimental.pallas import tpu as pltpu
from jax.sharding import PartitionSpec as P

BF = jnp.bfloat16
F32 = jnp.float32
I32 = jnp.int32


def dot_nn(a, b):
    return lax.dot_general(a, b, (((1,), (0,)), ((), ())), preferred_element_type=F32)


def dot_nt(a, b):
    return lax.dot_general(a, b, (((1,), (1,)), ((), ())), preferred_element_type=F32)


def dot_tn(a, b):
    return lax.dot_general(a, b, (((0,), (0,)), ((), ())), preferred_element_type=F32)


def three(x):
    a = x.astype(BF)
    rest = x - a.astype(F32)
    b = rest.astype(BF)
    c = (rest - b.astype(F32)).astype(BF)
    return a, b, c


def iota(shape, dim):
    return lax.broadcasted_iota(I32, shape, dim)

MESH = pl.DeviceIdType.MESH
NEAR = (1, 3, 2)


class Copies:
    def __init__(self, send_sems, recv_sems):
        self.send_sems, self.recv_sems = send_sems, recv_sems
        self.copies, self.got = [], []
        self.used = 0

    def take(self, number):
        self.used += number
        assert self.used <= self.send_sems.shape[0]
        return self.used - number

    def send(self, src, dst, device):
        at = self.take(1)
        copy = pltpu.make_async_remote_copy(
            src_ref=src,
            dst_ref=dst,
            send_sem=self.send_sems.at[at],
            recv_sem=self.recv_sems.at[at],
            device_id=device,
            device_id_type=MESH,
        )
        copy.start()
        self.copies.append(copy)
        self.got.append(False)
        return len(self.copies) - 1

    def wait(self, *which):
        for i in which:
            if not self.got[i]:
                self.copies[i].wait_recv()
                self.got[i] = True

    def finish(self):
        self.wait(*range(len(self.copies)))
        for copy in self.copies:
            copy.wait_send()


def whole_kernel(
    own, rows_t, picks_t, grad, inputs, weight, keys, values,
    in_grad, w_grad, k_grad, t_grad,
    pay, mid, arr, inp, wt, key, val, acc, low, soft, score, wsend, wrecv, back, ret, spread,
    tpart, tcore, thalf, tz, tfold, placed, hsend, hrecv, lrecv, qg, gq, ginp, near, ksend, krecv, kfin,
    psend, precv, wfin, load_sem, ssem, rsem,
):
    heads, tokens = own.shape
    width = grad.shape[1]
    side, rows = pay.shape[1], pay.shape[3]
    shards = side * side
    lanes = picks_t.shape[0]
    blocks = 2 * heads
    top = lanes // blocks
    cols = acc.shape[1]
    half = cols // blocks
    count = key.shape[0]
    tiles = count // 128
    table_rows = val.shape[0]
    slots = 2 * shards * rows
    me, r = lax.axis_index("tab"), lax.axis_index("rep")
    mx, my = me // side, lax.rem(me, side)
    mz, mc = r // 2, lax.rem(r, 2)
    mate = {"rep": mz * 2 + 1 - mc}
    copies = Copies(ssem, rsem)
    send, wait = copies.send, copies.wait

    def up(at, by):
        return lax.rem(at + by + side, side)

    def tab(dx, dy):
        return up(mx, dx) * side + up(my, dy)

    def at_z(d):
        return {"rep": up(mz, d) * 2 + mc}

    loads = [pltpu.make_async_copy(inputs, inp, load_sem.at[0])]
    depth = width // 4
    for i in range(4):
        piece = pl.ds(i * depth, depth)
        loads.append(pltpu.make_async_copy(weight.at[piece], wt.at[piece], load_sem.at[1 + i]))
    loads.append(pltpu.make_async_copy(keys, key, load_sem.at[5]))
    loads.append(pltpu.make_async_copy(values, val, load_sem.at[6]))
    for load in loads:
        load.start()
    barrier = pltpu.get_barrier_semaphore()
    for d in range(1, shards):
        pl.semaphore_signal(
            barrier, inc=1, device_id={"tab": lax.rem(me + d, shards)}, device_id_type=MESH
        )
    for d in range(1, 8):
        pl.semaphore_signal(
            barrier, inc=1, device_id={"rep": lax.rem(r + d, 8)}, device_id_type=MESH
        )

    owned = jnp.concatenate([own[h : h + 1, :] for h in range(heads)], axis=1)
    messages = heads * tokens
    across = jnp.broadcast_to(owned, (messages, messages))
    same = across == across.T
    earlier = iota((messages, messages), 0) < iota((messages, messages), 1)
    rank = jnp.sum(jnp.where(same & earlier, 1.0, 0.0), axis=0, keepdims=True).astype(I32)
    place = (rank // rows) * (shards * rows) + owned * rows + rank % rows

    def hit_rows(part):
        at = iota((shards * rows, messages), 0) + part * shards * rows
        return jnp.where(at == place, 1.0, 0.0)

    phase_one = {}
    for part in range(2):
        hit = hit_rows(part)
        either = hit[:, :tokens]
        for h in range(1, heads):
            either = either + hit[:, h * tokens : (h + 1) * tokens]
        either = either.astype(BF)
        for at in range(0, width, 512):
            block = dot_nn(either, grad[:, at : at + 512]).astype(BF)
            pay[part, :, :, :, at : at + 512] = block.reshape(side, side, rows, 512)
        if part == 0:
            pl.semaphore_wait(barrier, shards + 6)
        for d in NEAR:
            for e in (0,) + NEAR:
                if part == 0:
                    src, device = pay.at[0, up(mx, e), up(my, d)], {"tab": tab(0, d)}
                    onward = mid.at[0, my, up(mx, e)]
                else:
                    src, device = pay.at[1, up(mx, d), up(my, e)], {"tab": tab(d, 0)}
                    onward = mid.at[1, mx, up(my, e)]
                dst = onward if e else arr.at[part, me]
                phase_one[part, d, e] = send(src, dst, device)
    phase_two = {}

    def pass_on(part, d, e):
        if part == 0:
            src = mid.at[0, up(my, -d), up(mx, e)] if d else pay.at[0, up(mx, e), my]
            dst, device = arr.at[0, tab(0, -d)], {"tab": tab(e, 0)}
        else:
            src = mid.at[1, up(mx, -d), up(my, e)] if d else pay.at[1, mx, up(my, e)]
            dst, device = arr.at[1, tab(-d, 0)], {"tab": tab(0, e)}
        phase_two[part, d, e] = send(src, dst, device)

    for part in range(2):
        for e in NEAR:
            pass_on(part, 0, e)
        arr[part, me] = pay[part, mx, my]

    loads[0].wait()
    for i in range(4):
        loads[1 + i].wait()
        piece = dot_nn(inp[:, i * depth : (i + 1) * depth], wt[i * depth : (i + 1) * depth, :])
        acc[...] = piece if i == 0 else acc[...] + piece
    low[...] = acc[...].astype(BF)
    lows = []
    for d in range(1, 8):
        p = lax.rem(r + d, 8)
        piece = pl.ds(pl.multiple_of((p // 2) * half, half), half)
        lows.append(send(low.at[:, piece], lrecv.at[r], {"rep": p}))
    lrecv[r] = low[:, pl.ds(pl.multiple_of(mz * half, half), half)]
    pick = picks_t[...].T
    low_pick = pick % 128
    high_pick = pick // 128
    lane_block = iota((tokens, lanes), 1) // top
    head_of = lane_block // 2
    chosen = jnp.zeros((tokens, lanes), F32)
    loads[5].wait()
    for b in range(blocks):
        parts = three(acc[:, b * half : (b + 1) * half])
        for j in range(tiles):
            names = key[j * 128 : (j + 1) * 128, b * half : (b + 1) * half]
            part = dot_nt(parts[2], names) + dot_nt(parts[1], names) + dot_nt(parts[0], names)
            got = jnp.take_along_axis(part, low_pick, axis=1)
            chosen = jnp.where((high_pick == j) & (lane_block == b), got, chosen)
    even = lane_block % 2 == 0
    other = jnp.where(
        even, pltpu.roll(chosen, lanes - top, axis=1), pltpu.roll(chosen, top, axis=1)
    )
    scores = chosen + other

    def over_heads(x, fill, reduce):
        out = jnp.zeros((tokens, lanes), F32)
        for h in range(heads):
            one = reduce(jnp.where(head_of == h, x, fill), axis=1, keepdims=True)
            out = jnp.where(head_of == h, one, out)
        return out

    raised = jnp.exp(scores - over_heads(scores, -jnp.inf, jnp.max))
    weights = raised / (over_heads(raised, 0.0, jnp.sum) * 0.5)
    soft[...] = weights
    low_soft = weights.astype(BF).astype(F32)

    def hits(h):
        column = jnp.broadcast_to(place[:, h * tokens : (h + 1) * tokens], (tokens, tokens)).T
        column = jnp.concatenate([column] * (slots // tokens), axis=1)
        return jnp.where(iota((tokens, slots), 1) == column, 1.0, 0.0).astype(BF)

    sent = jnp.zeros((slots, 2 * lanes), F32)
    for h in range(heads):
        one = rows_t[h * top : (h + 1) * top, :].astype(F32)
        numbers = jnp.concatenate([one] * blocks, axis=0).T
        turned = low_soft if h == 0 else pltpu.roll(low_soft, lanes - h * 2 * top, axis=1)
        sent = sent + dot_tn(hits(h), jnp.concatenate([numbers, turned], axis=1).astype(BF))
    wsend[...] = sent.astype(BF).reshape(2, shards, rows, 2 * lanes)

    def pass_all(d):
        for e in (0,) + NEAR:
            for part in range(2):
                wait(phase_one[part, d, e])
                if e:
                    pass_on(part, d, e)

    pass_all(1)
    weighing = []
    for dx in range(side):
        for dy in range(side):
            if dx or dy:
                p = tab(dx, dy)
                weighing.append(send(wsend.at[:, p], wrecv.at[:, me], {"tab": p}))
    wrecv[:, me] = wsend[:, me]
    pass_all(3)
    pass_all(2)

    wait(*weighing)
    band = 128
    per_band = band // rows

    def spread_band(g, carry):
        part, at = g // (shards // per_band), lax.rem(g, shards // per_band) * per_band
        block = wrecv[part, pl.ds(at, per_band)].reshape(band, 2 * lanes).astype(F32)
        row_t, soft_t = block[:, :lanes].T, block[:, lanes:].T
        names = iota((table_rows, band), 0).astype(F32)
        held = jnp.zeros((table_rows, band), F32)
        for k in range(top):
            held = held + jnp.where(names == row_t[k : k + 1], soft_t[k : k + 1], 0.0)
        spread[:, pl.ds(pl.multiple_of(g * band, band), band)] = held.astype(BF)
        return carry

    lax.fori_loop(0, slots // band, spread_band, 0)

    loads[6].wait()
    for d in (0,) + NEAR:
        for e in NEAR:
            for part in range(2):
                wait(phase_two[part, d, e])
    for part in range(2):
        for q in range(0, shards, per_band):
            here = slice(q, q + per_band)
            product = dot_nt(arr[part, here].reshape(band, width), val[...])
            name = wrecv[part, here, :, :lanes].reshape(band, lanes).astype(I32)
            out = jnp.zeros((band, lanes), F32)
            for j in range(table_rows // 128):
                got = jnp.take_along_axis(product[:, j * 128 : (j + 1) * 128], name % 128, axis=1)
                out = jnp.where(name // 128 == j, got, out)
            back[part, here] = out.reshape(per_band, rows, lanes)
    returning = []
    for dx in range(side):
        for dy in range(side):
            if dx or dy:
                p = tab(dx, dy)
                returning.append(send(back.at[:, p], ret.at[:, me], {"tab": p}))
    ret[:, me] = back[:, me]
    spreading = []
    piece_width = width // shards
    for dx in (0,) + NEAR:
        for dy in (0,) + NEAR:
            if dx or dy:
                p = tab(dx, dy)
                piece = pl.ds(pl.multiple_of(p * piece_width, piece_width), piece_width)
                spreading.append(send(inp.at[:, piece], ginp.at[me], {"tab": p}))
    ginp[me] = inp[:, pl.ds(pl.multiple_of(me * piece_width, piece_width), piece_width)]

    own_half = table_rows // 2
    quarter = own_half // 4
    for at in range(0, width, 512):
        column = arr[:, :, :, at : at + 512].reshape(slots, 512)
        tpart[:, at : at + 512] = dot_nn(spread[...], column).astype(BF)
    swaps = {}
    for d in (2, 1, 3, 0):
        z = up(mz, d)
        row = pl.multiple_of((1 - mc) * own_half + z * quarter, quarter)
        swaps[d] = send(tpart.at[pl.ds(row, quarter)], tcore.at[z], mate)

    wait(*returning)
    parts = three(ret[...].reshape(slots, lanes))
    slot_grad = jnp.zeros((tokens, lanes), F32)
    for h in range(heads):
        hit = hits(h)
        got = dot_nn(hit, parts[2]) + dot_nn(hit, parts[1]) + dot_nn(hit, parts[0])
        slot_grad = jnp.where(head_of == h, got, slot_grad)
    weights = soft[...]
    mean = over_heads(weights * slot_grad, 0.0, jnp.sum) * 0.5
    score_grad = weights * (slot_grad - mean)
    pairs = tokens // 2
    early_lanes = iota((pairs, lanes), 1) < lanes // 2

    def place_head(h):
        def pack(x):
            turned = pltpu.roll(x, lanes // 2, axis=1)
            one, two = (x, turned) if h == 0 else (turned, x)
            return jnp.where(early_lanes, one[:pairs], two[pairs:])

        score[0] = pack(score_grad)
        score[1] = pack(low_pick.astype(F32))
        score[2] = pack(high_pick.astype(F32)) + (tiles * lane_block[:pairs]).astype(F32)

        def place_band(i, carry):
            here = pl.ds(pl.multiple_of(i * 8, 8), 8)
            amount, low8, high8 = score[0, here, :], score[1, here, :], score[2, here, :]
            high_names = iota((blocks * tiles, lanes), 0).astype(F32)
            low_names = iota((128, lanes), 0).astype(F32)
            for u in range(8):
                left = jnp.where(high_names == high8[u : u + 1], amount[u : u + 1], 0.0).astype(BF)
                right = jnp.where(low_names == low8[u : u + 1], 1.0, 0.0).astype(BF)
                sums = dot_nt(left, right)
                placed[i * 8 + u] = sums[: 2 * tiles]
                placed[i * 8 + u + pairs] = sums[2 * tiles :]
            return carry

        lax.fori_loop(0, pairs // 8, place_band, 0)

    first, second = {}, {}

    def crossed(b, one, two):
        return tab(two, one) if b % 2 == 0 else tab(one, two)

    def part_on(b, e, d):
        at = crossed(b, -e, 0)
        src = gq.at[b, at] if e else qg.at[b]
        second[b, e, d] = send(src, gq.at[b, at], {"tab": crossed(b, 0, d)})

    def joint(d):
        z = up(mz, d)
        wait(swaps[d])
        row = pl.multiple_of(mc * own_half + z * quarter, quarter)
        return tpart[pl.ds(row, quarter), :].astype(F32) + tcore[z].astype(F32)

    fold = quarter // 2
    distant = up(mz, 2)
    thalf[distant] = joint(2).astype(BF)
    fold_up = send(thalf.at[distant, pl.ds(0, fold)], tfold.at[0], at_z(1))
    fold_down = send(thalf.at[distant, pl.ds(fold, fold)], tfold.at[1], at_z(-1))
    table_in = {}
    for b in range(blocks):
        if b % 2 == 0:
            place_head(b // 2)
        total = jnp.zeros((tokens, half), F32)
        for j in range(tiles):
            sums = placed[:, b % 2 * tiles + j, :].astype(BF)
            hsend[2 * b + j % 2, :, (j // 2) * 128 : (j // 2 + 1) * 128] = sums
            total = total + dot_nn(sums, key[j * 128 : (j + 1) * 128, b * half : (b + 1) * half])
        qg[b] = total.astype(BF)
        gq[b, me] = total.astype(BF)
        for d in (1, -1, 2):
            first[b, d] = send(qg.at[b], gq.at[b, me], {"tab": crossed(b, d, 0)})
        if b < 2:
            for d in (1, -1):
                part_on(b, 0, d)
        if b != 1:
            continue
        whole = joint(1)
        wait(fold_up)
        thalf[up(mz, 1), :fold] = (whole[:fold] + tfold[0].astype(F32)).astype(BF)
        thalf[up(mz, 1), fold:] = whole[fold:].astype(BF)
        table_in[1] = send(thalf.at[up(mz, 1)], tz.at[0], at_z(1))
        whole = joint(3)
        wait(fold_down)
        thalf[up(mz, -1), :fold] = whole[:fold].astype(BF)
        thalf[up(mz, -1), fold:] = (whole[fold:] + tfold[1].astype(F32)).astype(BF)
        table_in[3] = send(thalf.at[up(mz, -1)], tz.at[1], at_z(-1))
        thalf[mz] = joint(0).astype(BF)

    halves = []
    for d in range(1, 8):
        p = lax.rem(r + d, 8)
        halves.append(send(hsend.at[p], hrecv.at[r], {"rep": p}))
    hrecv[r] = hsend[r]

    def cross(pair):
        for e in (1, -1, 2):
            for b in pair:
                wait(first[b, e])
                for d in (1, -1):
                    part_on(b, e, d)

    def round_again(pair):
        for e, d in ((0, 1), (1, 1), (-1, -1), (2, -1)):
            for b in pair:
                wait(second[b, e, d])
                at = crossed(b, -e, -d)
                block = gq.at[b, at]
                second[b, e, 2 * d] = send(block, block, {"tab": crossed(b, 0, d)})

    def whole_pair(pair):
        for (b, e, d), copy in list(second.items()):
            if b in pair:
                wait(copy)

    cross((0, 1))
    for b in (2, 3):
        for d in (1, -1):
            part_on(b, 0, d)
    joined = jnp.concatenate([qg[b] for b in range(blocks)], axis=1)
    for at in range(0, width, 512):
        in_grad[:, at : at + 512] = dot_nt(joined, wt[at : at + 512, :]).astype(BF)
    round_again((0, 1))
    cross((2, 3))
    wait(*table_in.values())
    summed = thalf[mz].astype(F32) + tz[0].astype(F32) + tz[1].astype(F32)

    def table_rows_of(z):
        return t_grad.at[pl.ds(pl.multiple_of(mc * own_half + z * quarter, quarter), quarter)]

    table_mine = table_rows_of(mz)
    table_mine[...] = summed.astype(BF)
    table_out = {d: send(table_mine, table_mine, at_z(d)) for d in (1, -1)}
    send(table_mine, table_mine, mate)
    wait(*spreading)

    def turn(q, carry):
        near[:, pl.ds(pl.multiple_of(q * tokens, tokens), tokens)] = ginp[q].astype(F32).T.astype(BF)
        return carry

    lax.fori_loop(0, shards, turn, 0)

    share = piece_width // 8
    sums_in = {}

    def weigh(pair, n):
        whole_pair(pair)
        for i, b in enumerate(pair):
            part = dot_nn(near[...], gq[b].reshape(shards * tokens, half)).astype(BF)
            psend[n, :, :, i * half : (i + 1) * half] = part.reshape(8, share, half)
        sums_in[n] = []
        for d in range(1, 8):
            p = lax.rem(r + d, 8)
            sums_in[n].append(send(psend.at[n, p], precv.at[n, r], {"rep": p}))
        precv[n, r] = psend[n, r]

    weigh((0, 1), 0)
    round_again((2, 3))

    weigh((2, 3), 1)

    wait(*lows, *halves)
    key_part = dot_tn(
        hrecv[...].reshape(8 * tokens, count // 2), lrecv[...].reshape(8 * tokens, half)
    )
    key_rows = count // shards
    ksend[...] = key_part.astype(BF).reshape(8, key_rows, half)
    key_base = copies.take(shards)
    key_out = []
    for i in range(2):
        for dx in range(side):
            x = lax.rem(mx + dx, side)
            copy = pltpu.make_async_remote_copy(
                src_ref=ksend.at[x * 2 + i],
                dst_ref=krecv.at[me],
                send_sem=ssem.at[key_base + i * side + dx],
                recv_sem=rsem.at[key_base + me],
                device_id={"tab": x * side + 2 * mc + i},
                device_id_type=MESH,
            )
            key_out.append((i, dx, copy))
            if dx:
                copy.start()
            else:

                @pl.when(my != 2 * mc + i)
                def _(copy=copy):
                    copy.start()

                @pl.when(my == 2 * mc + i)
                def _(x=x, i=i):
                    krecv[me] = ksend[x * 2 + i]

    before, after = table_rows_of(up(mz, -1)), table_rows_of(up(mz, 1))
    wait(table_out[1])
    lower = before.at[pl.ds(0, quarter // 2)]
    send(lower, lower, at_z(1))
    send(before, before, mate)
    wait(table_out[-1])
    upper = after.at[pl.ds(quarter // 2, quarter // 2)]
    send(upper, upper, at_z(-1))
    send(after, after, mate)
    table_far = [len(copies.copies) - 4, len(copies.copies) - 2]

    key_last = copies.take(8)
    keeper = my // 2

    def key_share(d):
        return pltpu.make_async_remote_copy(
            src_ref=kfin.at[mz],
            dst_ref=kfin.at[mz],
            send_sem=ssem.at[key_last + d],
            recv_sem=rsem.at[key_last + mz],
            device_id={"rep": lax.rem(r + d, 8)},
            device_id_type=MESH,
        )

    @pl.when(keeper == mc)
    def _():
        for d in range(1, shards):
            q = lax.rem(me + d, shards)
            pltpu.make_async_remote_copy(
                src_ref=ksend.at[0],
                dst_ref=krecv.at[q],
                send_sem=ssem.at[key_base],
                recv_sem=rsem.at[key_base + q],
                device_id={"tab": q},
                device_id_type=MESH,
            ).wait_recv()
        total = krecv[0].astype(F32)
        for q in range(1, shards):
            total = total + krecv[q].astype(F32)
        kfin[mz] = total.astype(BF)
        for d in range(1, 8):
            key_share(d).start()

    for n in range(2):
        wait(*sums_in[n])
        total = precv[n, 0].astype(F32)
        for q in range(1, 8):
            total = total + precv[n, q].astype(F32)
        wfin[n, r] = total.astype(BF)
        mine = wfin.at[n, r]
        if n == 0:
            along = {d: send(mine, mine, at_z(d)) for d in NEAR}
            send(mine, mine, mate)
        else:
            for d in range(1, 8):
                send(mine, mine, {"rep": lax.rem(r + d, 8)})
    for d in NEAR:
        wait(along[d])
        part = wfin.at[0, up(mz, -d) * 2 + mc]
        send(part, part, mate)
    wait(*table_far)
    across_z = table_rows_of(up(mz, 2))
    send(across_z, across_z, mate)

    for b in range(4):

        @pl.when((b != mz) | (keeper != mc))
        def _(b=b):
            pltpu.make_async_remote_copy(
                src_ref=kfin.at[b],
                dst_ref=kfin.at[b],
                send_sem=ssem.at[key_last],
                recv_sem=rsem.at[key_last + b],
                device_id=mate,
                device_id_type=MESH,
            ).wait_recv()

    for b in range(4):
        k_grad[:, b * half : (b + 1) * half] = kfin[b].astype(F32)
    wait(*range(len(copies.copies)))
    for n in range(2):
        done = wfin[n].reshape(piece_width, 2 * half).astype(F32)
        w_grad[:, n * 2 * half : (n + 1) * 2 * half] = done
    for i, dx, copy in key_out:
        if dx:
            copy.wait_send()
        else:

            @pl.when(my != 2 * mc + i)
            def _(copy=copy):
                copy.wait_send()

    @pl.when(keeper == mc)
    def _():
        for d in range(1, 8):
            key_share(d).wait_send()

    copies.finish()


def deliver_kernel(pieces, *refs):
    number = len(pieces)
    sources, targets = refs[:number], refs[number : 2 * number]
    held, sems = refs[2 * number : 3 * number], refs[-1]
    moves = []
    for i, count in enumerate(pieces):
        size = held[i].shape[0] // count
        for j in range(count):
            here = pl.ds(j * size, size)
            at = len(moves)
            moves.append(
                (
                    pltpu.make_async_copy(sources[i].at[here], held[i].at[here], sems.at[0, at]),
                    pltpu.make_async_copy(held[i].at[here], targets[i].at[here], sems.at[1, at]),
                )
            )
    for fetch, _ in moves:
        fetch.start()
    for fetch, store in moves:
        fetch.wait()
        store.start()
    for _, store in moves:
        store.wait()


def sds(shape, dtype):
    return jax.ShapeDtypeStruct(shape, dtype)


def on_device(inputs, grad_out, query_weight, sub_keys, values, owner, slot_rows, sub_index):
    tokens, width = inputs.shape
    cols = query_weight.shape[1]
    count = sub_keys.shape[0]
    heads, top = slot_rows.shape[1:]
    blocks = 2 * heads
    lanes = blocks * top
    half = cols // blocks
    shards = lax.axis_size("tab")
    side = 4
    rows = tokens * heads // shards
    slots = 2 * shards * rows
    table_rows = values.shape[0]
    own = jnp.transpose(owner, (1, 2, 0)).reshape(heads, tokens)
    rows_t = jnp.transpose(slot_rows, (1, 2, 0)).reshape(heads * top, tokens)
    picks_t = jnp.transpose(sub_index, (1, 2, 3, 0)).reshape(lanes, tokens)
    vmem = pl.BlockSpec(memory_space=pltpu.VMEM)
    anywhere = pl.BlockSpec(memory_space=pl.ANY)
    V = pltpu.VMEM
    shapes = (
        sds((tokens, width), BF),
        sds((width // shards, cols), F32),
        sds((count // shards, cols), F32),
        sds((table_rows, width), BF),
    )
    results = pl.pallas_call(
        whole_kernel,
        out_shape=shapes,
        in_specs=[vmem] * 4 + [anywhere] * 4,
        out_specs=(vmem,) * 4,
        scratch_shapes=[
            V((2, side, side, rows, width), BF),
            V((2, side, side, rows, width), BF),
            V((2, shards, rows, width), BF),
            V((tokens, width), BF),
            V((width, cols), BF),
            V((count, cols), BF),
            V((table_rows, width), BF),
            V((tokens, cols), F32),
            V((tokens, cols), BF),
            V((tokens, lanes), F32),
            V((3, tokens // 2, lanes), F32),
            V((2, shards, rows, 2 * lanes), BF),
            V((2, shards, rows, 2 * lanes), BF),
            V((2, shards, rows, lanes), F32),
            V((2, shards, rows, lanes), F32),
            V((table_rows, slots), BF),
            V((table_rows, width), BF),
            V((4, table_rows // 8, width), BF),
            V((4, table_rows // 8, width), BF),
            V((2, table_rows // 8, width), BF),
            V((2, table_rows // 16, width), BF),
            V((tokens, 2 * count // 128, 128), F32),
            V((8, tokens, count // 2), BF),
            V((8, tokens, count // 2), BF),
            V((8, tokens, half), BF),
            V((blocks, tokens, half), BF),
            V((blocks, shards, tokens, half), BF),
            V((shards, tokens, width // shards), BF),
            V((width // shards, shards * tokens), BF),
            V((8, count // shards, half), BF),
            V((shards, count // shards, half), BF),
            V((4, count // shards, half), BF),
            V((2, 8, width // shards // 8, 2 * half), BF),
            V((2, 8, width // shards // 8, 2 * half), BF),
            V((2, 8, width // shards // 8, 2 * half), BF),
            pltpu.SemaphoreType.DMA((7,)),
            pltpu.SemaphoreType.DMA((288,)),
            pltpu.SemaphoreType.DMA((288,)),
        ],
        compiler_params=pltpu.CompilerParams(
            collective_id=0, has_side_effects=True, vmem_limit_bytes=60 * 1024 * 1024
        ),
        name="whole",
    )(own, rows_t, picks_t, grad_out, inputs, query_weight, sub_keys, values)
    pieces = (4, 4, 1, 8)
    return pl.pallas_call(
        functools.partial(deliver_kernel, pieces),
        out_shape=shapes,
        in_specs=[anywhere] * 4,
        out_specs=(anywhere,) * 4,
        scratch_shapes=[V(x.shape, x.dtype) for x in shapes]
        + [pltpu.SemaphoreType.DMA((2, sum(pieces)))],
        name="deliver",
    )(*results)


def solution(mesh):
    placed = (
        P(("rep", "tab"), None),
        P(("rep", "tab"), None),
        P(),
        P(),
        P("tab", None),
        P(("rep", "tab"), None, None),
        P(("rep", "tab"), None, None),
        P(("rep", "tab"), None, None, None),
    )
    return jax.shard_map(
        on_device,
        mesh=mesh,
        in_specs=placed,
        out_specs=(P(("rep", "tab"), None), P("tab", None), P("tab", None), P("tab", None)),
        check_vma=False,
    )
```

```python
import functools

import jax
import jax.numpy as jnp
from jax import lax
from jax.experimental import pallas as pl
from jax.experimental.pallas import tpu as pltpu
from jax.sharding import PartitionSpec as P

BF = jnp.bfloat16
F32 = jnp.float32
I32 = jnp.int32


def dot_nn(a, b):
    return lax.dot_general(a, b, (((1,), (0,)), ((), ())), preferred_element_type=F32)


def dot_nt(a, b):
    return lax.dot_general(a, b, (((1,), (1,)), ((), ())), preferred_element_type=F32)


def dot_tn(a, b):
    return lax.dot_general(a, b, (((0,), (0,)), ((), ())), preferred_element_type=F32)


def three(x):
    a = x.astype(BF)
    rest = x - a.astype(F32)
    b = rest.astype(BF)
    c = (rest - b.astype(F32)).astype(BF)
    return a, b, c


def iota(shape, dim):
    return lax.broadcasted_iota(I32, shape, dim)

MESH = pl.DeviceIdType.MESH
NEAR = (1, 3, 2)


class Copies:
    def __init__(self, send_sems, recv_sems):
        self.send_sems, self.recv_sems = send_sems, recv_sems
        self.copies, self.got = [], []
        self.used = 0

    def take(self, number):
        self.used += number
        assert self.used <= self.send_sems.shape[0]
        return self.used - number

    def send(self, src, dst, device):
        at = self.take(1)
        copy = pltpu.make_async_remote_copy(
            src_ref=src,
            dst_ref=dst,
            send_sem=self.send_sems.at[at],
            recv_sem=self.recv_sems.at[at],
            device_id=device,
            device_id_type=MESH,
        )
        copy.start()
        self.copies.append(copy)
        self.got.append(False)
        return len(self.copies) - 1

    def wait(self, *which):
        for i in which:
            if not self.got[i]:
                self.copies[i].wait_recv()
                self.got[i] = True

    def finish(self):
        self.wait(*range(len(self.copies)))
        for copy in self.copies:
            copy.wait_send()


def whole_kernel(
    own, rows_t, picks_t, grad, inputs, weight, keys, values,
    in_grad, w_grad, k_grad, t_grad,
    pay, mid, arr, inp, wt, key, val, acc, low, soft, score, wsend, wrecv, back, ret, spread,
    tpart, tcore, thalf, tz, tfold, placed, hsend, hrecv, lrecv, qg, gq, ginp, near, ksend, krecv, kfin,
    psend, precv, wfin, load_sem, ssem, rsem,
):
    heads, tokens = own.shape
    width = grad.shape[1]
    side, rows = pay.shape[1], pay.shape[3]
    shards = side * side
    lanes = picks_t.shape[0]
    blocks = 2 * heads
    top = lanes // blocks
    cols = acc.shape[1]
    half = cols // blocks
    count = key.shape[0]
    tiles = count // 128
    table_rows = val.shape[0]
    slots = 2 * shards * rows
    me, r = lax.axis_index("tab"), lax.axis_index("rep")
    mx, my = me // side, lax.rem(me, side)
    mz, mc = r // 2, lax.rem(r, 2)
    mate = {"rep": mz * 2 + 1 - mc}
    copies = Copies(ssem, rsem)
    send, wait = copies.send, copies.wait

    def up(at, by):
        return lax.rem(at + by + side, side)

    def tab(dx, dy):
        return up(mx, dx) * side + up(my, dy)

    def at_z(d):
        return {"rep": up(mz, d) * 2 + mc}

    loads = [pltpu.make_async_copy(inputs, inp, load_sem.at[0])]
    depth = width // 4
    for i in range(4):
        piece = pl.ds(i * depth, depth)
        loads.append(pltpu.make_async_copy(weight.at[piece], wt.at[piece], load_sem.at[1 + i]))
    loads.append(pltpu.make_async_copy(keys, key, load_sem.at[5]))
    loads.append(pltpu.make_async_copy(values, val, load_sem.at[6]))
    for load in loads:
        load.start()
    barrier = pltpu.get_barrier_semaphore()
    for d in range(1, shards):
        pl.semaphore_signal(
            barrier, inc=1, device_id={"tab": lax.rem(me + d, shards)}, device_id_type=MESH
        )
    for d in range(1, 8):
        pl.semaphore_signal(
            barrier, inc=1, device_id={"rep": lax.rem(r + d, 8)}, device_id_type=MESH
        )

    owned = jnp.concatenate([own[h : h + 1, :] for h in range(heads)], axis=1)
    messages = heads * tokens
    across = jnp.broadcast_to(owned, (messages, messages))
    same = across == across.T
    earlier = iota((messages, messages), 0) < iota((messages, messages), 1)
    rank = jnp.sum(jnp.where(same & earlier, 1.0, 0.0), axis=0, keepdims=True).astype(I32)
    place = (rank // rows) * (shards * rows) + owned * rows + rank % rows

    def hit_rows(part):
        at = iota((shards * rows, messages), 0) + part * shards * rows
        return jnp.where(at == place, 1.0, 0.0)

    phase_one = {}
    for part in range(2):
        hit = hit_rows(part)
        either = hit[:, :tokens]
        for h in range(1, heads):
            either = either + hit[:, h * tokens : (h + 1) * tokens]
        either = either.astype(BF)
        for at in range(0, width, 512):
            block = dot_nn(either, grad[:, at : at + 512]).astype(BF)
            pay[part, :, :, :, at : at + 512] = block.reshape(side, side, rows, 512)
        if part == 0:
            pl.semaphore_wait(barrier, shards + 6)
        for d in NEAR:
            for e in (0,) + NEAR:
                if part == 0:
                    src, device = pay.at[0, up(mx, e), up(my, d)], {"tab": tab(0, d)}
                    onward = mid.at[0, my, up(mx, e)]
                else:
                    src, device = pay.at[1, up(mx, d), up(my, e)], {"tab": tab(d, 0)}
                    onward = mid.at[1, mx, up(my, e)]
                dst = onward if e else arr.at[part, me]
                phase_one[part, d, e] = send(src, dst, device)
    phase_two = {}

    def pass_on(part, d, e):
        if part == 0:
            src = mid.at[0, up(my, -d), up(mx, e)] if d else pay.at[0, up(mx, e), my]
            dst, device = arr.at[0, tab(0, -d)], {"tab": tab(e, 0)}
        else:
            src = mid.at[1, up(mx, -d), up(my, e)] if d else pay.at[1, mx, up(my, e)]
            dst, device = arr.at[1, tab(-d, 0)], {"tab": tab(0, e)}
        phase_two[part, d, e] = send(src, dst, device)

    for part in range(2):
        for e in NEAR:
            pass_on(part, 0, e)
        arr[part, me] = pay[part, mx, my]

    loads[0].wait()
    for i in range(4):
        loads[1 + i].wait()
        piece = dot_nn(inp[:, i * depth : (i + 1) * depth], wt[i * depth : (i + 1) * depth, :])
        acc[...] = piece if i == 0 else acc[...] + piece
    low[...] = acc[...].astype(BF)
    lows = []
    for d in range(1, 8):
        p = lax.rem(r + d, 8)
        piece = pl.ds(pl.multiple_of((p // 2) * half, half), half)
        lows.append(send(low.at[:, piece], lrecv.at[r], {"rep": p}))
    lrecv[r] = low[:, pl.ds(pl.multiple_of(mz * half, half), half)]
    pick = picks_t[...].T
    low_pick = pick % 128
    high_pick = pick // 128
    lane_block = iota((tokens, lanes), 1) // top
    head_of = lane_block // 2
    chosen = jnp.zeros((tokens, lanes), F32)
    loads[5].wait()
    for b in range(blocks):
        parts = three(acc[:, b * half : (b + 1) * half])
        for j in range(tiles):
            names = key[j * 128 : (j + 1) * 128, b * half : (b + 1) * half]
            part = dot_nt(parts[2], names) + dot_nt(parts[1], names) + dot_nt(parts[0], names)
            got = jnp.take_along_axis(part, low_pick, axis=1)
            chosen = jnp.where((high_pick == j) & (lane_block == b), got, chosen)
    even = lane_block % 2 == 0
    other = jnp.where(
        even, pltpu.roll(chosen, lanes - top, axis=1), pltpu.roll(chosen, top, axis=1)
    )
    scores = chosen + other

    def over_heads(x, fill, reduce):
        out = jnp.zeros((tokens, lanes), F32)
        for h in range(heads):
            one = reduce(jnp.where(head_of == h, x, fill), axis=1, keepdims=True)
            out = jnp.where(head_of == h, one, out)
        return out

    raised = jnp.exp(scores - over_heads(scores, -jnp.inf, jnp.max))
    weights = raised / (over_heads(raised, 0.0, jnp.sum) * 0.5)
    soft[...] = weights
    low_soft = weights.astype(BF).astype(F32)

    def hits(h):
        column = jnp.broadcast_to(place[:, h * tokens : (h + 1) * tokens], (tokens, tokens)).T
        column = jnp.concatenate([column] * (slots // tokens), axis=1)
        return jnp.where(iota((tokens, slots), 1) == column, 1.0, 0.0).astype(BF)

    sent = jnp.zeros((slots, 2 * lanes), F32)
    for h in range(heads):
        one = rows_t[h * top : (h + 1) * top, :].astype(F32)
        numbers = jnp.concatenate([one] * blocks, axis=0).T
        turned = low_soft if h == 0 else pltpu.roll(low_soft, lanes - h * 2 * top, axis=1)
        sent = sent + dot_tn(hits(h), jnp.concatenate([numbers, turned], axis=1).astype(BF))
    wsend[...] = sent.astype(BF).reshape(2, shards, rows, 2 * lanes)

    def pass_all(d):
        for e in (0,) + NEAR:
            for part in range(2):
                wait(phase_one[part, d, e])
                if e:
                    pass_on(part, d, e)

    pass_all(1)
    weighing = []
    for dx in range(side):
        for dy in range(side):
            if dx or dy:
                p = tab(dx, dy)
                weighing.append(send(wsend.at[:, p], wrecv.at[:, me], {"tab": p}))
    wrecv[:, me] = wsend[:, me]
    pass_all(3)
    pass_all(2)

    wait(*weighing)
    band = 128
    per_band = band // rows

    def spread_band(g, carry):
        part, at = g // (shards // per_band), lax.rem(g, shards // per_band) * per_band
        block = wrecv[part, pl.ds(at, per_band)].reshape(band, 2 * lanes).astype(F32)
        row_t, soft_t = block[:, :lanes].T, block[:, lanes:].T
        names = iota((table_rows, band), 0).astype(F32)
        held = jnp.zeros((table_rows, band), F32)
        for k in range(top):
            held = held + jnp.where(names == row_t[k : k + 1], soft_t[k : k + 1], 0.0)
        spread[:, pl.ds(pl.multiple_of(g * band, band), band)] = held.astype(BF)
        return carry

    lax.fori_loop(0, slots // band, spread_band, 0)

    loads[6].wait()
    for d in (0,) + NEAR:
        for e in NEAR:
            for part in range(2):
                wait(phase_two[part, d, e])
    for part in range(2):
        for q in range(0, shards, per_band):
            here = slice(q, q + per_band)
            product = dot_nt(arr[part, here].reshape(band, width), val[...])
            name = wrecv[part, here, :, :lanes].reshape(band, lanes).astype(I32)
            out = jnp.zeros((band, lanes), F32)
            for j in range(table_rows // 128):
                got = jnp.take_along_axis(product[:, j * 128 : (j + 1) * 128], name % 128, axis=1)
                out = jnp.where(name // 128 == j, got, out)
            back[part, here] = out.reshape(per_band, rows, lanes)
    returning = []
    for dx in range(side):
        for dy in range(side):
            if dx or dy:
                p = tab(dx, dy)
                returning.append(send(back.at[:, p], ret.at[:, me], {"tab": p}))
    ret[:, me] = back[:, me]
    spreading = []
    piece_width = width // shards
    for dx in (0,) + NEAR:
        for dy in (0,) + NEAR:
            if dx or dy:
                p = tab(dx, dy)
                piece = pl.ds(pl.multiple_of(p * piece_width, piece_width), piece_width)
                spreading.append(send(inp.at[:, piece], ginp.at[me], {"tab": p}))
    ginp[me] = inp[:, pl.ds(pl.multiple_of(me * piece_width, piece_width), piece_width)]

    own_half = table_rows // 2
    quarter = own_half // 4
    for at in range(0, width, 512):
        column = arr[:, :, :, at : at + 512].reshape(slots, 512)
        tpart[:, at : at + 512] = dot_nn(spread[...], column).astype(BF)
    swaps = {}
    for d in (2, 1, 3, 0):
        z = up(mz, d)
        row = pl.multiple_of((1 - mc) * own_half + z * quarter, quarter)
        swaps[d] = send(tpart.at[pl.ds(row, quarter)], tcore.at[z], mate)

    wait(*returning)
    parts = three(ret[...].reshape(slots, lanes))
    slot_grad = jnp.zeros((tokens, lanes), F32)
    for h in range(heads):
        hit = hits(h)
        got = dot_nn(hit, parts[2]) + dot_nn(hit, parts[1]) + dot_nn(hit, parts[0])
        slot_grad = jnp.where(head_of == h, got, slot_grad)
    weights = soft[...]
    mean = over_heads(weights * slot_grad, 0.0, jnp.sum) * 0.5
    score_grad = weights * (slot_grad - mean)
    pairs = tokens // 2
    early_lanes = iota((pairs, lanes), 1) < lanes // 2

    def place_head(h):
        def pack(x):
            turned = pltpu.roll(x, lanes // 2, axis=1)
            one, two = (x, turned) if h == 0 else (turned, x)
            return jnp.where(early_lanes, one[:pairs], two[pairs:])

        score[0] = pack(score_grad)
        score[1] = pack(low_pick.astype(F32))
        score[2] = pack(high_pick.astype(F32)) + (tiles * lane_block[:pairs]).astype(F32)

        def place_band(i, carry):
            here = pl.ds(pl.multiple_of(i * 8, 8), 8)
            amount, low8, high8 = score[0, here, :], score[1, here, :], score[2, here, :]
            high_names = iota((blocks * tiles, lanes), 0).astype(F32)
            low_names = iota((128, lanes), 0).astype(F32)
            for u in range(8):
                left = jnp.where(high_names == high8[u : u + 1], amount[u : u + 1], 0.0).astype(BF)
                right = jnp.where(low_names == low8[u : u + 1], 1.0, 0.0).astype(BF)
                sums = dot_nt(left, right)
                placed[i * 8 + u] = sums[: 2 * tiles]
                placed[i * 8 + u + pairs] = sums[2 * tiles :]
            return carry

        lax.fori_loop(0, pairs // 8, place_band, 0)

    first, second = {}, {}

    def crossed(b, one, two):
        return tab(two, one) if b % 2 == 0 else tab(one, two)

    def part_on(b, e, d):
        at = crossed(b, -e, 0)
        src = gq.at[b, at] if e else qg.at[b]
        second[b, e, d] = send(src, gq.at[b, at], {"tab": crossed(b, 0, d)})

    def joint(d):
        z = up(mz, d)
        wait(swaps[d])
        row = pl.multiple_of(mc * own_half + z * quarter, quarter)
        return tpart[pl.ds(row, quarter), :].astype(F32) + tcore[z].astype(F32)

    fold = quarter // 2
    distant = up(mz, 2)
    thalf[distant] = joint(2).astype(BF)
    fold_up = send(thalf.at[distant, pl.ds(0, fold)], tfold.at[0], at_z(1))
    fold_down = send(thalf.at[distant, pl.ds(fold, fold)], tfold.at[1], at_z(-1))
    table_in = {}
    for b in range(blocks):
        if b % 2 == 0:
            place_head(b // 2)
        total = jnp.zeros((tokens, half), F32)
        for j in range(tiles):
            sums = placed[:, b % 2 * tiles + j, :].astype(BF)
            hsend[2 * b + j % 2, :, (j // 2) * 128 : (j // 2 + 1) * 128] = sums
            total = total + dot_nn(sums, key[j * 128 : (j + 1) * 128, b * half : (b + 1) * half])
        qg[b] = total.astype(BF)
        gq[b, me] = total.astype(BF)
        for d in (1, -1, 2):
            first[b, d] = send(qg.at[b], gq.at[b, me], {"tab": crossed(b, d, 0)})
        if b < 2:
            for d in (1, -1):
                part_on(b, 0, d)
        if b != 1:
            continue
        whole = joint(1)
        wait(fold_up)
        thalf[up(mz, 1), :fold] = (whole[:fold] + tfold[0].astype(F32)).astype(BF)
        thalf[up(mz, 1), fold:] = whole[fold:].astype(BF)
        table_in[1] = send(thalf.at[up(mz, 1)], tz.at[0], at_z(1))
        whole = joint(3)
        wait(fold_down)
        thalf[up(mz, -1), :fold] = whole[:fold].astype(BF)
        thalf[up(mz, -1), fold:] = (whole[fold:] + tfold[1].astype(F32)).astype(BF)
        table_in[3] = send(thalf.at[up(mz, -1)], tz.at[1], at_z(-1))
        thalf[mz] = joint(0).astype(BF)

    halves = []
    for d in range(1, 8):
        p = lax.rem(r + d, 8)
        halves.append(send(hsend.at[p], hrecv.at[r], {"rep": p}))
    hrecv[r] = hsend[r]

    def cross(pair):
        for e in (1, -1, 2):
            for b in pair:
                wait(first[b, e])
                for d in (1, -1):
                    part_on(b, e, d)

    def round_again(pair):
        for e, d in ((0, 1), (1, 1), (-1, -1), (2, -1)):
            for b in pair:
                wait(second[b, e, d])
                at = crossed(b, -e, -d)
                block = gq.at[b, at]
                second[b, e, 2 * d] = send(block, block, {"tab": crossed(b, 0, d)})

    def whole_pair(pair):
        for (b, e, d), copy in list(second.items()):
            if b in pair:
                wait(copy)

    cross((0, 1))
    for b in (2, 3):
        for d in (1, -1):
            part_on(b, 0, d)
    joined = jnp.concatenate([qg[b] for b in range(blocks)], axis=1)
    for at in range(0, width, 512):
        in_grad[:, at : at + 512] = dot_nt(joined, wt[at : at + 512, :]).astype(BF)
    round_again((0, 1))
    cross((2, 3))
    wait(*table_in.values())
    summed = thalf[mz].astype(F32) + tz[0].astype(F32) + tz[1].astype(F32)

    def table_rows_of(z):
        return t_grad.at[pl.ds(pl.multiple_of(mc * own_half + z * quarter, quarter), quarter)]

    table_mine = table_rows_of(mz)
    table_mine[...] = summed.astype(BF)
    table_out = {d: send(table_mine, table_mine, at_z(d)) for d in (1, -1)}
    send(table_mine, table_mine, mate)
    wait(*spreading)

    def turn(q, carry):
        near[:, pl.ds(pl.multiple_of(q * tokens, tokens), tokens)] = ginp[q].astype(F32).T.astype(BF)
        return carry

    lax.fori_loop(0, shards, turn, 0)

    share = piece_width // 8
    sums_in = {}

    def weigh(pair, n):
        whole_pair(pair)
        for i, b in enumerate(pair):
            part = dot_nn(near[...], gq[b].reshape(shards * tokens, half)).astype(BF)
            psend[n, :, :, i * half : (i + 1) * half] = part.reshape(8, share, half)
        sums_in[n] = []
        for d in range(1, 8):
            p = lax.rem(r + d, 8)
            sums_in[n].append(send(psend.at[n, p], precv.at[n, r], {"rep": p}))
        precv[n, r] = psend[n, r]

    weigh((0, 1), 0)
    round_again((2, 3))

    weigh((2, 3), 1)

    before, after = table_rows_of(up(mz, -1)), table_rows_of(up(mz, 1))
    wait(table_out[1])
    lower = before.at[pl.ds(0, quarter // 2)]
    send(lower, lower, at_z(1))
    send(before, before, mate)
    wait(table_out[-1])
    upper = after.at[pl.ds(quarter // 2, quarter // 2)]
    send(upper, upper, at_z(-1))
    send(after, after, mate)
    table_far = [len(copies.copies) - 4, len(copies.copies) - 2]

    wait(*lows, *halves)
    key_part = dot_tn(
        hrecv[...].reshape(8 * tokens, count // 2), lrecv[...].reshape(8 * tokens, half)
    )
    key_rows = count // shards
    ksend[...] = key_part.astype(BF).reshape(8, key_rows, half)
    key_base = copies.take(shards)
    key_out = []
    for i in range(2):
        for dx in range(side):
            x = lax.rem(mx + dx, side)
            copy = pltpu.make_async_remote_copy(
                src_ref=ksend.at[x * 2 + i],
                dst_ref=krecv.at[me],
                send_sem=ssem.at[key_base + i * side + dx],
                recv_sem=rsem.at[key_base + me],
                device_id={"tab": x * side + 2 * mc + i},
                device_id_type=MESH,
            )
            key_out.append((i, dx, copy))
            if dx:
                copy.start()
            else:

                @pl.when(my != 2 * mc + i)
                def _(copy=copy):
                    copy.start()

                @pl.when(my == 2 * mc + i)
                def _(x=x, i=i):
                    krecv[me] = ksend[x * 2 + i]

    key_last = copies.take(8)
    keeper = my // 2

    def key_share(d):
        return pltpu.make_async_remote_copy(
            src_ref=kfin.at[mz],
            dst_ref=kfin.at[mz],
            send_sem=ssem.at[key_last + d],
            recv_sem=rsem.at[key_last + mz],
            device_id={"rep": lax.rem(r + d, 8)},
            device_id_type=MESH,
        )

    @pl.when(keeper == mc)
    def _():
        for d in range(1, shards):
            q = lax.rem(me + d, shards)
            pltpu.make_async_remote_copy(
                src_ref=ksend.at[0],
                dst_ref=krecv.at[q],
                send_sem=ssem.at[key_base],
                recv_sem=rsem.at[key_base + q],
                device_id={"tab": q},
                device_id_type=MESH,
            ).wait_recv()
        total = krecv[0].astype(F32)
        for q in range(1, shards):
            total = total + krecv[q].astype(F32)
        kfin[mz] = total.astype(BF)
        for d in range(1, 8):
            key_share(d).start()

    for n in range(2):
        wait(*sums_in[n])
        total = precv[n, 0].astype(F32)
        for q in range(1, 8):
            total = total + precv[n, q].astype(F32)
        wfin[n, r] = total.astype(BF)
        mine = wfin.at[n, r]
        if n == 0:
            along = {d: send(mine, mine, at_z(d)) for d in NEAR}
            send(mine, mine, mate)
        else:
            for d in range(1, 8):
                send(mine, mine, {"rep": lax.rem(r + d, 8)})
    for d in NEAR:
        wait(along[d])
        part = wfin.at[0, up(mz, -d) * 2 + mc]
        send(part, part, mate)
    wait(*table_far)
    across_z = table_rows_of(up(mz, 2))
    send(across_z, across_z, mate)

    for b in range(4):

        @pl.when((b != mz) | (keeper != mc))
        def _(b=b):
            pltpu.make_async_remote_copy(
                src_ref=kfin.at[b],
                dst_ref=kfin.at[b],
                send_sem=ssem.at[key_last],
                recv_sem=rsem.at[key_last + b],
                device_id=mate,
                device_id_type=MESH,
            ).wait_recv()

    for b in range(4):
        k_grad[:, b * half : (b + 1) * half] = kfin[b].astype(F32)
    wait(*range(len(copies.copies)))
    for n in range(2):
        done = wfin[n].reshape(piece_width, 2 * half).astype(F32)
        w_grad[:, n * 2 * half : (n + 1) * 2 * half] = done
    for i, dx, copy in key_out:
        if dx:
            copy.wait_send()
        else:

            @pl.when(my != 2 * mc + i)
            def _(copy=copy):
                copy.wait_send()

    @pl.when(keeper == mc)
    def _():
        for d in range(1, 8):
            key_share(d).wait_send()

    copies.finish()


def deliver_kernel(pieces, *refs):
    number = len(pieces)
    sources, targets = refs[:number], refs[number : 2 * number]
    held, sems = refs[2 * number : 3 * number], refs[-1]
    moves = []
    for i, count in enumerate(pieces):
        size = held[i].shape[0] // count
        for j in range(count):
            here = pl.ds(j * size, size)
            at = len(moves)
            moves.append(
                (
                    pltpu.make_async_copy(sources[i].at[here], held[i].at[here], sems.at[0, at]),
                    pltpu.make_async_copy(held[i].at[here], targets[i].at[here], sems.at[1, at]),
                )
            )
    for fetch, _ in moves:
        fetch.start()
    for fetch, store in moves:
        fetch.wait()
        store.start()
    for _, store in moves:
        store.wait()


def sds(shape, dtype):
    return jax.ShapeDtypeStruct(shape, dtype)


def on_device(inputs, grad_out, query_weight, sub_keys, values, owner, slot_rows, sub_index):
    tokens, width = inputs.shape
    cols = query_weight.shape[1]
    count = sub_keys.shape[0]
    heads, top = slot_rows.shape[1:]
    blocks = 2 * heads
    lanes = blocks * top
    half = cols // blocks
    shards = lax.axis_size("tab")
    side = 4
    rows = tokens * heads // shards
    slots = 2 * shards * rows
    table_rows = values.shape[0]
    own = jnp.transpose(owner, (1, 2, 0)).reshape(heads, tokens)
    rows_t = jnp.transpose(slot_rows, (1, 2, 0)).reshape(heads * top, tokens)
    picks_t = jnp.transpose(sub_index, (1, 2, 3, 0)).reshape(lanes, tokens)
    vmem = pl.BlockSpec(memory_space=pltpu.VMEM)
    anywhere = pl.BlockSpec(memory_space=pl.ANY)
    V = pltpu.VMEM
    shapes = (
        sds((tokens, width), BF),
        sds((width // shards, cols), F32),
        sds((count // shards, cols), F32),
        sds((table_rows, width), BF),
    )
    results = pl.pallas_call(
        whole_kernel,
        out_shape=shapes,
        in_specs=[vmem] * 4 + [anywhere] * 4,
        out_specs=(vmem,) * 4,
        scratch_shapes=[
            V((2, side, side, rows, width), BF),
            V((2, side, side, rows, width), BF),
            V((2, shards, rows, width), BF),
            V((tokens, width), BF),
            V((width, cols), BF),
            V((count, cols), BF),
            V((table_rows, width), BF),
            V((tokens, cols), F32),
            V((tokens, cols), BF),
            V((tokens, lanes), F32),
            V((3, tokens // 2, lanes), F32),
            V((2, shards, rows, 2 * lanes), BF),
            V((2, shards, rows, 2 * lanes), BF),
            V((2, shards, rows, lanes), F32),
            V((2, shards, rows, lanes), F32),
            V((table_rows, slots), BF),
            V((table_rows, width), BF),
            V((4, table_rows // 8, width), BF),
            V((4, table_rows // 8, width), BF),
            V((2, table_rows // 8, width), BF),
            V((2, table_rows // 16, width), BF),
            V((tokens, 2 * count // 128, 128), F32),
            V((8, tokens, count // 2), BF),
            V((8, tokens, count // 2), BF),
            V((8, tokens, half), BF),
            V((blocks, tokens, half), BF),
            V((blocks, shards, tokens, half), BF),
            V((shards, tokens, width // shards), BF),
            V((width // shards, shards * tokens), BF),
            V((8, count // shards, half), BF),
            V((shards, count // shards, half), BF),
            V((4, count // shards, half), BF),
            V((2, 8, width // shards // 8, 2 * half), BF),
            V((2, 8, width // shards // 8, 2 * half), BF),
            V((2, 8, width // shards // 8, 2 * half), BF),
            pltpu.SemaphoreType.DMA((7,)),
            pltpu.SemaphoreType.DMA((288,)),
            pltpu.SemaphoreType.DMA((288,)),
        ],
        compiler_params=pltpu.CompilerParams(
            collective_id=0, has_side_effects=True, vmem_limit_bytes=60 * 1024 * 1024
        ),
        name="whole",
    )(own, rows_t, picks_t, grad_out, inputs, query_weight, sub_keys, values)
    pieces = (4, 4, 1, 8)
    return pl.pallas_call(
        functools.partial(deliver_kernel, pieces),
        out_shape=shapes,
        in_specs=[anywhere] * 4,
        out_specs=(anywhere,) * 4,
        scratch_shapes=[V(x.shape, x.dtype) for x in shapes]
        + [pltpu.SemaphoreType.DMA((2, sum(pieces)))],
        name="deliver",
    )(*results)


def solution(mesh):
    placed = (
        P(("rep", "tab"), None),
        P(("rep", "tab"), None),
        P(),
        P(),
        P("tab", None),
        P(("rep", "tab"), None, None),
        P(("rep", "tab"), None, None),
        P(("rep", "tab"), None, None, None),
    )
    return jax.shard_map(
        on_device,
        mesh=mesh,
        in_specs=placed,
        out_specs=(P(("rep", "tab"), None), P("tab", None), P("tab", None), P("tab", None)),
        check_vma=False,
    )
```
